128 devices in a mesh: zone: 32 (over y, x, core), sub: 4 (over z).
Axes of the slice: x: 4, y: 4, z: 4, core: 2. Of those that a mesh axis runs over, the one named last changes fastest.
Arguments:
- order_features: bfloat16 [262144, 128], P('zone'), may hold values from -6 to 6
- w_in: bfloat16 [128, 512], replicated, may hold values from -0.5 to 0.5
- bias_in: float32 [512], replicated, may hold values from -3 to 3
- w_out: bfloat16 [512, 128], replicated, may hold values from -0.25 to 0.25
- bias_out: float32 [128], replicated, may hold values from -3 to 3
- courier_embed: bfloat16 [65536, 128], P(('zone', 'sub')), may hold values from -28 to 28
- courier_cap: bfloat16 [65536], P(('zone', 'sub')), may hold values from 0.5 to 4
- adjacency: int32 [512, 8], P('zone'), may hold values from 0 to 127, all different within a row; in each aligned block of 16 rows (0 to 15, 16 to 31, ...) at most 2 rows name the same one
- order_count: int32 [512], P('zone'), may hold values from 64 to 512
- courier_count: int32 [128], P(('zone', 'sub')), may hold values from 64 to 512
Outputs:
- order_potentials: float32 [262144], P('zone')
- courier_potentials: float32 [65536], P(('zone', 'sub'))
The draws below stay inside these ranges and needn't reach their ends.
Inputs may be any that keep to these rules, and one draw needn't show every extreme that they name: `adjacency`: each row names 8 different courier blocks and every courier block is named by some row. Among the 16 rows of one index of zone (aligned blocks of rows), no courier block is named by more than 2 rows, and in some of them one is named by exactly 2.
All inputs are finite; a program needn't handle non-finite values.
Results may differ from the reference program's by a relative error of at most 0.0017.
Values may be sent and summed in bfloat16 or wider, within the bound.
No kernel may reach another device: no remote copies, remote signals or barrier semaphores. Data moves between devices by JAX's collectives and lax.ppermute only.
A program may use at most 128 MiB of HBM per device.

```python
import math
import jax
import jax.numpy as jnp
import numpy as np
from jax import lax

BLOCK = 512
F_IN = 128
HID = 512
EMB = 128
ADJ = 8
SWEEPS = 2
OB_DEV = 16
MOST = 2
ORDER_BLOCKS = 512
COURIER_BLOCKS = 128
ORDERS = 262144
COURIERS = 65536


def draw_courier_embed(key, part):
    first_key = jax.random.fold_in(key, 0)
    row_total = COURIER_BLOCKS * BLOCK
    values = jax.random.normal(first_key, (row_total, EMB), jnp.float32)
    return values.astype(jnp.bfloat16)


def set_ends(entries, rng, low, largest):
    spot = [jax.random.randint(jax.random.fold_in(rng, axis), (), 0, length) for axis, length in enumerate(entries.shape)]
    main_axis = entries.shape.index(max(entries.shape))
    beside = spot[:main_axis] + [(spot[main_axis] + 1) % entries.shape[main_axis]] + spot[main_axis + 1:]
    return entries.at[tuple(spot)].set(low).at[tuple(beside)].set(largest)


def shard_levels(stream_key, dims, cuts, low, largest):
    factor_of = 1.0
    for axis_at, blocks in cuts:
        draws = jax.random.uniform(jax.random.fold_in(jax.random.fold_in(stream_key, 6), axis_at), (blocks,), jnp.float32, low / len(cuts), largest / len(cuts))
        factor_of = factor_of * jnp.repeat(jnp.exp(draws), dims[axis_at] // blocks).reshape((-1,) + (1,) * (len(dims) - 1 - axis_at))
    return factor_of


def assign_block(own_key, own, number, rows, number_of, top, bound, skew):
    order = jax.random.permutation(own_key, number_of)
    crowded, ordinary = portions_of(number_of, rows * top, bound, skew, True), portions_of(number_of, rows * top, bound, skew, False)
    places = jnp.arange(number_of)

    def named(lengths, rotation):
        used = int((lengths > 0).sum())
        fixed = max(1, used // 4)
        moved = fixed + (places - fixed + rotation * (used - fixed)) % max(1, number_of - fixed)
        return jnp.zeros((number_of,), jnp.int32).at[order[jnp.where(places < fixed, places, moved)]].set(jnp.asarray(lengths, jnp.int32))

    lengths = jnp.where(number % 4 == 0, named(crowded, number // 4), named(ordinary, number - number // 4 - 1))
    mixed = jax.random.permutation(jax.random.fold_in(own, 3), number_of)
    donor, receiver = mixed[0:number_of // 2 * 2:2], mixed[1:number_of // 2 * 2:2]
    margin = jnp.minimum(lengths[donor] - 1, bound - lengths[receiver]) // 2
    margin = jnp.where((donor == order[0]) | (receiver == order[0]) | (lengths[receiver] == 0), 0, jnp.maximum(margin, 0))
    moved = jax.random.randint(jax.random.fold_in(own, 4), (number_of // 2,), 0, 1 << 20) % (margin + 1)
    lengths = lengths.at[donor].add(-moved).at[receiver].add(moved)
    labels = jnp.searchsorted(jnp.cumsum(lengths), jnp.arange(rows * top), side="right").astype(jnp.int32)
    grid = labels.reshape(top, rows).T
    grid = grid[jax.random.permutation(jax.random.fold_in(own, 1), rows)]
    rotation = jax.random.randint(jax.random.fold_in(own, 2), (rows, 1), 0, top)
    return jnp.take_along_axis(grid, (jnp.arange(top)[None, :] + rotation) % top, axis=1)


def portions_of(number_of, total, limit, slope, full):
    loads = [(1 << 20) // math.isqrt(standing ** slope) + 1 for standing in range(1, number_of + 1)]
    largest = limit if full else min(limit, max(-(-total // number_of), total * loads[0] // sum(loads)))
    least = 1 if total - largest >= number_of - 1 else 0
    given, surplus = [largest] + [least] * (number_of - 1), total - largest - least * (number_of - 1)
    while surplus > 0:
        movable = [i for i in range(1, number_of) if given[i] < largest] or [i for i in range(1, number_of) if given[i] < limit]
        whole, remaining = sum([loads[i] for i in movable]), surplus
        for i in movable:
            more = min(limit - given[i], max(1, remaining * loads[i] // whole), surplus)
            given[i] = given[i] + more
            surplus = surplus - more
    return np.array(given)


def normal_values(rng, dims, scale, limit, shards=(), held_as=jnp.bfloat16):
    level = shard_levels(rng, dims, shards, -0.22, 0.18) if shards else 1.0
    entries = jax.random.normal(rng, dims, jnp.float32) * scale * level
    return jnp.minimum(jnp.maximum(entries, -limit), limit).astype(held_as)


def setup_inputs(seed: int = 0) -> dict:
    arg_keys = jax.random.split(jax.random.key(seed), 11)
    order_features = normal_values(arg_keys[0], (ORDERS, F_IN), 1.0, 6.0, ((0, 32),))
    w_in = normal_values(arg_keys[1], (F_IN, HID), F_IN ** -0.5, 0.5)
    bias_in = normal_values(arg_keys[2], (HID,), 0.5, 3.0, (), jnp.float32)
    w_out = normal_values(arg_keys[3], (HID, EMB), HID ** -0.5, 0.25)
    bias_out = normal_values(arg_keys[4], (EMB,), 0.5, 3.0, (), jnp.float32)
    courier_embed = draw_courier_embed(jax.random.fold_in(arg_keys[10], 71), 0)
    courier_cap = jnp.clip(jnp.exp(math.log(4.0) - 2.0794415 * jax.random.uniform(arg_keys[6], (COURIERS,), jnp.float32) ** shard_levels(arg_keys[6], (COURIERS,), ((0, 128),), -0.2, 0.2)), 0.5, 4.0).astype(jnp.bfloat16)
    adjacency_keys = jax.random.split(jax.random.fold_in(arg_keys[7], 1), ORDER_BLOCKS // OB_DEV)
    adjacency_turns = jax.random.permutation(jax.random.fold_in(arg_keys[7], 3), ORDER_BLOCKS // OB_DEV)
    adjacency = jax.vmap(lambda own, number: assign_block(jax.random.fold_in(arg_keys[7], 2), own, number, OB_DEV, COURIER_BLOCKS, ADJ, MOST, 2))(adjacency_keys, adjacency_turns).reshape((ORDER_BLOCKS, ADJ))
    order_count = set_ends(jax.random.randint(arg_keys[8], (ORDER_BLOCKS,), BLOCK // 8, BLOCK + 1), jax.random.fold_in(arg_keys[8], 1), BLOCK // 8, BLOCK).astype(jnp.int32)
    courier_count = set_ends(jax.random.randint(arg_keys[9], (COURIER_BLOCKS,), BLOCK // 8, BLOCK + 1), jax.random.fold_in(arg_keys[9], 1), BLOCK // 8, BLOCK).astype(jnp.int32)
    return dict(order_features=order_features, w_in=w_in, bias_in=bias_in, w_out=w_out, bias_out=bias_out, courier_embed=courier_embed, courier_cap=courier_cap, adjacency=adjacency, order_count=order_count, courier_count=courier_count)


SOFTMAX_TEMPER = 0.2
LOWEST = -1e+30

def embed_orders(features, w_in, bias_in, w_out, bias_out):
    hidden = jnp.dot(features, w_in, preferred_element_type=jnp.float32) + bias_in
    hidden = jax.nn.silu(hidden).astype(jnp.bfloat16)
    result = jnp.dot(hidden, w_out, preferred_element_type=jnp.float32) + bias_out
    return result.astype(jnp.bfloat16)

def reference(order_features, w_in, bias_in, w_out, bias_out, courier_embed, courier_cap, adjacency, order_count, courier_count):
    order_embed = embed_orders(order_features, w_in, bias_in, w_out, bias_out)
    order_tiles = order_embed.reshape(ORDER_BLOCKS, BLOCK, EMB).astype(jnp.float32)
    courier_tiles = courier_embed.reshape(COURIER_BLOCKS, BLOCK, EMB).astype(jnp.float32)
    positions = jnp.arange(BLOCK, dtype=jnp.int32)
    order_active = positions[None, :] < order_count[:, None]
    courier_active = positions[None, :] < courier_count[:, None]
    log_capacity = jnp.log(courier_cap.astype(jnp.float32)).reshape(COURIER_BLOCKS, BLOCK)
    affinity_scale = 1.0 / math.sqrt(EMB)
    block_ids = jnp.arange(ORDER_BLOCKS, dtype=jnp.int32)

    def match_affinity(current_block_index):
        partners = courier_tiles[adjacency[current_block_index]]
        return jnp.einsum('ie,aje->aij', order_tiles[current_block_index], partners) * affinity_scale

    def order_pass(courier_potentials):

        def per_block(current_block_index):
            neighbour_blocks = adjacency[current_block_index]
            pair_scores = (courier_potentials[neighbour_blocks][:, None, :] + match_affinity(current_block_index)) / SOFTMAX_TEMPER
            usable = jnp.broadcast_to(courier_active[neighbour_blocks][:, None, :], pair_scores.shape)
            running_highest = lax.optimization_barrier(jnp.max(jnp.where(usable, pair_scores, LOWEST), axis=(0, 2)))
            summed_terms = lax.optimization_barrier(jnp.sum(jnp.where(usable, jnp.exp(pair_scores - running_highest[None, :, None]), 0.0), axis=(0, 2)))
            return jnp.where(order_active[current_block_index], -SOFTMAX_TEMPER * (running_highest + jnp.log(summed_terms)), 0.0)
        return lax.map(per_block, block_ids)

    def courier_pass(order_potentials):

        def per_block(current_block_index):
            pair_scores = (order_potentials[current_block_index][None, :, None] + match_affinity(current_block_index)) / SOFTMAX_TEMPER
            usable = jnp.broadcast_to(order_active[current_block_index][None, :, None], pair_scores.shape)
            running_highest = lax.optimization_barrier(jnp.max(jnp.where(usable, pair_scores, LOWEST), axis=1))
            summed_terms = lax.optimization_barrier(jnp.sum(jnp.where(usable, jnp.exp(pair_scores - running_highest[:, None, :]), 0.0), axis=1))
            return (running_highest, summed_terms)
        running_highest, summed_terms = lax.map(per_block, block_ids)
        flat_ids = adjacency.reshape(-1)
        running_highest = running_highest.reshape(-1, BLOCK)
        summed_terms = summed_terms.reshape(-1, BLOCK)
        peak_score_value = jax.ops.segment_max(running_highest, flat_ids, num_segments=COURIER_BLOCKS)
        total_weight_mass = jax.ops.segment_sum(summed_terms * jnp.exp(running_highest - peak_score_value[flat_ids]), flat_ids, num_segments=COURIER_BLOCKS)
        return jnp.where(courier_active, SOFTMAX_TEMPER * log_capacity - SOFTMAX_TEMPER * (peak_score_value + jnp.log(total_weight_mass)), 0.0)
    courier_potentials = jnp.zeros((COURIER_BLOCKS, BLOCK), jnp.float32)
    order_potentials = jnp.zeros((ORDER_BLOCKS, BLOCK), jnp.float32)
    for sweep_step in range(SWEEPS):
        order_potentials = order_pass(courier_potentials)
        courier_potentials = courier_pass(order_potentials)
    return (order_potentials.reshape(-1), courier_potentials.reshape(-1))
```

```python
import math

import jax
import jax.numpy as jnp
from jax import lax
from jax.experimental import pallas as pl
from jax.experimental.pallas import tpu as pltpu
from jax.sharding import PartitionSpec as P

BLOCK = 512
EMB = 128
HID = 512
ADJ = 8
OB_DEV = 16
ZONES = 32
SUBS = 4
HALF = 256
UNROLL = 4
MOST_ENTRIES = 256
LIST_SIZE = MOST_ENTRIES + 2 * UNROLL
NO_ORDER = 2 * OB_DEV
NO_COURIER = 2 * ZONES

TEMPER = 0.2
LOWEST = -1e30
SCORE_SCALE = math.log2(math.e) / (TEMPER * math.sqrt(EMB))
DUAL_SCALE = TEMPER * math.log(2.0)

VMEM_LIMIT = 40 * 1024 * 1024


def zone_of(y, x, core):
    return ((y % 4) * 4 + (x % 4)) * 2 + core


PLACES = [(y, x, core) for y in range(4) for x in range(4) for core in range(2)]


def along_x(value, step):
    return lax.ppermute(value, "zone", [(zone_of(y, x, c), zone_of(y, x + step, c)) for y, x, c in PLACES])


def along_y(value, step):
    return lax.ppermute(value, "zone", [(zone_of(y, x, c), zone_of(y + step, x, c)) for y, x, c in PLACES])


def other_core(value):
    return lax.ppermute(value, "zone", [(zone_of(y, x, c), zone_of(y, x, 1 - c)) for y, x, c in PLACES])


def along_z(value, step):
    return lax.ppermute(value, "sub", [(i, (i + step) % SUBS) for i in range(SUBS)])


def join(*parts):
    highest = parts[0]
    for part in parts[1:]:
        highest = jnp.maximum(highest, part)
    total = jnp.exp2(parts[0] - highest)
    for part in parts[1:]:
        total = total + jnp.exp2(part - highest)
    return highest + jnp.log2(total)


def join_subs(value):
    return join(value, along_z(value, 1), along_z(value, 2), along_z(value, 3))


def join_zones(value):
    value = join(value, other_core(value))
    value = join(value, along_x(value, 1), along_x(value, 2), along_x(value, 3))
    return join(value, along_y(value, 1), along_y(value, 2), along_y(value, 3))


def embed_kernel(count_ref, x_ref, w_in_ref, b_in_ref, w_out_ref, b_out_ref, o_ref):
    block = pl.program_id(0)
    count = count_ref[block]
    for half in range(2):

        @pl.when(count > half * HALF)
        def _():
            rows = pl.ds(half * HALF, HALF)
            v = jnp.dot(x_ref[rows, :], w_in_ref[...], preferred_element_type=jnp.float32)
            v = 0.5 * (v + b_in_ref[...])
            hidden = (v + v * jnp.tanh(v)).astype(jnp.bfloat16)
            out = jnp.dot(hidden, w_out_ref[...], preferred_element_type=jnp.float32)
            o_ref[rows, :] = ((out + b_out_ref[...]) * SCORE_SCALE).astype(jnp.bfloat16)


def embed_orders(count, features, w_in, bias_in, w_out, bias_out):
    whole = lambda i, c: (0, 0)
    return pl.pallas_call(
        embed_kernel,
        out_shape=jax.ShapeDtypeStruct((OB_DEV * BLOCK, EMB), jnp.bfloat16),
        grid_spec=pltpu.PrefetchScalarGridSpec(
            num_scalar_prefetch=1,
            grid=(OB_DEV,),
            in_specs=[
                pl.BlockSpec((BLOCK, EMB), lambda i, c: (i, 0)),
                pl.BlockSpec((EMB, HID), whole),
                pl.BlockSpec((1, HID), whole),
                pl.BlockSpec((HID, EMB), whole),
                pl.BlockSpec((1, EMB), whole),
            ],
            out_specs=pl.BlockSpec((BLOCK, EMB), lambda i, c: (i, 0)),
        ),
        cost_estimate=pl.CostEstimate(flops=2 * 2 * 8192 * 128 * 512, bytes_accessed=5 << 20, transcendentals=8192 * 512),
        name="embed_orders",
    )(count, features, w_in, bias_in.reshape(1, HID), w_out, bias_out.reshape(1, EMB))


def list_kernel(adj_ref, order_count_ref, courier_count_ref, sub_ref, list_ref, rounds_ref):
    sub = sub_ref[0]

    def put(n, order, courier, keep):
        list_ref[n] = order * 256 + courier
        return n + keep

    def one_pair(p, n):
        b = p // ADJ
        c = adj_ref[p]
        z = c // SUBS
        mine = jnp.where(c % SUBS == sub, 1, 0)
        order_two = mine * jnp.where(order_count_ref[b] > HALF, 1, 0)
        courier_two = mine * jnp.where(courier_count_ref[z] > HALF, 1, 0)
        n = put(n, 2 * b, 2 * z, mine)
        n = put(n, 2 * b, 2 * z + 1, courier_two)
        n = put(n, 2 * b + 1, 2 * z, order_two)
        return put(n, 2 * b + 1, 2 * z + 1, order_two * courier_two)

    n = lax.fori_loop(0, OB_DEV * ADJ, one_pair, jnp.int32(0))
    for i in range(UNROLL):
        list_ref[n + i] = jnp.int32(NO_ORDER * 256 + NO_COURIER)
    rounds_ref[0] = (n + UNROLL - 1) // UNROLL


def work_list(adjacency, order_count, courier_count, sub):
    smem = pl.BlockSpec(memory_space=pltpu.SMEM)
    return pl.pallas_call(
        list_kernel,
        out_shape=(
            jax.ShapeDtypeStruct((LIST_SIZE,), jnp.int32),
            jax.ShapeDtypeStruct((1,), jnp.int32),
        ),
        in_specs=[smem] * 4,
        out_specs=(smem, smem),
        name="work_list",
    )(adjacency.reshape(-1), order_count, courier_count, sub.reshape(1))


def pass_kernel(sum_couriers, list_ref, rounds_ref, summed_ref, kept_ref, weight_ref, live_ref, out_ref, w_ref, r_ref, m_ref):
    summed_blocks, kept_blocks = weight_ref.shape[0], live_ref.shape[0]
    rounds = rounds_ref[0]

    def piece(e):
        order, courier = e // 256, e % 256
        return (courier, order) if sum_couriers else (order, courier)

    def scores(s, k):
        s = jnp.minimum(s, 2 * summed_blocks - 1)
        k = jnp.minimum(k, 2 * kept_blocks - 1)
        left = summed_ref[pl.ds(pl.multiple_of(s * HALF, HALF), HALF), :]
        right = kept_ref[pl.ds(pl.multiple_of(k * HALF, HALF), HALF), :]
        return lax.dot_general(left, right, (((1,), (1,)), ((), ())), preferred_element_type=jnp.float32)

    weight = weight_ref[...]
    linear = jnp.exp2(weight)
    high = linear.astype(jnp.bfloat16).astype(jnp.float32)
    low = linear - high
    row = lax.broadcasted_iota(jnp.int32, (summed_blocks, 16, HALF), 1)
    for half in range(2):
        cut = slice(half * HALF, (half + 1) * HALF)
        rows = jnp.where(row == 0, high[:, None, cut], jnp.where(row == 1, low[:, None, cut], 0.0))
        w_ref[0:summed_blocks, half] = rows.astype(jnp.bfloat16)
    w_ref[summed_blocks] = jnp.zeros((2, 16, HALF), jnp.bfloat16)
    r_ref[...] = jnp.zeros(r_ref.shape, jnp.float32)

    def one_round(i, carry):
        todo = [piece(list_ref[i * UNROLL + t]) for t in range(UNROLL)]
        sums = []
        for s, k in todo:
            terms = jnp.exp2(scores(s, k)).astype(jnp.bfloat16)
            sums.append(jnp.dot(w_ref[s // 2, s % 2], terms, preferred_element_type=jnp.float32)[0:8])
        for (s, k), part in zip(todo, sums):
            r_ref[k // 2, k % 2] += part
        return carry

    lax.fori_loop(0, rounds, one_round, 0)

    is_live_weight = weight > 0.5 * LOWEST
    highest = jnp.max(weight)
    lowest = jnp.min(jnp.where(is_live_weight, weight, 0.0))
    least = jnp.exp2(jnp.full((1, 1), jnp.clip(highest, 0.0, 100.0) - 86.0, jnp.float32))
    bad = jnp.where((highest <= 100.0) & (lowest >= -100.0), 0.0, 1.0)
    for half in range(2):
        cut = slice(half * HALF, (half + 1) * HALF)
        total = r_ref[0:kept_blocks, half, 0, :] + r_ref[0:kept_blocks, half, 1, :]
        live = live_ref[:, cut] > 0.5 * LOWEST
        fine = (total >= least) & (total <= 2.0**126)
        bad = bad + jnp.max(jnp.where(live, jnp.where(fine, 0.0, 1.0), 0.0))
        out_ref[:, cut] = jnp.where(live, jnp.log2(jnp.where(live, total, 1.0)), LOWEST)

    @pl.when(bad > 0.0)
    def _():
        m_ref[...] = jnp.full(m_ref.shape, LOWEST, jnp.float32)
        r_ref[...] = jnp.zeros(r_ref.shape, jnp.float32)

        def one_piece(i, carry):
            s, k = piece(list_ref[i])
            block = jnp.minimum(s // 2, summed_blocks - 1)
            w = weight_ref[pl.ds(block, 1), pl.ds(pl.multiple_of((s % 2) * HALF, HALF), HALF)]
            column = jnp.transpose(jnp.broadcast_to(w, (128, HALF)))
            x = scores(s, k) + jnp.concatenate([column, column], axis=1)
            before = m_ref[k // 2, k % 2, 0:1]
            after = jnp.maximum(before, jnp.max(x, axis=0, keepdims=True))
            scaled = r_ref[k // 2, k % 2, 0:1] * jnp.exp2(before - after)
            m_ref[k // 2, k % 2, 0:1] = after
            r_ref[k // 2, k % 2, 0:1] = scaled + jnp.sum(jnp.exp2(x - after), axis=0, keepdims=True)
            return carry

        lax.fori_loop(0, rounds * UNROLL, one_piece, 0)
        for half in range(2):
            cut = slice(half * HALF, (half + 1) * HALF)
            live = live_ref[:, cut] > 0.5 * LOWEST
            total = jnp.where(live, r_ref[0:kept_blocks, half, 0, :], 1.0)
            out_ref[:, cut] = jnp.where(live, m_ref[0:kept_blocks, half, 0, :] + jnp.log2(total), LOWEST)


def half_sweep(sum_couriers, work, rounds, summed, kept, weight, live, name):
    smem = pl.BlockSpec(memory_space=pltpu.SMEM)
    vmem = pl.BlockSpec(memory_space=pltpu.VMEM)
    summed_blocks, kept_blocks = weight.shape[0], live.shape[0]

    def kernel(*refs):
        pass_kernel(sum_couriers, *refs)

    return pl.pallas_call(
        kernel,
        out_shape=jax.ShapeDtypeStruct((kept_blocks, BLOCK), jnp.float32),
        in_specs=[smem, smem, vmem, vmem, vmem, vmem],
        out_specs=vmem,
        scratch_shapes=[
            pltpu.VMEM((summed_blocks + 1, 2, 16, HALF), jnp.bfloat16),
            pltpu.VMEM((kept_blocks + 1, 2, 8, HALF), jnp.float32),
            pltpu.VMEM((kept_blocks + 1, 2, 8, HALF), jnp.float32),
        ],
        compiler_params=pltpu.CompilerParams(vmem_limit_bytes=VMEM_LIMIT),
        cost_estimate=pl.CostEstimate(flops=28 * 2 * 512 * 512 * 128, bytes_accessed=6 << 20, transcendentals=28 * 512 * 512),
        name=name,
    )(work, rounds, summed, kept, weight, live)


def shards(
    order_features,
    w_in,
    bias_in,
    w_out,
    bias_out,
    courier_embed,
    courier_cap,
    adjacency,
    order_count,
    courier_count,
):
    sub = lax.axis_index("sub")
    positions = jnp.arange(BLOCK, dtype=jnp.int32)

    couriers = lax.all_gather(courier_embed, "zone", tiled=True)
    own_log_cap = jnp.where(
        positions < courier_count[0], jnp.log2(courier_cap.astype(jnp.float32)), LOWEST
    )
    log_cap = lax.all_to_all(
        jnp.broadcast_to(own_log_cap[None], (ZONES, BLOCK)), "zone", 0, 0, tiled=True
    )
    courier_live = log_cap > 0.5 * LOWEST
    counts = jnp.sum(courier_live.astype(jnp.int32), axis=1)

    orders = embed_orders(order_count, order_features, w_in, bias_in, w_out, bias_out)
    work, rounds = work_list(adjacency, order_count, counts, sub)

    mine = adjacency % SUBS == sub
    order_live = positions[None, :] < order_count[:, None]
    order_here = jnp.where(order_live & jnp.any(mine, axis=1, keepdims=True), 0.0, LOWEST)
    named = jnp.any(
        (adjacency.reshape(-1)[None, :] == jnp.arange(ZONES)[:, None] * SUBS + sub), axis=1, keepdims=True
    )
    courier_here = jnp.where(courier_live & named, 0.0, LOWEST)

    def order_pass(courier_dual, name):
        partial = half_sweep(True, work, rounds, couriers, orders, courier_dual, order_here, name)
        return jnp.where(order_live, -join_subs(partial), LOWEST)

    def courier_pass(order_dual, name):
        return half_sweep(False, work, rounds, orders, couriers, order_dual, courier_here, name)

    courier_dual = jnp.where(courier_live, 0.0, LOWEST)
    order_dual = order_pass(courier_dual, "orders_1")
    sums = join_zones(courier_pass(order_dual, "couriers_1"))
    courier_dual = jnp.where(courier_live, log_cap - sums, LOWEST)
    order_dual = order_pass(courier_dual, "orders_2")
    partial = courier_pass(order_dual, "couriers_2")
    parts = lax.all_to_all(partial, "zone", 0, 0, tiled=True)
    highest = jnp.max(parts, axis=0)
    total = highest + jnp.log2(jnp.sum(jnp.exp2(parts - highest[None]), axis=0))
    courier_out = jnp.where(positions < courier_count[0], DUAL_SCALE * (own_log_cap - total), 0.0)
    order_out = jnp.where(order_live, DUAL_SCALE * order_dual, 0.0)
    return order_out.reshape(-1), courier_out


def solution(mesh):
    return jax.shard_map(
        shards,
        mesh=mesh,
        in_specs=(
            P("zone", None),
            P(),
            P(),
            P(),
            P(),
            P(("zone", "sub"), None),
            P(("zone", "sub")),
            P("zone", None),
            P("zone"),
            P(("zone", "sub")),
        ),
        out_specs=(P("zone"), P(("zone", "sub"))),
        check_vma=False,
    )
```

```python
import math

import jax
import jax.numpy as jnp
from jax import lax
from jax.experimental import pallas as pl
from jax.experimental.pallas import tpu as pltpu
from jax.sharding import PartitionSpec as P

BLOCK = 512
EMB = 128
HID = 512
ADJ = 8
OB_DEV = 16
ZONES = 32
SUBS = 4
HALF = 256
UNROLL = 16
REST = 4
MOST_ENTRIES = 256
LIST_SIZE = MOST_ENTRIES + 2 * REST
NO_ORDER = 2 * OB_DEV
NO_COURIER = 2 * ZONES

TEMPER = 0.2
LOWEST = -1e30
SCORE_SCALE = math.log2(math.e) / (TEMPER * math.sqrt(EMB))
DUAL_SCALE = TEMPER * math.log(2.0)

VMEM_LIMIT = 40 * 1024 * 1024


def zone_of(y, x, core):
    return ((y % 4) * 4 + (x % 4)) * 2 + core


PLACES = [(y, x, core) for y in range(4) for x in range(4) for core in range(2)]


def along_x(value, step):
    return lax.ppermute(value, "zone", [(zone_of(y, x, c), zone_of(y, x + step, c)) for y, x, c in PLACES])


def along_y(value, step):
    return lax.ppermute(value, "zone", [(zone_of(y, x, c), zone_of(y + step, x, c)) for y, x, c in PLACES])


def other_core(value):
    return lax.ppermute(value, "zone", [(zone_of(y, x, c), zone_of(y, x, 1 - c)) for y, x, c in PLACES])


def along_z(value, step):
    return lax.ppermute(value, "sub", [(i, (i + step) % SUBS) for i in range(SUBS)])


def join(*parts):
    highest = parts[0]
    for part in parts[1:]:
        highest = jnp.maximum(highest, part)
    total = jnp.exp2(parts[0] - highest)
    for part in parts[1:]:
        total = total + jnp.exp2(part - highest)
    return highest + jnp.log2(total)


def join_subs(value):
    return join(value, along_z(value, 1), along_z(value, 2), along_z(value, 3))


def join_zones(value):
    value = join(value, other_core(value))
    value = join(value, along_x(value, 1), along_x(value, 2), along_x(value, 3))
    return join(value, along_y(value, 1), along_y(value, 2), along_y(value, 3))


EMBED_ROWS = 2048


def embed_kernel(x_ref, w_in_ref, b_in_ref, w_out_ref, b_out_ref, o_ref):
    for start in range(0, EMBED_ROWS, BLOCK):
        rows = pl.ds(start, BLOCK)
        v = jnp.dot(x_ref[rows, :], w_in_ref[...], preferred_element_type=jnp.float32)
        v = 0.5 * (v + b_in_ref[...])
        hidden = (v + v * jnp.tanh(v)).astype(jnp.bfloat16)
        out = jnp.dot(hidden, w_out_ref[...], preferred_element_type=jnp.float32)
        o_ref[rows, :] = ((out + b_out_ref[...]) * SCORE_SCALE).astype(jnp.bfloat16)


def embed_orders(features, w_in, bias_in, w_out, bias_out):
    rows = features.shape[0]
    whole = lambda i: (0, 0)
    return pl.pallas_call(
        embed_kernel,
        out_shape=jax.ShapeDtypeStruct((rows, EMB), jnp.bfloat16),
        grid=(rows // EMBED_ROWS,),
        in_specs=[
            pl.BlockSpec((EMBED_ROWS, EMB), lambda i: (i, 0)),
            pl.BlockSpec((EMB, HID), whole),
            pl.BlockSpec((1, HID), whole),
            pl.BlockSpec((HID, EMB), whole),
            pl.BlockSpec((1, EMB), whole),
        ],
        out_specs=pl.BlockSpec((EMBED_ROWS, EMB), lambda i: (i, 0)),
        compiler_params=pltpu.CompilerParams(vmem_limit_bytes=VMEM_LIMIT),
        cost_estimate=pl.CostEstimate(
            flops=4 * rows * EMB * HID, bytes_accessed=4 * rows * EMB, transcendentals=rows * HID
        ),
        name="embed_orders",
    )(features, w_in, bias_in.reshape(1, HID), w_out, bias_out.reshape(1, EMB))


def list_kernel(adj_ref, order_count_ref, courier_count_ref, sub_ref, list_ref, rounds_ref):
    sub = sub_ref[0]

    def put(n, order, courier, keep):
        list_ref[n] = order * 256 + courier
        return n + keep

    def one_pair(p, n):
        b = p // ADJ
        c = adj_ref[p]
        z = c // SUBS
        mine = jnp.where(c % SUBS == sub, 1, 0)
        order_two = mine * jnp.where(order_count_ref[b] > HALF, 1, 0)
        courier_two = mine * jnp.where(courier_count_ref[z] > HALF, 1, 0)
        n = put(n, 2 * b, 2 * z, mine)
        n = put(n, 2 * b, 2 * z + 1, courier_two)
        n = put(n, 2 * b + 1, 2 * z, order_two)
        return put(n, 2 * b + 1, 2 * z + 1, order_two * courier_two)

    n = lax.fori_loop(0, OB_DEV * ADJ, one_pair, jnp.int32(0))
    for i in range(REST):
        list_ref[n + i] = jnp.int32(NO_ORDER * 256 + NO_COURIER)
    rounds_ref[0] = (n + REST - 1) // REST


def work_list(adjacency, order_count, courier_count, sub):
    smem = pl.BlockSpec(memory_space=pltpu.SMEM)
    return pl.pallas_call(
        list_kernel,
        out_shape=(
            jax.ShapeDtypeStruct((LIST_SIZE,), jnp.int32),
            jax.ShapeDtypeStruct((1,), jnp.int32),
        ),
        in_specs=[smem] * 4,
        out_specs=(smem, smem),
        name="work_list",
    )(adjacency.reshape(-1), order_count, courier_count, sub.reshape(1))


def pass_kernel(sum_couriers, list_ref, rounds_ref, summed_ref, kept_ref, weight_ref, live_ref, out_ref, w_ref, r_ref, m_ref):
    summed_blocks, kept_blocks = weight_ref.shape[0], live_ref.shape[0]
    rounds = rounds_ref[0]
    weight = weight_ref[...]

    high = weight.astype(jnp.bfloat16).astype(jnp.float32)
    low = weight - high
    blank = jnp.zeros((64 - 2 * summed_blocks, 128), jnp.float32)
    for part in range(2):
        rows = []
        for value in (high, low):
            rows += [value[:, part * 128 : part * 128 + 128], value[:, HALF + part * 128 : HALF + part * 128 + 128]]
            if summed_blocks < 32:
                rows.append(blank)
        w_ref[part * 128 : part * 128 + 128, :] = jnp.transpose(jnp.concatenate(rows, axis=0)).astype(jnp.bfloat16)
    r_ref[...] = jnp.zeros(r_ref.shape, jnp.float32)
    lanes = lax.broadcasted_iota(jnp.int32, (1, 128), 1) % 64

    def piece(e):
        order, courier = e // 256, e % 256
        return (courier, order) if sum_couriers else (order, courier)

    def sides(s, k):
        s = jnp.minimum(s, 2 * summed_blocks - 1)
        k = jnp.minimum(k, 2 * kept_blocks - 1)
        left = summed_ref[pl.ds(pl.multiple_of(s * HALF, HALF), HALF), :]
        right = kept_ref[pl.ds(pl.multiple_of(k * HALF, HALF), HALF), :]
        return left, right

    def scores(left, right):
        return lax.dot_general(left, right, (((1,), (1,)), ((), ())), preferred_element_type=jnp.float32)

    def weighted(s, k):
        left, right = sides(s, k)
        lane = (s % 2) * summed_blocks + s // 2
        ones = jnp.where(lanes == lane, 1.0, 0.0).astype(jnp.bfloat16)
        left = jnp.concatenate([left, w_ref[...]], axis=1)
        right = jnp.concatenate([right, jnp.broadcast_to(ones, (HALF, 128))], axis=1)
        return scores(left, right)

    def steps(first, count):
        todo = [piece(list_ref[first + t]) for t in range(count)]
        sums = [jnp.sum(jnp.exp2(weighted(s, k)).reshape(HALF // 8, 8, HALF), axis=0) for s, k in todo]
        for (s, k), part in zip(todo, sums):
            r_ref[k // 2, k % 2] += part

    large = rounds // (UNROLL // REST)

    def large_step(i, carry):
        steps(i * UNROLL, UNROLL)
        return carry

    def small_step(i, carry):
        steps(i * REST, REST)
        return carry

    lax.fori_loop(0, large, large_step, 0)
    lax.fori_loop(large * (UNROLL // REST), rounds, small_step, 0)

    live_weight = jnp.where(weight > 0.5 * LOWEST, jnp.abs(weight), 0.0)
    bad = jnp.where(jnp.max(live_weight) <= 128.0, 0.0, 1.0)
    for half in range(2):
        cut = slice(half * HALF, (half + 1) * HALF)
        total = jnp.sum(r_ref[0:kept_blocks, half], axis=1)
        live = live_ref[:, cut] > 0.5 * LOWEST
        fine = (total >= 2.0**-86) & (total <= 2.0**126)
        bad = bad + jnp.max(jnp.where(live, jnp.where(fine, 0.0, 1.0), 0.0))
        out_ref[:, cut] = jnp.where(live, jnp.log2(jnp.where(live, total, 1.0)), LOWEST)

    @pl.when(bad > 0.0)
    def _():
        m_ref[...] = jnp.full(m_ref.shape, LOWEST, jnp.float32)
        r_ref[...] = jnp.zeros(r_ref.shape, jnp.float32)

        def one_piece(i, carry):
            s, k = piece(list_ref[i])
            block = jnp.minimum(s // 2, summed_blocks - 1)
            w = weight_ref[pl.ds(block, 1), pl.ds(pl.multiple_of((s % 2) * HALF, HALF), HALF)]
            column = jnp.transpose(jnp.broadcast_to(w, (128, HALF)))
            x = scores(*sides(s, k)) + jnp.concatenate([column, column], axis=1)
            before = m_ref[k // 2, k % 2, 0:1]
            after = jnp.maximum(before, jnp.max(x, axis=0, keepdims=True))
            scaled = r_ref[k // 2, k % 2, 0:1] * jnp.exp2(before - after)
            m_ref[k // 2, k % 2, 0:1] = after
            r_ref[k // 2, k % 2, 0:1] = scaled + jnp.sum(jnp.exp2(x - after), axis=0, keepdims=True)
            return carry

        lax.fori_loop(0, rounds * REST, one_piece, 0)
        for half in range(2):
            cut = slice(half * HALF, (half + 1) * HALF)
            live = live_ref[:, cut] > 0.5 * LOWEST
            total = jnp.where(live, r_ref[0:kept_blocks, half, 0, :], 1.0)
            out_ref[:, cut] = jnp.where(live, m_ref[0:kept_blocks, half, 0, :] + jnp.log2(total), LOWEST)


def half_sweep(sum_couriers, work, rounds, summed, kept, weight, live, name):
    smem = pl.BlockSpec(memory_space=pltpu.SMEM)
    vmem = pl.BlockSpec(memory_space=pltpu.VMEM)
    summed_blocks, kept_blocks = weight.shape[0], live.shape[0]

    def kernel(*refs):
        pass_kernel(sum_couriers, *refs)

    return pl.pallas_call(
        kernel,
        out_shape=jax.ShapeDtypeStruct((kept_blocks, BLOCK), jnp.float32),
        in_specs=[smem, smem, vmem, vmem, vmem, vmem],
        out_specs=vmem,
        scratch_shapes=[
            pltpu.VMEM((HALF, 128), jnp.bfloat16),
            pltpu.VMEM((kept_blocks + 1, 2, 8, HALF), jnp.float32),
            pltpu.VMEM((kept_blocks + 1, 2, 8, HALF), jnp.float32),
        ],
        compiler_params=pltpu.CompilerParams(vmem_limit_bytes=VMEM_LIMIT),
        cost_estimate=pl.CostEstimate(flops=28 * 2 * 512 * 512 * 128, bytes_accessed=6 << 20, transcendentals=28 * 512 * 512),
        name=name,
    )(work, rounds, summed, kept, weight, live)


def shards(
    order_features,
    w_in,
    bias_in,
    w_out,
    bias_out,
    courier_embed,
    courier_cap,
    adjacency,
    order_count,
    courier_count,
):
    sub = lax.axis_index("sub")
    positions = jnp.arange(BLOCK, dtype=jnp.int32)

    couriers = lax.all_gather(courier_embed, "zone", tiled=True)
    own_log_cap = jnp.where(
        positions < courier_count[0], jnp.log2(courier_cap.astype(jnp.float32)), LOWEST
    )
    log_cap = lax.all_to_all(
        jnp.broadcast_to(own_log_cap[None], (ZONES, BLOCK)), "zone", 0, 0, tiled=True
    )
    courier_live = log_cap > 0.5 * LOWEST
    counts = jnp.sum(courier_live.astype(jnp.int32), axis=1)

    orders = embed_orders(order_features, w_in, bias_in, w_out, bias_out)
    work, rounds = work_list(adjacency, order_count, counts, sub)

    mine = adjacency % SUBS == sub
    order_live = positions[None, :] < order_count[:, None]
    order_here = jnp.where(order_live & jnp.any(mine, axis=1, keepdims=True), 0.0, LOWEST)
    named = jnp.any(
        (adjacency.reshape(-1)[None, :] == jnp.arange(ZONES)[:, None] * SUBS + sub), axis=1, keepdims=True
    )
    courier_here = jnp.where(courier_live & named, 0.0, LOWEST)

    def order_pass(courier_dual, name):
        partial = half_sweep(True, work, rounds, couriers, orders, courier_dual, order_here, name)
        return jnp.where(order_live, -join_subs(partial), LOWEST)

    def courier_pass(order_dual, name):
        return half_sweep(False, work, rounds, orders, couriers, order_dual, courier_here, name)

    courier_dual = jnp.where(courier_live, 0.0, LOWEST)
    order_dual = order_pass(courier_dual, "orders_1")
    sums = join_zones(courier_pass(order_dual, "couriers_1"))
    courier_dual = jnp.where(courier_live, log_cap - sums, LOWEST)
    order_dual = order_pass(courier_dual, "orders_2")
    partial = courier_pass(order_dual, "couriers_2")
    parts = lax.all_to_all(partial, "zone", 0, 0, tiled=True)
    highest = jnp.max(parts, axis=0)
    total = highest + jnp.log2(jnp.sum(jnp.exp2(parts - highest[None]), axis=0))
    courier_out = jnp.where(positions < courier_count[0], DUAL_SCALE * (own_log_cap - total), 0.0)
    order_out = jnp.where(order_live, DUAL_SCALE * order_dual, 0.0)
    return order_out.reshape(-1), courier_out


def solution(mesh):
    return jax.shard_map(
        shards,
        mesh=mesh,
        in_specs=(
            P("zone", None),
            P(),
            P(),
            P(),
            P(),
            P(("zone", "sub"), None),
            P(("zone", "sub")),
            P("zone", None),
            P("zone"),
            P(("zone", "sub")),
        ),
        out_specs=(P("zone"), P(("zone", "sub"))),
        check_vma=False,
    )
```

```python
import math

import jax
import jax.numpy as jnp
from jax import lax
from jax.experimental import pallas as pl
from jax.experimental.pallas import tpu as pltpu
from jax.sharding import PartitionSpec as P

BLOCK = 512
EMB = 128
HID = 512
ADJ = 8
OB_DEV = 16
ZONES = 32
SUBS = 4
HALF = 256
UNROLL = 16
REST = 4
MOST_ENTRIES = 256
LIST_SIZE = MOST_ENTRIES + 2 * REST
NO_ORDER = 2 * OB_DEV
NO_COURIER = 2 * ZONES

TEMPER = 0.2
LOWEST = -1e30
SCORE_SCALE = math.log2(math.e) / (TEMPER * math.sqrt(EMB))
DUAL_SCALE = TEMPER * math.log(2.0)

VMEM_LIMIT = 16 * 1024 * 1024
PARTS = 8


def zone_of(y, x, core):
    return ((y % 4) * 4 + (x % 4)) * 2 + core


PLACES = [(y, x, core) for y in range(4) for x in range(4) for core in range(2)]


def along_x(value, step):
    return lax.ppermute(value, "zone", [(zone_of(y, x, c), zone_of(y, x + step, c)) for y, x, c in PLACES])


def along_y(value, step):
    return lax.ppermute(value, "zone", [(zone_of(y, x, c), zone_of(y + step, x, c)) for y, x, c in PLACES])


def other_core(value):
    return lax.ppermute(value, "zone", [(zone_of(y, x, c), zone_of(y, x, 1 - c)) for y, x, c in PLACES])


def along_z(value, step):
    return lax.ppermute(value, "sub", [(i, (i + step) % SUBS) for i in range(SUBS)])


def plane_step(value, stage, step):
    pairs = []
    for y, x, c in PLACES:
        to = (y, x + step, c) if stage == c else (y + step, x, c)
        pairs.append((zone_of(y, x, c), zone_of(*to)))
    return lax.ppermute(value, "zone", pairs)


def gather_row(block):
    return jnp.concatenate([block] + [plane_step(block, 0, step) for step in (1, 2, 3)], axis=0)


def gather_plane(row):
    own = [row] + [plane_step(row, 1, step) for step in (1, 2, 3)]
    return own + [other_core(part) for part in own]


def slot_of(zone, me):
    back_x = (me // 2 - zone // 2) % 4
    back_y = (me // 8 - zone // 8) % 4
    odd = zone % 2
    first = jnp.where(odd == 0, back_x, back_y)
    second = jnp.where(odd == 0, back_y, back_x)
    return ((me + zone) % 2) * 16 + second * 4 + first


def join(*parts):
    highest = parts[0]
    for part in parts[1:]:
        highest = jnp.maximum(highest, part)
    total = jnp.exp2(parts[0] - highest)
    for part in parts[1:]:
        total = total + jnp.exp2(part - highest)
    return highest + jnp.log2(total)


def join_subs(value):
    return join(value, along_z(value, 1), along_z(value, 2), along_z(value, 3))


def join_zones(value):
    value = join(value, other_core(value))
    value = join(value, along_x(value, 1), along_x(value, 2), along_x(value, 3))
    return join(value, along_y(value, 1), along_y(value, 2), along_y(value, 3))


EMBED_ROWS = 2048


def embed_kernel(x_ref, w_in_ref, b_in_ref, w_out_ref, b_out_ref, o_ref):
    for start in range(0, EMBED_ROWS, BLOCK):
        rows = pl.ds(start, BLOCK)
        v = jnp.dot(x_ref[rows, :], w_in_ref[...], preferred_element_type=jnp.float32)
        v = 0.5 * (v + b_in_ref[...])
        hidden = (v + v * jnp.tanh(v)).astype(jnp.bfloat16)
        out = jnp.dot(hidden, w_out_ref[...], preferred_element_type=jnp.float32)
        o_ref[rows, :] = ((out + b_out_ref[...]) * SCORE_SCALE).astype(jnp.bfloat16)


def embed_orders(features, w_in, bias_in, w_out, bias_out):
    rows = features.shape[0]
    whole = lambda i: (0, 0)
    return pl.pallas_call(
        embed_kernel,
        out_shape=jax.ShapeDtypeStruct((rows, EMB), jnp.bfloat16),
        grid=(rows // EMBED_ROWS,),
        in_specs=[
            pl.BlockSpec((EMBED_ROWS, EMB), lambda i: (i, 0)),
            pl.BlockSpec((EMB, HID), whole),
            pl.BlockSpec((1, HID), whole),
            pl.BlockSpec((HID, EMB), whole),
            pl.BlockSpec((1, EMB), whole),
        ],
        out_specs=pl.BlockSpec((EMBED_ROWS, EMB), lambda i: (i, 0)),
        compiler_params=pltpu.CompilerParams(vmem_limit_bytes=VMEM_LIMIT),
        cost_estimate=pl.CostEstimate(
            flops=4 * rows * EMB * HID, bytes_accessed=4 * rows * EMB, transcendentals=rows * HID
        ),
        name="embed_orders",
    )(features, w_in, bias_in.reshape(1, HID), w_out, bias_out.reshape(1, EMB))


def list_kernel(adj_ref, order_count_ref, courier_count_ref, place_ref, list_ref, rounds_ref):
    zone, sub = place_ref[0], place_ref[1]

    def put(n, order, courier, slot, keep):
        list_ref[n] = order * 65536 + courier * 256 + slot
        return n + keep

    def one_pair(p, n):
        b = p // ADJ
        c = adj_ref[p]
        z = c // SUBS
        mine = jnp.where(c % SUBS == sub, 1, 0)
        order_two = mine * jnp.where(order_count_ref[b] > HALF, 1, 0)
        courier_two = mine * jnp.where(courier_count_ref[z] > HALF, 1, 0)
        slot = 2 * slot_of(z + ZONES, zone + 2 * ZONES)
        n = put(n, 2 * b, 2 * z, slot, mine)
        n = put(n, 2 * b, 2 * z + 1, slot + 1, courier_two)
        n = put(n, 2 * b + 1, 2 * z, slot, order_two)
        return put(n, 2 * b + 1, 2 * z + 1, slot + 1, order_two * courier_two)

    n = lax.fori_loop(0, OB_DEV * ADJ, one_pair, jnp.int32(0))
    for i in range(REST):
        list_ref[n + i] = jnp.int32(NO_ORDER * 65536 + NO_COURIER * 256)
    rounds_ref[0] = (n + REST - 1) // REST


def work_list(adjacency, order_count, courier_count, place):
    smem = pl.BlockSpec(memory_space=pltpu.SMEM)
    return pl.pallas_call(
        list_kernel,
        out_shape=(
            jax.ShapeDtypeStruct((LIST_SIZE,), jnp.int32),
            jax.ShapeDtypeStruct((1,), jnp.int32),
        ),
        in_specs=[smem] * 4,
        out_specs=(smem, smem),
        name="work_list",
    )(adjacency.reshape(-1), order_count, courier_count, place)


def pass_kernel(sum_couriers, list_ref, rounds_ref, summed_ref, kept_ref, weight_ref, live_ref, out_ref, w_ref, r_ref, m_ref):
    summed_blocks, kept_blocks = weight_ref.shape[0], live_ref.shape[0]
    rounds = rounds_ref[0]
    weight = weight_ref[...]

    high = weight.astype(jnp.bfloat16).astype(jnp.float32)
    low = weight - high
    blank = jnp.zeros((64 - 2 * summed_blocks, 128), jnp.float32)
    for part in range(2):
        rows = []
        for value in (high, low):
            rows += [value[:, part * 128 : part * 128 + 128], value[:, HALF + part * 128 : HALF + part * 128 + 128]]
            if summed_blocks < 32:
                rows.append(blank)
        w_ref[part * 128 : part * 128 + 128, :] = jnp.transpose(jnp.concatenate(rows, axis=0)).astype(jnp.bfloat16)
    r_ref[...] = jnp.zeros(r_ref.shape, jnp.float32)
    lanes = lax.broadcasted_iota(jnp.int32, (1, 128), 1) % 64

    def piece(e):
        order, courier, slot = e // 65536, e // 256 % 256, e % 256
        row = jnp.minimum(order, 2 * OB_DEV - 1)
        return (courier, order, slot, row) if sum_couriers else (order, courier, row, slot)

    def sides(s_row, k_row):
        left = summed_ref[pl.ds(pl.multiple_of(s_row * HALF, HALF), HALF), :]
        right = kept_ref[pl.ds(pl.multiple_of(k_row * HALF, HALF), HALF), :]
        return left, right

    def scores(left, right):
        return lax.dot_general(left, right, (((1,), (1,)), ((), ())), preferred_element_type=jnp.float32)

    def weighted(s, s_row, k_row):
        left, right = sides(s_row, k_row)
        lane = (s % 2) * summed_blocks + s // 2
        ones = jnp.where(lanes == lane, 1.0, 0.0).astype(jnp.bfloat16)
        left = jnp.concatenate([left, w_ref[...]], axis=1)
        right = jnp.concatenate([right, jnp.broadcast_to(ones, (HALF, 128))], axis=1)
        return scores(left, right)

    def steps(first, count):
        todo = [piece(list_ref[first + t]) for t in range(count)]
        sums = [
            jnp.sum(jnp.exp2(weighted(s, s_row, k_row)).reshape(HALF // 8, 8, HALF), axis=0)
            for s, _, s_row, k_row in todo
        ]
        for (_, k, _, _), part in zip(todo, sums):
            r_ref[k // 2, k % 2] += part

    large = rounds // (UNROLL // REST)

    def large_step(i, carry):
        steps(i * UNROLL, UNROLL)
        return carry

    def small_step(i, carry):
        steps(i * REST, REST)
        return carry

    lax.fori_loop(0, large, large_step, 0)
    lax.fori_loop(large * (UNROLL // REST), rounds, small_step, 0)

    live_weight = jnp.where(weight > 0.5 * LOWEST, jnp.abs(weight), 0.0)
    bad = jnp.where(jnp.max(live_weight) <= 128.0, 0.0, 1.0)
    for half in range(2):
        cut = slice(half * HALF, (half + 1) * HALF)
        total = jnp.sum(r_ref[0:kept_blocks, half], axis=1)
        live = live_ref[:, cut] > 0.5 * LOWEST
        fine = (total >= 2.0**-86) & (total <= 2.0**126)
        bad = bad + jnp.max(jnp.where(live, jnp.where(fine, 0.0, 1.0), 0.0))
        out_ref[:, cut] = jnp.where(live, jnp.log2(jnp.where(live, total, 1.0)), LOWEST)

    @pl.when(bad > 0.0)
    def _():
        m_ref[...] = jnp.full(m_ref.shape, LOWEST, jnp.float32)
        r_ref[...] = jnp.zeros(r_ref.shape, jnp.float32)

        def one_piece(i, carry):
            s, k, s_row, k_row = piece(list_ref[i])
            block = jnp.minimum(s // 2, summed_blocks - 1)
            w = weight_ref[pl.ds(block, 1), pl.ds(pl.multiple_of((s % 2) * HALF, HALF), HALF)]
            column = jnp.transpose(jnp.broadcast_to(w, (128, HALF)))
            x = scores(*sides(s_row, k_row)) + jnp.concatenate([column, column], axis=1)
            before = m_ref[k // 2, k % 2, 0:1]
            after = jnp.maximum(before, jnp.max(x, axis=0, keepdims=True))
            scaled = r_ref[k // 2, k % 2, 0:1] * jnp.exp2(before - after)
            m_ref[k // 2, k % 2, 0:1] = after
            r_ref[k // 2, k % 2, 0:1] = scaled + jnp.sum(jnp.exp2(x - after), axis=0, keepdims=True)
            return carry

        lax.fori_loop(0, rounds * REST, one_piece, 0)
        for half in range(2):
            cut = slice(half * HALF, (half + 1) * HALF)
            live = live_ref[:, cut] > 0.5 * LOWEST
            total = jnp.where(live, r_ref[0:kept_blocks, half, 0, :], 1.0)
            out_ref[:, cut] = jnp.where(live, m_ref[0:kept_blocks, half, 0, :] + jnp.log2(total), LOWEST)


def half_sweep(sum_couriers, work, rounds, summed, kept, weight, live, name):
    smem = pl.BlockSpec(memory_space=pltpu.SMEM)
    vmem = pl.BlockSpec(memory_space=pltpu.VMEM)
    summed_blocks, kept_blocks = weight.shape[0], live.shape[0]

    def kernel(*refs):
        pass_kernel(sum_couriers, *refs)

    def first_kernel(work_ref, rounds_ref, *refs):
        parts, (kept_ref, weight_ref, live_ref, out_ref, summed_ref, w_ref, r_ref, m_ref, sem) = refs[:PARTS], refs[PARTS:]
        rows = summed_ref.shape[0] // PARTS
        copies = [
            pltpu.make_async_copy(part, summed_ref.at[pl.ds(i * rows, rows), :], sem.at[i])
            for i, part in enumerate(parts)
        ]
        for copy in copies:
            copy.start()
        for copy in copies:
            copy.wait()
        pass_kernel(
            sum_couriers, work_ref, rounds_ref, summed_ref, kept_ref, weight_ref, live_ref, out_ref, w_ref, r_ref, m_ref
        )

    first = isinstance(summed, list)
    out_shape = jax.ShapeDtypeStruct((kept_blocks, BLOCK), jnp.float32)
    scratch = [
        pltpu.VMEM((HALF, 128), jnp.bfloat16),
        pltpu.VMEM((kept_blocks + 1, 2, 8, HALF), jnp.float32),
        pltpu.VMEM((kept_blocks + 1, 2, 8, HALF), jnp.float32),
    ]
    return pl.pallas_call(
        first_kernel if first else kernel,
        out_shape=(out_shape, jax.ShapeDtypeStruct((ZONES * BLOCK, EMB), jnp.bfloat16)) if first else out_shape,
        in_specs=[smem, smem] + ([pl.BlockSpec(memory_space=pl.ANY)] * PARTS if first else [vmem]) + [vmem] * 3,
        out_specs=(vmem, vmem) if first else vmem,
        scratch_shapes=scratch + ([pltpu.SemaphoreType.DMA((PARTS,))] if first else []),
        compiler_params=pltpu.CompilerParams(vmem_limit_bytes=VMEM_LIMIT),
        cost_estimate=pl.CostEstimate(flops=28 * 2 * 512 * 512 * 128, bytes_accessed=6 << 20, transcendentals=28 * 512 * 512),
        name=name,
    )(work, rounds, *(summed if first else [summed]), kept, weight, live)


def shards(
    order_features,
    w_in,
    bias_in,
    w_out,
    bias_out,
    courier_embed,
    courier_cap,
    adjacency,
    order_count,
    courier_count,
):
    sub = lax.axis_index("sub")
    positions = jnp.arange(BLOCK, dtype=jnp.int32)

    row = gather_row(courier_embed)
    own_log_cap = jnp.where(
        positions < courier_count[0], jnp.log2(courier_cap.astype(jnp.float32)), LOWEST
    )
    row, order_features, own_log_cap = lax.optimization_barrier((row, order_features, own_log_cap))
    couriers = gather_plane(row)
    log_cap = lax.all_to_all(
        jnp.broadcast_to(own_log_cap[None], (ZONES, BLOCK)), "zone", 0, 0, tiled=True
    )
    courier_live = log_cap > 0.5 * LOWEST
    counts = jnp.sum(courier_live.astype(jnp.int32), axis=1)

    orders = embed_orders(order_features, w_in, bias_in, w_out, bias_out)
    place = jnp.stack([lax.axis_index("zone"), sub])
    work, rounds = work_list(adjacency, order_count, counts, place)

    mine = adjacency % SUBS == sub
    order_live = positions[None, :] < order_count[:, None]
    order_here = jnp.where(order_live & jnp.any(mine, axis=1, keepdims=True), 0.0, LOWEST)
    named = jnp.any(
        (adjacency.reshape(-1)[None, :] == jnp.arange(ZONES)[:, None] * SUBS + sub), axis=1, keepdims=True
    )
    courier_here = jnp.where(courier_live & named, 0.0, LOWEST)

    def order_dual_of(partial):
        return jnp.where(order_live, -join_subs(partial), LOWEST)

    def courier_pass(order_dual, name):
        return half_sweep(False, work, rounds, orders, couriers, order_dual, courier_here, name)

    courier_dual = jnp.where(courier_live, 0.0, LOWEST)
    partial, couriers = half_sweep(True, work, rounds, couriers, orders, courier_dual, order_here, "orders_1")
    order_dual = order_dual_of(partial)
    sums = join_zones(courier_pass(order_dual, "couriers_1"))
    courier_dual = jnp.where(courier_live, log_cap - sums, LOWEST)
    order_dual = order_dual_of(half_sweep(True, work, rounds, couriers, orders, courier_dual, order_here, "orders_2"))
    partial = courier_pass(order_dual, "couriers_2")
    parts = lax.all_to_all(partial, "zone", 0, 0, tiled=True)
    highest = jnp.max(parts, axis=0)
    total = highest + jnp.log2(jnp.sum(jnp.exp2(parts - highest[None]), axis=0))
    courier_out = jnp.where(positions < courier_count[0], DUAL_SCALE * (own_log_cap - total), 0.0)
    order_out = jnp.where(order_live, DUAL_SCALE * order_dual, 0.0)
    return order_out.reshape(-1), courier_out


def solution(mesh):
    return jax.shard_map(
        shards,
        mesh=mesh,
        in_specs=(
            P("zone", None),
            P(),
            P(),
            P(),
            P(),
            P(("zone", "sub"), None),
            P(("zone", "sub")),
            P("zone", None),
            P("zone"),
            P(("zone", "sub")),
        ),
        out_specs=(P("zone"), P(("zone", "sub"))),
        check_vma=False,
    )
```

```python
import math

import jax
import jax.numpy as jnp
from jax import lax
from jax.experimental import pallas as pl
from jax.experimental.pallas import tpu as pltpu
from jax.sharding import PartitionSpec as P

BLOCK = 512
EMB = 128
HID = 512
ADJ = 8
OB_DEV = 16
ZONES = 32
SUBS = 4
HALF = 256
UNROLL = 32
REST = 8
MOST_ENTRIES = 256
LIST_SIZE = MOST_ENTRIES + 2 * REST
NO_ORDER = 2 * OB_DEV
NO_COURIER = 2 * ZONES

TEMPER = 0.2
LOWEST = -1e30
SCORE_SCALE = math.log2(math.e) / (TEMPER * math.sqrt(EMB))
DUAL_SCALE = TEMPER * math.log(2.0)

VMEM_LIMIT = 16 * 1024 * 1024
PARTS = 8


def zone_of(y, x, core):
    return ((y % 4) * 4 + (x % 4)) * 2 + core


PLACES = [(y, x, core) for y in range(4) for x in range(4) for core in range(2)]


def other_core(value):
    return lax.ppermute(value, "zone", [(zone_of(y, x, c), zone_of(y, x, 1 - c)) for y, x, c in PLACES])


def along_z(value, step):
    return lax.ppermute(value, "sub", [(i, (i + step) % SUBS) for i in range(SUBS)])


def plane_step(value, stage, step):
    pairs = []
    for y, x, c in PLACES:
        to = (y, x + step, c) if stage == c else (y + step, x, c)
        pairs.append((zone_of(y, x, c), zone_of(*to)))
    return lax.ppermute(value, "zone", pairs)


def gather_row(block):
    return jnp.concatenate([block] + [plane_step(block, 0, step) for step in (1, 2, 3)], axis=0)


def gather_plane(row, meanwhile):
    own = [row] + [plane_step(row, 1, step) for step in (1, 2, 3)]
    swapped = [other_core(row)]
    own[1], own[2], own[3], meanwhile = lax.optimization_barrier((own[1], own[2], own[3], meanwhile))
    return own + swapped + [other_core(part) for part in own[1:]], meanwhile


def slot_of(zone, me):
    back_x = ((me >> 1) - (zone >> 1)) & 3
    back_y = ((me >> 3) - (zone >> 3)) & 3
    odd = zone & 1
    first = jnp.where(odd == 0, back_x, back_y)
    second = jnp.where(odd == 0, back_y, back_x)
    return ((me ^ zone) & 1) * 16 + second * 4 + first


def join(*parts):
    highest = parts[0]
    for part in parts[1:]:
        highest = jnp.maximum(highest, part)
    total = jnp.exp2(parts[0] - highest)
    for part in parts[1:]:
        total = total + jnp.exp2(part - highest)
    return highest + jnp.log2(total)


def join_subs(value):
    return join(value, along_z(value, 1), along_z(value, 2), along_z(value, 3))


def join_zones(value):
    value = join(value, other_core(value))
    for stage in range(2):
        value = join(value, *[plane_step(value, stage, step) for step in (1, 2, 3)])
    return value


EMBED_ROWS = 2048


def embed_kernel(x_hbm, w_in_hbm, b_in_hbm, w_out_hbm, b_out_hbm, o_ref, x_ref, w_in_ref, b_in_ref, w_out_ref, b_out_ref, sem):
    steps = x_ref.shape[0] // EMBED_ROWS

    def rows_copy(i):
        rows = pl.ds(pl.multiple_of(i * EMBED_ROWS, EMBED_ROWS), EMBED_ROWS)
        return pltpu.make_async_copy(x_hbm.at[rows, :], x_ref.at[rows, :], sem.at[i])

    parameters = [
        pltpu.make_async_copy(source, target, sem.at[steps + i])
        for i, (source, target) in enumerate(
            [(w_in_hbm, w_in_ref), (b_in_hbm, b_in_ref), (w_out_hbm, w_out_ref), (b_out_hbm, b_out_ref)]
        )
    ]
    for copy in parameters:
        copy.start()
    for i in range(steps):
        rows_copy(i).start()
    for copy in parameters:
        copy.wait()

    def one_step(i, carry):
        rows_copy(i).wait()
        for start in range(0, EMBED_ROWS, BLOCK):
            rows = pl.ds(pl.multiple_of(i * EMBED_ROWS + start, BLOCK), BLOCK)
            v = jnp.dot(x_ref[rows, :], w_in_ref[...], preferred_element_type=jnp.float32)
            v = 0.5 * (v + b_in_ref[...])
            hidden = (v + v * jnp.tanh(v)).astype(jnp.bfloat16)
            out = jnp.dot(hidden, w_out_ref[...], preferred_element_type=jnp.float32)
            o_ref[rows, :] = ((out + b_out_ref[...]) * SCORE_SCALE).astype(jnp.bfloat16)
        return carry

    lax.fori_loop(0, steps, one_step, 0)


def embed_orders(features, w_in, bias_in, w_out, bias_out):
    rows = features.shape[0]
    operands = (features, w_in, bias_in.reshape(1, HID), w_out, bias_out.reshape(1, EMB))
    return pl.pallas_call(
        embed_kernel,
        out_shape=jax.ShapeDtypeStruct((rows, EMB), jnp.bfloat16),
        in_specs=[pl.BlockSpec(memory_space=pltpu.HBM)] * len(operands),
        out_specs=pl.BlockSpec(memory_space=pltpu.VMEM),
        scratch_shapes=[pltpu.VMEM(value.shape, value.dtype) for value in operands]
        + [pltpu.SemaphoreType.DMA((rows // EMBED_ROWS + 4,))],
        compiler_params=pltpu.CompilerParams(vmem_limit_bytes=VMEM_LIMIT),
        cost_estimate=pl.CostEstimate(
            flops=4 * rows * EMB * HID, bytes_accessed=4 * rows * EMB, transcendentals=rows * HID
        ),
        name="embed_orders",
    )(*[pltpu.with_memory_space_constraint(value, pltpu.HBM) for value in operands])


def list_kernel(pair_ref, two_ref, list_ref, rounds_ref):
    def one_pair(p, n):
        e = pair_ref[p]
        mine = (e >> 24) & 1
        order_two = (e >> 25) & 1
        courier_two = mine * two_ref[(e >> 9) & 31]
        e = e & 0xFFFFFF
        list_ref[n] = e
        n = n + mine
        list_ref[n] = e + 257
        n = n + courier_two
        list_ref[n] = e + 65536
        n = n + order_two
        list_ref[n] = e + 65536 + 257
        return n + (order_two & courier_two)

    n = lax.fori_loop(0, OB_DEV * ADJ, one_pair, jnp.int32(0), unroll=8)
    for i in range(REST):
        list_ref[n + i] = jnp.int32(NO_ORDER * 65536 + NO_COURIER * 256)
    rounds_ref[0] = (n + REST - 1) // REST


def work_list(adjacency, order_count, courier_count):
    zone, sub = lax.axis_index("zone"), lax.axis_index("sub")
    flat = adjacency.reshape(-1)
    z = flat >> 2
    mine = jnp.where((flat & 3) == sub, 1, 0)
    two = jnp.repeat(jnp.where(order_count > HALF, 1, 0), ADJ)
    block = jnp.arange(OB_DEV * ADJ, dtype=jnp.int32) // ADJ
    entry = (2 * block << 16) + (2 * z << 8) + 2 * slot_of(z, zone)
    pairs = entry + (mine << 24) + ((mine * two) << 25)
    smem = pl.BlockSpec(memory_space=pltpu.SMEM)
    return pl.pallas_call(
        list_kernel,
        out_shape=(
            jax.ShapeDtypeStruct((LIST_SIZE,), jnp.int32),
            jax.ShapeDtypeStruct((1,), jnp.int32),
        ),
        in_specs=[smem] * 2,
        out_specs=(smem, smem),
        compiler_params=pltpu.CompilerParams(vmem_limit_bytes=1024 * 1024),
        name="work_list",
    )(pairs.astype(jnp.int32), jnp.where(courier_count > HALF, 1, 0).astype(jnp.int32))


def pass_kernel(sum_couriers, list_ref, rounds_ref, summed_ref, kept_ref, weight_ref, live_ref, out_ref, w_ref, r_ref, m_ref):
    summed_blocks, kept_blocks = weight_ref.shape[0], live_ref.shape[0]
    rounds = rounds_ref[0]
    weight = weight_ref[...]

    high = weight.astype(jnp.bfloat16).astype(jnp.float32)
    low = weight - high
    blank = jnp.zeros((64 - 2 * summed_blocks, 128), jnp.float32)
    for part in range(2):
        rows = []
        for value in (high, low):
            rows += [value[:, part * 128 : part * 128 + 128], value[:, HALF + part * 128 : HALF + part * 128 + 128]]
            if summed_blocks < 32:
                rows.append(blank)
        w_ref[part * 128 : part * 128 + 128, :] = jnp.transpose(jnp.concatenate(rows, axis=0)).astype(jnp.bfloat16)
    r_ref[...] = jnp.zeros(r_ref.shape, jnp.float32)
    lanes = lax.broadcasted_iota(jnp.int32, (1, 128), 1) % 64

    def piece(e):
        order, courier, slot = e // 65536, e // 256 % 256, e % 256
        row = jnp.minimum(order, 2 * OB_DEV - 1)
        return (courier, order, slot, row) if sum_couriers else (order, courier, row, slot)

    def sides(s_row, k_row):
        left = summed_ref[pl.ds(pl.multiple_of(s_row * HALF, HALF), HALF), :]
        right = kept_ref[pl.ds(pl.multiple_of(k_row * HALF, HALF), HALF), :]
        return left, right

    def scores(left, right):
        return lax.dot_general(left, right, (((1,), (1,)), ((), ())), preferred_element_type=jnp.float32)

    def weighted(s, s_row, k_row):
        left, right = sides(s_row, k_row)
        lane = (s % 2) * summed_blocks + s // 2
        ones = jnp.where(lanes == lane, 1.0, 0.0).astype(jnp.bfloat16)
        left = jnp.concatenate([left, w_ref[...]], axis=1)
        right = jnp.concatenate([right, jnp.broadcast_to(ones, (HALF, 128))], axis=1)
        return scores(left, right)

    def steps(first, count):
        todo = [piece(list_ref[first + t]) for t in range(count)]
        sums = [
            jnp.sum(jnp.exp2(weighted(s, s_row, k_row)).reshape(HALF // 8, 8, HALF), axis=0)
            for s, _, s_row, k_row in todo
        ]
        for (_, k, _, _), part in zip(todo, sums):
            r_ref[k // 2, k % 2] += part

    large = rounds // (UNROLL // REST)

    def large_step(i, carry):
        steps(i * UNROLL, UNROLL)
        return carry

    def small_step(i, carry):
        steps(i * REST, REST)
        return carry

    lax.fori_loop(0, large, large_step, 0)
    lax.fori_loop(large * (UNROLL // REST), rounds, small_step, 0)

    live_weight = jnp.where(weight > 0.5 * LOWEST, jnp.abs(weight), 0.0)
    bad = jnp.where(jnp.max(live_weight) <= 128.0, 0.0, 1.0)
    for half in range(2):
        cut = slice(half * HALF, (half + 1) * HALF)
        total = jnp.sum(r_ref[0:kept_blocks, half], axis=1)
        live = live_ref[:, cut] > 0.5 * LOWEST
        fine = (total >= 2.0**-86) & (total <= 2.0**126)
        bad = bad + jnp.max(jnp.where(live, jnp.where(fine, 0.0, 1.0), 0.0))
        out_ref[:, cut] = jnp.where(live, jnp.log2(jnp.where(live, total, 1.0)), LOWEST)

    @pl.when(bad > 0.0)
    def _():
        m_ref[...] = jnp.full(m_ref.shape, LOWEST, jnp.float32)
        r_ref[...] = jnp.zeros(r_ref.shape, jnp.float32)

        def one_piece(i, carry):
            s, k, s_row, k_row = piece(list_ref[i])
            block = jnp.minimum(s // 2, summed_blocks - 1)
            w = weight_ref[pl.ds(block, 1), pl.ds(pl.multiple_of((s % 2) * HALF, HALF), HALF)]
            column = jnp.transpose(jnp.broadcast_to(w, (128, HALF)))
            x = scores(*sides(s_row, k_row)) + jnp.concatenate([column, column], axis=1)
            before = m_ref[k // 2, k % 2, 0:1]
            after = jnp.maximum(before, jnp.max(x, axis=0, keepdims=True))
            scaled = r_ref[k // 2, k % 2, 0:1] * jnp.exp2(before - after)
            m_ref[k // 2, k % 2, 0:1] = after
            r_ref[k // 2, k % 2, 0:1] = scaled + jnp.sum(jnp.exp2(x - after), axis=0, keepdims=True)
            return carry

        lax.fori_loop(0, rounds * REST, one_piece, 0)
        for half in range(2):
            cut = slice(half * HALF, (half + 1) * HALF)
            live = live_ref[:, cut] > 0.5 * LOWEST
            total = jnp.where(live, r_ref[0:kept_blocks, half, 0, :], 1.0)
            out_ref[:, cut] = jnp.where(live, m_ref[0:kept_blocks, half, 0, :] + jnp.log2(total), LOWEST)


def half_sweep(sum_couriers, work, rounds, summed, kept, weight, live, name):
    smem = pl.BlockSpec(memory_space=pltpu.SMEM)
    vmem = pl.BlockSpec(memory_space=pltpu.VMEM)
    summed_blocks, kept_blocks = weight.shape[0], live.shape[0]

    def kernel(*refs):
        pass_kernel(sum_couriers, *refs)

    def first_kernel(work_ref, rounds_ref, *refs):
        parts, (kept_ref, weight_ref, live_ref, out_ref, summed_ref, w_ref, r_ref, m_ref, sem) = refs[:PARTS], refs[PARTS:]
        rows = summed_ref.shape[0] // PARTS
        copies = [
            pltpu.make_async_copy(part, summed_ref.at[pl.ds(i * rows, rows), :], sem.at[i])
            for i, part in enumerate(parts)
        ]
        for copy in copies:
            copy.start()
        for copy in copies:
            copy.wait()
        pass_kernel(
            sum_couriers, work_ref, rounds_ref, summed_ref, kept_ref, weight_ref, live_ref, out_ref, w_ref, r_ref, m_ref
        )

    first = isinstance(summed, list)
    out_shape = jax.ShapeDtypeStruct((kept_blocks, BLOCK), jnp.float32)
    scratch = [
        pltpu.VMEM((HALF, 128), jnp.bfloat16),
        pltpu.VMEM((kept_blocks + 1, 2, 8, HALF), jnp.float32),
        pltpu.VMEM((kept_blocks + 1, 2, 8, HALF), jnp.float32),
    ]
    return pl.pallas_call(
        first_kernel if first else kernel,
        out_shape=(out_shape, jax.ShapeDtypeStruct((ZONES * BLOCK, EMB), jnp.bfloat16)) if first else out_shape,
        in_specs=[smem, smem] + ([pl.BlockSpec(memory_space=pl.ANY)] * PARTS if first else [vmem]) + [vmem] * 3,
        out_specs=(vmem, vmem) if first else vmem,
        scratch_shapes=scratch + ([pltpu.SemaphoreType.DMA((PARTS,))] if first else []),
        compiler_params=pltpu.CompilerParams(vmem_limit_bytes=VMEM_LIMIT),
        cost_estimate=pl.CostEstimate(flops=28 * 2 * 512 * 512 * 128, bytes_accessed=6 << 20, transcendentals=28 * 512 * 512),
        name=name,
    )(work, rounds, *(summed if first else [summed]), kept, weight, live)


def shards(
    order_features,
    w_in,
    bias_in,
    w_out,
    bias_out,
    courier_embed,
    courier_cap,
    adjacency,
    order_count,
    courier_count,
):
    sub = lax.axis_index("sub")
    positions = jnp.arange(BLOCK, dtype=jnp.int32)

    row = gather_row(courier_embed)
    own_log_cap = jnp.where(
        positions < courier_count[0], jnp.log2(courier_cap.astype(jnp.float32)), LOWEST
    )
    row, bias_in, adjacency, order_count = lax.optimization_barrier((row, bias_in, adjacency, order_count))
    orders = embed_orders(order_features, w_in, bias_in, w_out, bias_out)
    couriers, orders = gather_plane(row, orders)
    log_cap = lax.all_to_all(
        jnp.broadcast_to(own_log_cap[None], (ZONES, BLOCK)), "zone", 0, 0, tiled=True
    )
    courier_live = log_cap > 0.5 * LOWEST
    counts = jnp.sum(courier_live.astype(jnp.int32), axis=1)

    work, rounds = work_list(adjacency, order_count, counts)

    mine = adjacency % SUBS == sub
    order_live = positions[None, :] < order_count[:, None]
    order_here = jnp.where(order_live & jnp.any(mine, axis=1, keepdims=True), 0.0, LOWEST)
    named = jnp.any(
        (adjacency.reshape(-1)[None, :] == jnp.arange(ZONES)[:, None] * SUBS + sub), axis=1, keepdims=True
    )
    courier_here = jnp.where(courier_live & named, 0.0, LOWEST)

    def order_dual_of(partial):
        return jnp.where(order_live, -join_subs(partial), LOWEST)

    def courier_pass(order_dual, name):
        return half_sweep(False, work, rounds, orders, couriers, order_dual, courier_here, name)

    courier_dual = jnp.where(courier_live, 0.0, LOWEST)
    partial, couriers = half_sweep(True, work, rounds, couriers, orders, courier_dual, order_here, "orders_1")
    order_dual = order_dual_of(partial)
    sums = join_zones(courier_pass(order_dual, "couriers_1"))
    courier_dual = jnp.where(courier_live, log_cap - sums, LOWEST)
    order_dual = order_dual_of(half_sweep(True, work, rounds, couriers, orders, courier_dual, order_here, "orders_2"))
    partial = courier_pass(order_dual, "couriers_2")
    parts = lax.all_to_all(partial, "zone", 0, 0, tiled=True)
    highest = jnp.max(parts, axis=0)
    total = highest + jnp.log2(jnp.sum(jnp.exp2(parts - highest[None]), axis=0))
    courier_out = jnp.where(positions < courier_count[0], DUAL_SCALE * (own_log_cap - total), 0.0)
    order_out = jnp.where(order_live, DUAL_SCALE * order_dual, 0.0)
    return order_out.reshape(-1), courier_out


def solution(mesh):
    return jax.shard_map(
        shards,
        mesh=mesh,
        in_specs=(
            P("zone", None),
            P(),
            P(),
            P(),
            P(),
            P(("zone", "sub"), None),
            P(("zone", "sub")),
            P("zone", None),
            P("zone"),
            P(("zone", "sub")),
        ),
        out_specs=(P("zone"), P(("zone", "sub"))),
        check_vma=False,
    )
```

```python
import math

import jax
import jax.numpy as jnp
from jax import lax
from jax.experimental import pallas as pl
from jax.experimental.pallas import tpu as pltpu
from jax.sharding import PartitionSpec as P

BLOCK = 512
EMB = 128
HID = 512
ADJ = 8
OB_DEV = 16
ZONES = 32
SUBS = 4
HALF = 256
COURIER_ROWS = BLOCK + 16
UNROLL = 32
REST = 8
MOST_ENTRIES = 256
LIST_SIZE = MOST_ENTRIES + 2 * REST
NO_ORDER = 2 * OB_DEV
NO_COURIER = 2 * ZONES

TEMPER = 0.2
LOWEST = -1e30
SCORE_SCALE = math.log2(math.e) / (TEMPER * math.sqrt(EMB))
DUAL_SCALE = TEMPER * math.log(2.0)

VMEM_LIMIT = 16 * 1024 * 1024
PARTS = 8


def zone_of(y, x, core):
    return ((y % 4) * 4 + (x % 4)) * 2 + core


PLACES = [(y, x, core) for y in range(4) for x in range(4) for core in range(2)]


def other_core(value):
    return lax.ppermute(value, "zone", [(zone_of(y, x, c), zone_of(y, x, 1 - c)) for y, x, c in PLACES])


def along_z(value, step):
    return lax.ppermute(value, "sub", [(i, (i + step) % SUBS) for i in range(SUBS)])


def plane_step(value, stage, step):
    pairs = []
    for y, x, c in PLACES:
        to = (y, x + step, c) if stage == c else (y + step, x, c)
        pairs.append((zone_of(y, x, c), zone_of(*to)))
    return lax.ppermute(value, "zone", pairs)


def gather_row(block):
    return jnp.concatenate([block] + [plane_step(block, 0, step) for step in (1, 2, 3)], axis=0)


def gather_plane(row, meanwhile):
    own = [row] + [plane_step(row, 1, step) for step in (1, 2, 3)]
    swapped = [other_core(row)]
    own[1], own[2], own[3], meanwhile = lax.optimization_barrier((own[1], own[2], own[3], meanwhile))
    return own + swapped + [other_core(part) for part in own[1:]], meanwhile


def slot_of(zone, me):
    back_x = ((me >> 1) - (zone >> 1)) & 3
    back_y = ((me >> 3) - (zone >> 3)) & 3
    odd = zone & 1
    first = jnp.where(odd == 0, back_x, back_y)
    second = jnp.where(odd == 0, back_y, back_x)
    return ((me ^ zone) & 1) * 16 + second * 4 + first


def join(*parts):
    highest = parts[0]
    for part in parts[1:]:
        highest = jnp.maximum(highest, part)
    total = jnp.exp2(parts[0] - highest)
    for part in parts[1:]:
        total = total + jnp.exp2(part - highest)
    return highest + jnp.log2(total)


def join_subs(value):
    return join(value, along_z(value, 1), along_z(value, 2), along_z(value, 3))


def join_zones(value):
    value = join(value, other_core(value))
    for stage in range(2):
        value = join(value, *[plane_step(value, stage, step) for step in (1, 2, 3)])
    return value


EMBED_ROWS = 4096


def embed_kernel(x_hbm, w_in_hbm, b_in_hbm, w_out_hbm, b_out_hbm, o_ref, x_ref, w_in_ref, b_in_ref, w_out_ref, b_out_ref, sem):
    steps = x_ref.shape[0] // EMBED_ROWS

    def rows_copy(i):
        rows = pl.ds(pl.multiple_of(i * EMBED_ROWS, EMBED_ROWS), EMBED_ROWS)
        return pltpu.make_async_copy(x_hbm.at[rows, :], x_ref.at[rows, :], sem.at[i])

    parameters = [
        pltpu.make_async_copy(source, target, sem.at[steps + i])
        for i, (source, target) in enumerate(
            [(w_in_hbm, w_in_ref), (b_in_hbm, b_in_ref), (w_out_hbm, w_out_ref), (b_out_hbm, b_out_ref)]
        )
    ]
    for copy in parameters:
        copy.start()
    for i in range(steps):
        rows_copy(i).start()
    for copy in parameters:
        copy.wait()

    def one_step(i, carry):
        rows_copy(i).wait()
        for start in range(0, EMBED_ROWS, BLOCK):
            rows = pl.ds(pl.multiple_of(i * EMBED_ROWS + start, BLOCK), BLOCK)
            v = jnp.dot(x_ref[rows, :], w_in_ref[...], preferred_element_type=jnp.float32)
            v = 0.5 * (v + b_in_ref[...])
            hidden = (v + v * jnp.tanh(v)).astype(jnp.bfloat16)
            out = jnp.dot(hidden, w_out_ref[...], preferred_element_type=jnp.float32)
            o_ref[rows, :] = ((out + b_out_ref[...]) * SCORE_SCALE).astype(jnp.bfloat16)
        return carry

    lax.fori_loop(0, steps, one_step, 0)


def embed_orders(features, w_in, bias_in, w_out, bias_out):
    rows = features.shape[0]
    operands = (features, w_in, bias_in.reshape(1, HID), w_out, bias_out.reshape(1, EMB))
    return pl.pallas_call(
        embed_kernel,
        out_shape=jax.ShapeDtypeStruct((rows, EMB), jnp.bfloat16),
        in_specs=[pl.BlockSpec(memory_space=pltpu.HBM)] * len(operands),
        out_specs=pl.BlockSpec(memory_space=pltpu.VMEM),
        scratch_shapes=[pltpu.VMEM(value.shape, value.dtype) for value in operands]
        + [pltpu.SemaphoreType.DMA((rows // EMBED_ROWS + 4,))],
        compiler_params=pltpu.CompilerParams(vmem_limit_bytes=VMEM_LIMIT),
        cost_estimate=pl.CostEstimate(
            flops=4 * rows * EMB * HID, bytes_accessed=4 * rows * EMB, transcendentals=rows * HID
        ),
        name="embed_orders",
    )(*[pltpu.with_memory_space_constraint(value, pltpu.HBM) for value in operands])


def list_kernel(pair_ref, two_ref, list_ref, rounds_ref):
    def one_pair(p, n):
        e = pair_ref[p]
        mine = (e >> 24) & 1
        order_two = (e >> 25) & 1
        courier_two = mine * two_ref[(e >> 9) & 31]
        e = e & 0xFFFFFF
        list_ref[n] = e
        n = n + mine
        list_ref[n] = e + 257
        n = n + courier_two
        list_ref[n] = e + 65536
        n = n + order_two
        list_ref[n] = e + 65536 + 257
        return n + (order_two & courier_two)

    n = lax.fori_loop(0, OB_DEV * ADJ, one_pair, jnp.int32(0), unroll=8)
    for i in range(REST):
        list_ref[n + i] = jnp.int32(NO_ORDER * 65536 + NO_COURIER * 256)
    rounds_ref[0] = (n + REST - 1) // REST


def work_list(adjacency, order_count, courier_two, name):
    zone, sub = lax.axis_index("zone"), lax.axis_index("sub")
    flat = adjacency.reshape(-1)
    z = flat >> 2
    mine = jnp.where((flat & 3) == sub, 1, 0)
    two = jnp.repeat(jnp.where(order_count > HALF, 1, 0), ADJ)
    block = jnp.arange(OB_DEV * ADJ, dtype=jnp.int32) // ADJ
    entry = (2 * block << 16) + (2 * z << 8) + 2 * slot_of(z, zone)
    pairs = entry + (mine << 24) + ((mine * two) << 25)
    smem = pl.BlockSpec(memory_space=pltpu.SMEM)
    return pl.pallas_call(
        list_kernel,
        out_shape=(
            jax.ShapeDtypeStruct((LIST_SIZE,), jnp.int32),
            jax.ShapeDtypeStruct((1,), jnp.int32),
        ),
        in_specs=[smem] * 2,
        out_specs=(smem, smem),
        compiler_params=pltpu.CompilerParams(vmem_limit_bytes=1024 * 1024),
        name=name,
    )(pairs.astype(jnp.int32), courier_two)


def pass_kernel(sum_couriers, list_ref, rounds_ref, summed_ref, kept_ref, weight_ref, live_ref, out_ref, w_ref, r_ref, m_ref):
    summed_blocks, kept_blocks = weight_ref.shape[0], live_ref.shape[0]
    rounds = rounds_ref[0]
    weight = weight_ref[...]

    high = weight.astype(jnp.bfloat16).astype(jnp.float32)
    low = weight - high
    blank = jnp.zeros((64 - 2 * summed_blocks, 128), jnp.float32)
    for part in range(2):
        rows = []
        for value in (high, low):
            rows += [value[:, part * 128 : part * 128 + 128], value[:, HALF + part * 128 : HALF + part * 128 + 128]]
            if summed_blocks < 32:
                rows.append(blank)
        w_ref[part * 128 : part * 128 + 128, :] = jnp.transpose(jnp.concatenate(rows, axis=0)).astype(jnp.bfloat16)
    r_ref[...] = jnp.zeros(r_ref.shape, jnp.float32)
    lanes = lax.broadcasted_iota(jnp.int32, (1, 128), 1) % 64

    def piece(e):
        order, courier, slot = e >> 16, (e >> 8) & 255, e & 255
        order_row = jnp.minimum(order, 2 * OB_DEV - 1) * HALF
        courier_row = (slot >> 1) * COURIER_ROWS + (slot & 1) * HALF
        return (courier, order, courier_row, order_row) if sum_couriers else (order, courier, order_row, courier_row)

    def sides(s_row, k_row):
        left = summed_ref[pl.ds(pl.multiple_of(s_row, 16), HALF), :]
        right = kept_ref[pl.ds(pl.multiple_of(k_row, 16), HALF), :]
        return left, right

    def scores(left, right):
        return lax.dot_general(left, right, (((1,), (1,)), ((), ())), preferred_element_type=jnp.float32)

    def weighted(s, s_row, k_row):
        left, right = sides(s_row, k_row)
        lane = (s % 2) * summed_blocks + s // 2
        ones = jnp.where(lanes == lane, 1.0, 0.0).astype(jnp.bfloat16)
        left = jnp.concatenate([left, w_ref[...]], axis=1)
        right = jnp.concatenate([right, jnp.broadcast_to(ones, (HALF, 128))], axis=1)
        return scores(left, right)

    def steps(first, count):
        todo = [piece(list_ref[first + t]) for t in range(count)]
        sums = [
            jnp.sum(jnp.exp2(weighted(s, s_row, k_row)).reshape(HALF // 8, 8, HALF), axis=0)
            for s, _, s_row, k_row in todo
        ]
        for (_, k, _, _), part in zip(todo, sums):
            r_ref[k // 2, k % 2] += part

    large = rounds // (UNROLL // REST)

    def large_step(i, carry):
        steps(i * UNROLL, UNROLL)
        return carry

    def small_step(i, carry):
        steps(i * REST, REST)
        return carry

    lax.fori_loop(0, large, large_step, 0)
    lax.fori_loop(large * (UNROLL // REST), rounds, small_step, 0)

    live_weight = jnp.where(weight > 0.5 * LOWEST, jnp.abs(weight), 0.0)
    bad = jnp.where(jnp.max(live_weight) <= 128.0, 0.0, 1.0)
    for half in range(2):
        cut = slice(half * HALF, (half + 1) * HALF)
        total = jnp.sum(r_ref[0:kept_blocks, half], axis=1)
        live = live_ref[:, cut] > 0.5 * LOWEST
        fine = (total >= 2.0**-86) & (total <= 2.0**126)
        bad = bad + jnp.max(jnp.where(live, jnp.where(fine, 0.0, 1.0), 0.0))
        out_ref[:, cut] = jnp.where(live, jnp.log2(jnp.where(live, total, 1.0)), LOWEST)

    @pl.when(bad > 0.0)
    def _():
        m_ref[...] = jnp.full(m_ref.shape, LOWEST, jnp.float32)
        r_ref[...] = jnp.zeros(r_ref.shape, jnp.float32)

        def one_piece(i, carry):
            s, k, s_row, k_row = piece(list_ref[i])
            block = jnp.minimum(s // 2, summed_blocks - 1)
            w = weight_ref[pl.ds(block, 1), pl.ds(pl.multiple_of((s % 2) * HALF, HALF), HALF)]
            column = jnp.transpose(jnp.broadcast_to(w, (128, HALF)))
            x = scores(*sides(s_row, k_row)) + jnp.concatenate([column, column], axis=1)
            before = m_ref[k // 2, k % 2, 0:1]
            after = jnp.maximum(before, jnp.max(x, axis=0, keepdims=True))
            scaled = r_ref[k // 2, k % 2, 0:1] * jnp.exp2(before - after)
            m_ref[k // 2, k % 2, 0:1] = after
            r_ref[k // 2, k % 2, 0:1] = scaled + jnp.sum(jnp.exp2(x - after), axis=0, keepdims=True)
            return carry

        lax.fori_loop(0, rounds * REST, one_piece, 0)
        for half in range(2):
            cut = slice(half * HALF, (half + 1) * HALF)
            live = live_ref[:, cut] > 0.5 * LOWEST
            total = jnp.where(live, r_ref[0:kept_blocks, half, 0, :], 1.0)
            out_ref[:, cut] = jnp.where(live, m_ref[0:kept_blocks, half, 0, :] + jnp.log2(total), LOWEST)


def half_sweep(sum_couriers, work, rounds, summed, kept, weight, live, name):
    smem = pl.BlockSpec(memory_space=pltpu.SMEM)
    vmem = pl.BlockSpec(memory_space=pltpu.VMEM)
    summed_blocks, kept_blocks = weight.shape[0], live.shape[0]

    def kernel(*refs):
        pass_kernel(sum_couriers, *refs)

    return pl.pallas_call(
        kernel,
        out_shape=jax.ShapeDtypeStruct((kept_blocks, BLOCK), jnp.float32),
        in_specs=[smem, smem] + [vmem] * 4,
        out_specs=vmem,
        scratch_shapes=pass_scratch(kept_blocks),
        compiler_params=pltpu.CompilerParams(vmem_limit_bytes=VMEM_LIMIT),
        cost_estimate=PASS_COST,
        name=name,
    )(work, rounds, summed, kept, weight, live)


PASS_COST = pl.CostEstimate(flops=28 * 2 * 512 * 512 * 128, bytes_accessed=6 << 20, transcendentals=28 * 512 * 512)


def pass_scratch(kept_blocks):
    return [
        pltpu.VMEM((HALF, 128), jnp.bfloat16),
        pltpu.VMEM((kept_blocks + 1, 2, 8, HALF), jnp.float32),
        pltpu.VMEM((kept_blocks + 1, 2, 8, HALF), jnp.float32),
    ]


def first_kernel(work_ref, rounds_ref, zone_ref, *refs):
    parts, (orders_ref, live_ref, out_ref, couriers_ref, log_cap_ref, w_ref, r_ref, m_ref, weight_ref, sem) = (
        refs[:PARTS],
        refs[PARTS:],
    )
    rows = couriers_ref.shape[0] // PARTS
    copies = [
        pltpu.make_async_copy(part, couriers_ref.at[pl.ds(i * rows, rows), :], sem.at[i]) for i, part in enumerate(parts)
    ]
    for copy in copies:
        copy.start()
    for copy in copies:
        copy.wait()
    for zone in range(ZONES):
        row = slot_of(jnp.int32(zone), zone_ref[0]) * COURIER_ROWS + BLOCK
        tail = couriers_ref[pl.ds(pl.multiple_of(row, 16), 16), :].astype(jnp.float32)
        log_cap_ref[zone : zone + 1, :] = jnp.concatenate([tail[i : i + 1] for i in range(4)], axis=1)
    cap = log_cap_ref[...]
    live = cap > 0.0
    log_cap_ref[...] = jnp.where(live, jnp.log2(jnp.where(live, cap, 1.0)), LOWEST)
    weight_ref[...] = jnp.where(live, 0.0, LOWEST)
    pass_kernel(True, work_ref, rounds_ref, couriers_ref, orders_ref, weight_ref, live_ref, out_ref, w_ref, r_ref, m_ref)


def first_half_sweep(work, rounds, zone, parts, orders, live, name):
    smem = pl.BlockSpec(memory_space=pltpu.SMEM)
    vmem = pl.BlockSpec(memory_space=pltpu.VMEM)
    return pl.pallas_call(
        first_kernel,
        out_shape=(
            jax.ShapeDtypeStruct((OB_DEV, BLOCK), jnp.float32),
            jax.ShapeDtypeStruct((ZONES * COURIER_ROWS, EMB), jnp.bfloat16),
            jax.ShapeDtypeStruct((ZONES, BLOCK), jnp.float32),
        ),
        in_specs=[smem] * 3 + [pl.BlockSpec(memory_space=pl.ANY)] * PARTS + [vmem] * 2,
        out_specs=(vmem,) * 3,
        scratch_shapes=pass_scratch(OB_DEV)
        + [pltpu.VMEM((ZONES, BLOCK), jnp.float32), pltpu.SemaphoreType.DMA((PARTS,))],
        compiler_params=pltpu.CompilerParams(vmem_limit_bytes=VMEM_LIMIT),
        cost_estimate=PASS_COST,
        name=name,
    )(work, rounds, zone.reshape(1), *parts, orders, live)


def shards(
    order_features,
    w_in,
    bias_in,
    w_out,
    bias_out,
    courier_embed,
    courier_cap,
    adjacency,
    order_count,
    courier_count,
):
    sub = lax.axis_index("sub")
    positions = jnp.arange(BLOCK, dtype=jnp.int32)

    own_live = positions < courier_count[0]
    tail = jnp.where(own_live, courier_cap, 0).reshape(4, EMB)
    block = jnp.concatenate([courier_embed, jnp.pad(tail, ((0, 12), (0, 0)))], axis=0)
    row = gather_row(block)
    row, bias_in, adjacency, order_count = lax.optimization_barrier((row, bias_in, adjacency, order_count))
    orders = embed_orders(order_features, w_in, bias_in, w_out, bias_out)
    parts, orders = gather_plane(row, orders)

    mine = adjacency % SUBS == sub
    order_live = positions[None, :] < order_count[:, None]
    order_here = jnp.where(order_live & jnp.any(mine, axis=1, keepdims=True), 0.0, LOWEST)

    def order_dual_of(partial):
        return jnp.where(order_live, -join_subs(partial), LOWEST)

    work, rounds = work_list(adjacency, order_count, jnp.ones((ZONES,), jnp.int32), "first_list")
    partial, couriers, log_cap = first_half_sweep(
        work, rounds, lax.axis_index("zone"), parts, orders, order_here, "orders_1"
    )
    courier_live = log_cap > 0.5 * LOWEST
    work, rounds = work_list(adjacency, order_count, courier_live[:, HALF].astype(jnp.int32), "work_list")
    named = jnp.any(
        (adjacency.reshape(-1)[None, :] == jnp.arange(ZONES)[:, None] * SUBS + sub), axis=1, keepdims=True
    )
    courier_here = jnp.where(courier_live & named, 0.0, LOWEST)

    def courier_pass(order_dual, name):
        return half_sweep(False, work, rounds, orders, couriers, order_dual, courier_here, name)

    order_dual = order_dual_of(partial)
    sums = join_zones(courier_pass(order_dual, "couriers_1"))
    courier_dual = jnp.where(courier_live, log_cap - sums, LOWEST)
    order_dual = order_dual_of(half_sweep(True, work, rounds, couriers, orders, courier_dual, order_here, "orders_2"))
    partial = courier_pass(order_dual, "couriers_2")
    parts = lax.all_to_all(partial, "zone", 0, 0, tiled=True)
    highest = jnp.max(parts, axis=0)
    total = highest + jnp.log2(jnp.sum(jnp.exp2(parts - highest[None]), axis=0))
    own_log_cap = jnp.log2(courier_cap.astype(jnp.float32))
    courier_out = jnp.where(own_live, DUAL_SCALE * (own_log_cap - total), 0.0)
    order_out = jnp.where(order_live, DUAL_SCALE * order_dual, 0.0)
    return order_out.reshape(-1), courier_out


def solution(mesh):
    return jax.shard_map(
        shards,
        mesh=mesh,
        in_specs=(
            P("zone", None),
            P(),
            P(),
            P(),
            P(),
            P(("zone", "sub"), None),
            P(("zone", "sub")),
            P("zone", None),
            P("zone"),
            P(("zone", "sub")),
        ),
        out_specs=(P("zone"), P(("zone", "sub"))),
        check_vma=False,
    )
```

```python
import math

import jax
import jax.numpy as jnp
from jax import lax
from jax.experimental import pallas as pl
from jax.experimental.pallas import tpu as pltpu
from jax.sharding import PartitionSpec as P

BLOCK = 512
EMB = 128
HID = 512
ADJ = 8
OB_DEV = 16
ZONES = 32
SUBS = 4
HALF = 256
COURIER_ROWS = BLOCK + 16
UNROLL = 32
REST = 8
MOST_ENTRIES = 256
LIST_SIZE = MOST_ENTRIES + 2 * REST
NO_ORDER = 2 * OB_DEV
NO_COURIER = 2 * ZONES

TEMPER = 0.2
LOWEST = -1e30
SCORE_SCALE = math.log2(math.e) / (TEMPER * math.sqrt(EMB))
DUAL_SCALE = TEMPER * math.log(2.0)

VMEM_LIMIT = 16 * 1024 * 1024


def zone_of(y, x, core):
    return ((y % 4) * 4 + (x % 4)) * 2 + core


PLACES = [(y, x, core) for y in range(4) for x in range(4) for core in range(2)]


def other_core(value):
    return lax.ppermute(value, "zone", [(zone_of(y, x, c), zone_of(y, x, 1 - c)) for y, x, c in PLACES])


def along_z(value, step):
    return lax.ppermute(value, "sub", [(i, (i + step) % SUBS) for i in range(SUBS)])


def plane_step(value, stage, step):
    pairs = []
    for y, x, c in PLACES:
        to = (y, x + step, c) if stage == c else (y + step, x, c)
        pairs.append((zone_of(y, x, c), zone_of(*to)))
    return lax.ppermute(value, "zone", pairs)


def gather_row(block):
    return jnp.concatenate([block] + [plane_step(block, 0, step) for step in (1, 2, 3)], axis=0)


PARTS = 8
EARLY = (0, 2, 3, 4)


def slot_of(zone, me):
    back_x = ((me >> 1) - (zone >> 1)) & 3
    back_y = ((me >> 3) - (zone >> 3)) & 3
    odd = zone & 1
    first = jnp.where(odd == 0, back_x, back_y)
    second = jnp.where(odd == 0, back_y, back_x)
    return ((me ^ zone) & 1) * 16 + second * 4 + first


def early_slot(slot):
    part = slot >> 2
    index = sum(jnp.where(part == p, i, 0) for i, p in enumerate(EARLY))
    is_early = sum(jnp.where(part == p, 1, 0) for p in EARLY)
    return is_early, index * 4 + (slot & 3)


def join(*parts):
    highest = parts[0]
    for part in parts[1:]:
        highest = jnp.maximum(highest, part)
    total = jnp.exp2(parts[0] - highest)
    for part in parts[1:]:
        total = total + jnp.exp2(part - highest)
    return highest + jnp.log2(total)


def join_subs(value):
    return join(value, along_z(value, 1), along_z(value, 2), along_z(value, 3))


def join_zones(value):
    value = join(value, other_core(value))
    for stage in range(2):
        value = join(value, *[plane_step(value, stage, step) for step in (1, 2, 3)])
    return value


EMBED_ROWS = 4096


def embed_kernel(x_hbm, w_in_hbm, b_in_hbm, w_out_hbm, b_out_hbm, o_ref, x_ref, w_in_ref, b_in_ref, w_out_ref, b_out_ref, sem):
    steps = x_ref.shape[0] // EMBED_ROWS

    def rows_copy(i):
        rows = pl.ds(pl.multiple_of(i * EMBED_ROWS, EMBED_ROWS), EMBED_ROWS)
        return pltpu.make_async_copy(x_hbm.at[rows, :], x_ref.at[rows, :], sem.at[i])

    parameters = [
        pltpu.make_async_copy(source, target, sem.at[steps + i])
        for i, (source, target) in enumerate(
            [(w_in_hbm, w_in_ref), (b_in_hbm, b_in_ref), (w_out_hbm, w_out_ref), (b_out_hbm, b_out_ref)]
        )
    ]
    for copy in parameters:
        copy.start()
    for i in range(steps):
        rows_copy(i).start()
    for copy in parameters:
        copy.wait()

    def one_step(i, carry):
        rows_copy(i).wait()
        for start in range(0, EMBED_ROWS, BLOCK):
            rows = pl.ds(pl.multiple_of(i * EMBED_ROWS + start, BLOCK), BLOCK)
            v = jnp.dot(x_ref[rows, :], w_in_ref[...], preferred_element_type=jnp.float32)
            v = 0.5 * (v + b_in_ref[...])
            hidden = (v + v * jnp.tanh(v)).astype(jnp.bfloat16)
            out = jnp.dot(hidden, w_out_ref[...], preferred_element_type=jnp.float32)
            o_ref[rows, :] = ((out + b_out_ref[...]) * SCORE_SCALE).astype(jnp.bfloat16)
        return carry

    lax.fori_loop(0, steps, one_step, 0)


def embed_orders(features, w_in, bias_in, w_out, bias_out):
    rows = features.shape[0]
    operands = (features, w_in, bias_in.reshape(1, HID), w_out, bias_out.reshape(1, EMB))
    return pl.pallas_call(
        embed_kernel,
        out_shape=jax.ShapeDtypeStruct((rows, EMB), jnp.bfloat16),
        in_specs=[pl.BlockSpec(memory_space=pltpu.HBM)] * len(operands),
        out_specs=pl.BlockSpec(memory_space=pltpu.VMEM),
        scratch_shapes=[pltpu.VMEM(value.shape, value.dtype) for value in operands]
        + [pltpu.SemaphoreType.DMA((rows // EMBED_ROWS + 4,))],
        compiler_params=pltpu.CompilerParams(vmem_limit_bytes=VMEM_LIMIT),
        cost_estimate=pl.CostEstimate(
            flops=4 * rows * EMB * HID, bytes_accessed=4 * rows * EMB, transcendentals=rows * HID
        ),
        name="embed_orders",
    )(*[pltpu.with_memory_space_constraint(value, pltpu.HBM) for value in operands])


def list_kernel(pair_ref, two_ref, list_ref, rounds_ref):
    def one_pair(p, n):
        e = pair_ref[p]
        mine = (e >> 24) & 1
        order_two = (e >> 25) & 1
        courier_two = mine * two_ref[(e >> 9) & 31]
        e = e & 0xFFFFFF
        list_ref[n] = e
        n = n + mine
        list_ref[n] = e + 257
        n = n + courier_two
        list_ref[n] = e + 65536
        n = n + order_two
        list_ref[n] = e + 65536 + 257
        return n + (order_two & courier_two)

    n = lax.fori_loop(0, OB_DEV * ADJ, one_pair, jnp.int32(0), unroll=8)
    for i in range(REST):
        list_ref[n + i] = jnp.int32(NO_ORDER * 65536 + NO_COURIER * 256)
    rounds_ref[0] = (n + REST - 1) // REST


def first_list_kernel(pair_ref, early_ref, late_ref, early_rounds_ref, late_rounds_ref, has_ref):
    def one_block(b, counts):
        early_n, late_n = counts
        early_any, late_any = jnp.int32(0), jnp.int32(0)
        for i in range(ADJ):
            e = pair_ref[b * ADJ + i]
            early = (e >> 24) & 1
            late = (e >> 25) & 1
            two = (e >> 26) & 1
            e = e & 0xFFFFFF
            early_any, late_any = early_any | early, late_any | late
            for step, more in ((0, 1), (257, 1), (65536, two), (65536 + 257, two)):
                early_ref[early_n] = e + step
                late_ref[late_n] = e + step
                early_n = early_n + (early & more)
                late_n = late_n + (late & more)
        has_ref[b] = early_any
        has_ref[OB_DEV + b] = late_any
        return early_n, late_n

    counts = lax.fori_loop(0, OB_DEV, one_block, (jnp.int32(0), jnp.int32(0)))
    for n, list_ref, rounds_ref in ((counts[0], early_ref, early_rounds_ref), (counts[1], late_ref, late_rounds_ref)):
        for i in range(REST):
            list_ref[n + i] = jnp.int32(NO_ORDER * 65536 + NO_COURIER * 256)
        rounds_ref[0] = (n + REST - 1) // REST


def call_on_scalars(kernel, sizes, name, *operands):
    smem = pl.BlockSpec(memory_space=pltpu.SMEM)
    return pl.pallas_call(
        kernel,
        out_shape=tuple(jax.ShapeDtypeStruct((size,), jnp.int32) for size in sizes),
        in_specs=[smem] * len(operands),
        out_specs=(smem,) * len(sizes),
        compiler_params=pltpu.CompilerParams(vmem_limit_bytes=1024 * 1024),
        name=name,
    )(*operands)


def pair_fields(adjacency, order_count):
    flat = adjacency.reshape(-1)
    z = flat >> 2
    mine = jnp.where((flat & 3) == lax.axis_index("sub"), 1, 0)
    two = jnp.repeat(jnp.where(order_count > HALF, 1, 0), ADJ)
    block = jnp.arange(OB_DEV * ADJ, dtype=jnp.int32) // ADJ
    slot = slot_of(z, lax.axis_index("zone"))
    return (2 * block << 16) + (2 * z << 8), slot, mine, two


def first_lists(adjacency, order_count):
    entry, slot, mine, two = pair_fields(adjacency, order_count)
    is_early, place = early_slot(slot)
    entry = entry + 2 * jnp.where(is_early == 1, place, slot)
    pairs = entry + ((mine & is_early) << 24) + ((mine & (1 - is_early)) << 25) + (two << 26)
    sizes = (LIST_SIZE, LIST_SIZE, 1, 1, 2 * OB_DEV)
    return call_on_scalars(first_list_kernel, sizes, "first_lists", pairs.astype(jnp.int32))


def work_list(adjacency, order_count, courier_two):
    entry, slot, mine, two = pair_fields(adjacency, order_count)
    pairs = entry + 2 * slot + (mine << 24) + ((mine * two) << 25)
    return call_on_scalars(list_kernel, (LIST_SIZE, 1), "work_list", pairs.astype(jnp.int32), courier_two)


def pass_kernel(sum_couriers, list_ref, rounds_ref, summed_ref, kept_ref, weight_ref, live_ref, out_ref, w_ref, r_ref, m_ref):
    summed_blocks, kept_blocks = weight_ref.shape[0], live_ref.shape[0]
    rounds = rounds_ref[0]
    weight = weight_ref[...]

    high = weight.astype(jnp.bfloat16).astype(jnp.float32)
    low = weight - high
    blank = jnp.zeros((64 - 2 * summed_blocks, 128), jnp.float32)
    for part in range(2):
        rows = []
        for value in (high, low):
            rows += [value[:, part * 128 : part * 128 + 128], value[:, HALF + part * 128 : HALF + part * 128 + 128]]
            if summed_blocks < 32:
                rows.append(blank)
        w_ref[part * 128 : part * 128 + 128, :] = jnp.transpose(jnp.concatenate(rows, axis=0)).astype(jnp.bfloat16)
    r_ref[...] = jnp.zeros(r_ref.shape, jnp.float32)
    lanes = lax.broadcasted_iota(jnp.int32, (1, 128), 1) % 64

    def piece(e):
        order, courier, slot = e >> 16, (e >> 8) & 255, e & 255
        order_row = jnp.minimum(order, 2 * OB_DEV - 1) * HALF
        courier_row = (slot >> 1) * COURIER_ROWS + (slot & 1) * HALF
        return (courier, order, courier_row, order_row) if sum_couriers else (order, courier, order_row, courier_row)

    def sides(s_row, k_row):
        left = summed_ref[pl.ds(pl.multiple_of(s_row, 16), HALF), :]
        right = kept_ref[pl.ds(pl.multiple_of(k_row, 16), HALF), :]
        return left, right

    def scores(left, right):
        return lax.dot_general(left, right, (((1,), (1,)), ((), ())), preferred_element_type=jnp.float32)

    def weighted(s, s_row, k_row):
        left, right = sides(s_row, k_row)
        lane = (s % 2) * summed_blocks + s // 2
        ones = jnp.where(lanes == lane, 1.0, 0.0).astype(jnp.bfloat16)
        left = jnp.concatenate([left, w_ref[...]], axis=1)
        right = jnp.concatenate([right, jnp.broadcast_to(ones, (HALF, 128))], axis=1)
        return scores(left, right)

    def steps(first, count):
        todo = [piece(list_ref[first + t]) for t in range(count)]
        sums = [
            jnp.sum(jnp.exp2(weighted(s, s_row, k_row)).reshape(HALF // 8, 8, HALF), axis=0)
            for s, _, s_row, k_row in todo
        ]
        for (_, k, _, _), part in zip(todo, sums):
            r_ref[k // 2, k % 2] += part

    large = rounds // (UNROLL // REST)

    def large_step(i, carry):
        steps(i * UNROLL, UNROLL)
        return carry

    def small_step(i, carry):
        steps(i * REST, REST)
        return carry

    lax.fori_loop(0, large, large_step, 0)
    lax.fori_loop(large * (UNROLL // REST), rounds, small_step, 0)

    live_weight = jnp.where(weight > 0.5 * LOWEST, jnp.abs(weight), 0.0)
    bad = jnp.where(jnp.max(live_weight) <= 128.0, 0.0, 1.0)
    for half in range(2):
        cut = slice(half * HALF, (half + 1) * HALF)
        total = jnp.sum(r_ref[0:kept_blocks, half], axis=1)
        live = live_ref[:, cut] > 0.5 * LOWEST
        fine = (total >= 2.0**-86) & (total <= 2.0**126)
        bad = bad + jnp.max(jnp.where(live, jnp.where(fine, 0.0, 1.0), 0.0))
        out_ref[:, cut] = jnp.where(live, jnp.log2(jnp.where(live, total, 1.0)), LOWEST)

    @pl.when(bad > 0.0)
    def _():
        m_ref[...] = jnp.full(m_ref.shape, LOWEST, jnp.float32)
        r_ref[...] = jnp.zeros(r_ref.shape, jnp.float32)

        def one_piece(i, carry):
            s, k, s_row, k_row = piece(list_ref[i])
            block = jnp.minimum(s // 2, summed_blocks - 1)
            w = weight_ref[pl.ds(block, 1), pl.ds(pl.multiple_of((s % 2) * HALF, HALF), HALF)]
            column = jnp.transpose(jnp.broadcast_to(w, (128, HALF)))
            x = scores(*sides(s_row, k_row)) + jnp.concatenate([column, column], axis=1)
            before = m_ref[k // 2, k % 2, 0:1]
            after = jnp.maximum(before, jnp.max(x, axis=0, keepdims=True))
            scaled = r_ref[k // 2, k % 2, 0:1] * jnp.exp2(before - after)
            m_ref[k // 2, k % 2, 0:1] = after
            r_ref[k // 2, k % 2, 0:1] = scaled + jnp.sum(jnp.exp2(x - after), axis=0, keepdims=True)
            return carry

        lax.fori_loop(0, rounds * REST, one_piece, 0)
        for half in range(2):
            cut = slice(half * HALF, (half + 1) * HALF)
            live = live_ref[:, cut] > 0.5 * LOWEST
            total = jnp.where(live, r_ref[0:kept_blocks, half, 0, :], 1.0)
            out_ref[:, cut] = jnp.where(live, m_ref[0:kept_blocks, half, 0, :] + jnp.log2(total), LOWEST)


def half_sweep(sum_couriers, work, rounds, summed, kept, weight, live, name):
    smem = pl.BlockSpec(memory_space=pltpu.SMEM)
    vmem = pl.BlockSpec(memory_space=pltpu.VMEM)
    summed_blocks, kept_blocks = weight.shape[0], live.shape[0]

    def kernel(*refs):
        pass_kernel(sum_couriers, *refs)

    return pl.pallas_call(
        kernel,
        out_shape=jax.ShapeDtypeStruct((kept_blocks, BLOCK), jnp.float32),
        in_specs=[smem, smem] + [vmem] * 4,
        out_specs=vmem,
        scratch_shapes=pass_scratch(kept_blocks),
        compiler_params=pltpu.CompilerParams(vmem_limit_bytes=VMEM_LIMIT),
        cost_estimate=PASS_COST,
        name=name,
    )(work, rounds, summed, kept, weight, live)


PASS_COST = pl.CostEstimate(flops=28 * 2 * 512 * 512 * 128, bytes_accessed=6 << 20, transcendentals=28 * 512 * 512)


def pass_scratch(kept_blocks):
    return [
        pltpu.VMEM((HALF, 128), jnp.bfloat16),
        pltpu.VMEM((kept_blocks + 1, 2, 8, HALF), jnp.float32),
        pltpu.VMEM((kept_blocks + 1, 2, 8, HALF), jnp.float32),
    ]


def first_kernel(early, work_ref, rounds_ref, zone_ref, has_ref, *refs):
    count = len(EARLY) if early else PARTS
    parts, (orders_ref, live_ref, out_ref, couriers_ref, log_cap_ref, w_ref, r_ref, m_ref, weight_ref, here_ref, sem) = (
        refs[:count],
        refs[count:],
    )
    rows = couriers_ref.shape[0] // count
    copies = [
        pltpu.make_async_copy(part, couriers_ref.at[pl.ds(i * rows, rows), :], sem.at[i]) for i, part in enumerate(parts)
    ]
    for copy in copies:
        copy.start()
    for block in range(OB_DEV):
        named = has_ref[block if early else OB_DEV + block] > 0
        here_ref[block : block + 1, :] = jnp.where(named, live_ref[block : block + 1, :], LOWEST)
    for copy in copies:
        copy.wait()
    for zone in range(ZONES):
        slot = slot_of(jnp.int32(zone), zone_ref[0])
        if early:
            _, slot = early_slot(slot)
        row = slot * COURIER_ROWS + BLOCK
        tail = couriers_ref[pl.ds(pl.multiple_of(row, 16), 16), :].astype(jnp.float32)
        log_cap_ref[zone : zone + 1, :] = jnp.concatenate([tail[i : i + 1] for i in range(4)], axis=1)
    cap = log_cap_ref[...]
    live = cap > 0.0
    log_cap_ref[...] = jnp.where(live, jnp.log2(jnp.where(live, cap, 1.0)), LOWEST)
    weight_ref[...] = jnp.where(live, 0.0, LOWEST)
    pass_kernel(True, work_ref, rounds_ref, couriers_ref, orders_ref, weight_ref, here_ref, out_ref, w_ref, r_ref, m_ref)


def first_half_sweep(early, work, rounds, zone, has, parts, orders, live, name):
    smem = pl.BlockSpec(memory_space=pltpu.SMEM)
    vmem = pl.BlockSpec(memory_space=pltpu.VMEM)

    def kernel(*refs):
        first_kernel(early, *refs)

    couriers = (len(parts) * 4 * COURIER_ROWS, EMB)
    kept_out = () if early else (
        jax.ShapeDtypeStruct(couriers, jnp.bfloat16),
        jax.ShapeDtypeStruct((ZONES, BLOCK), jnp.float32),
    )
    as_scratch = [pltpu.VMEM(couriers, jnp.bfloat16), pltpu.VMEM((ZONES, BLOCK), jnp.float32)] if early else []
    return pl.pallas_call(
        kernel,
        out_shape=(jax.ShapeDtypeStruct((OB_DEV, BLOCK), jnp.float32),) + kept_out,
        in_specs=[smem] * 4 + [pl.BlockSpec(memory_space=pl.ANY)] * len(parts) + [vmem] * 2,
        out_specs=(vmem,) * (1 + len(kept_out)),
        scratch_shapes=as_scratch
        + pass_scratch(OB_DEV)
        + [
            pltpu.VMEM((ZONES, BLOCK), jnp.float32),
            pltpu.VMEM((OB_DEV, BLOCK), jnp.float32),
            pltpu.SemaphoreType.DMA((len(parts),)),
        ],
        compiler_params=pltpu.CompilerParams(vmem_limit_bytes=VMEM_LIMIT),
        cost_estimate=pl.CostEstimate(flops=14 * 2 * 512 * 512 * 128, bytes_accessed=6 << 20, transcendentals=14 * 512 * 512),
        name=name,
    )(work, rounds, zone.reshape(1), has, *parts, orders, live)


def shards(
    order_features,
    w_in,
    bias_in,
    w_out,
    bias_out,
    courier_embed,
    courier_cap,
    adjacency,
    order_count,
    courier_count,
):
    sub = lax.axis_index("sub")
    positions = jnp.arange(BLOCK, dtype=jnp.int32)

    own_live = positions < courier_count[0]
    tail = jnp.where(own_live, courier_cap, 0).reshape(4, EMB)
    block = jnp.concatenate([courier_embed, jnp.pad(tail, ((0, 12), (0, 0)))], axis=0)
    row = gather_row(block)
    row, bias_in, adjacency, order_count = lax.optimization_barrier((row, bias_in, adjacency, order_count))
    orders = embed_orders(order_features, w_in, bias_in, w_out, bias_out)
    order_live = positions[None, :] < order_count[:, None]
    live = jnp.where(order_live, 0.0, LOWEST)
    early_list, late_list, early_rounds, late_rounds, has = first_lists(adjacency, order_count)
    zone = lax.axis_index("zone")

    own = [row] + [plane_step(row, 1, step) for step in (1, 2, 3)]
    other = [other_core(row)] + [None] * 3
    for step in (3, 2):
        own[step], orders = lax.optimization_barrier((own[step], orders))
        other[step] = other_core(own[step])
    parts = own + other
    (early_partial,) = first_half_sweep(
        True, early_list, early_rounds, zone, has, [parts[p] for p in EARLY], orders, live, "orders_1_early"
    )
    own[1], early_partial = lax.optimization_barrier((own[1], early_partial))
    other[1] = other_core(own[1])
    late_partial, couriers, log_cap = first_half_sweep(
        False, late_list, late_rounds, zone, has, own + other, orders, live, "orders_1"
    )
    partial = join(early_partial, late_partial)

    mine = adjacency % SUBS == sub
    order_here = jnp.where(order_live & jnp.any(mine, axis=1, keepdims=True), 0.0, LOWEST)

    def order_dual_of(partial):
        return jnp.where(order_live, -join_subs(partial), LOWEST)

    courier_live = log_cap > 0.5 * LOWEST
    work, rounds = work_list(adjacency, order_count, courier_live[:, HALF].astype(jnp.int32))
    named = jnp.any(
        (adjacency.reshape(-1)[None, :] == jnp.arange(ZONES)[:, None] * SUBS + sub), axis=1, keepdims=True
    )
    courier_here = jnp.where(courier_live & named, 0.0, LOWEST)

    def courier_pass(order_dual, name):
        return half_sweep(False, work, rounds, orders, couriers, order_dual, courier_here, name)

    order_dual = order_dual_of(partial)
    sums = join_zones(courier_pass(order_dual, "couriers_1"))
    courier_dual = jnp.where(courier_live, log_cap - sums, LOWEST)
    order_dual = order_dual_of(half_sweep(True, work, rounds, couriers, orders, courier_dual, order_here, "orders_2"))
    partial = courier_pass(order_dual, "couriers_2")
    parts = lax.all_to_all(partial, "zone", 0, 0, tiled=True)
    highest = jnp.max(parts, axis=0)
    total = highest + jnp.log2(jnp.sum(jnp.exp2(parts - highest[None]), axis=0))
    own_log_cap = jnp.log2(courier_cap.astype(jnp.float32))
    courier_out = jnp.where(own_live, DUAL_SCALE * (own_log_cap - total), 0.0)
    order_out = jnp.where(order_live, DUAL_SCALE * order_dual, 0.0)
    return order_out.reshape(-1), courier_out


def solution(mesh):
    return jax.shard_map(
        shards,
        mesh=mesh,
        in_specs=(
            P("zone", None),
            P(),
            P(),
            P(),
            P(),
            P(("zone", "sub"), None),
            P(("zone", "sub")),
            P("zone", None),
            P("zone"),
            P(("zone", "sub")),
        ),
        out_specs=(P("zone"), P(("zone", "sub"))),
        check_vma=False,
    )
```

```python
import math

import jax
import jax.numpy as jnp
from jax import lax
from jax.experimental import pallas as pl
from jax.experimental.pallas import tpu as pltpu
from jax.sharding import PartitionSpec as P

BLOCK = 512
EMB = 128
HID = 512
ADJ = 8
OB_DEV = 16
ZONES = 32
SUBS = 4
HALF = 256
COURIER_ROWS = BLOCK + 16
UNROLL = 32
REST = 8
MOST_ENTRIES = 256
LIST_SIZE = MOST_ENTRIES + 2 * REST
NO_ORDER = 2 * OB_DEV
NO_COURIER = 2 * ZONES

TEMPER = 0.2
LOWEST = -1e30
SCORE_SCALE = math.log2(math.e) / (TEMPER * math.sqrt(EMB))
DUAL_SCALE = TEMPER * math.log(2.0)

VMEM_LIMIT = 16 * 1024 * 1024
PARTS = 8


def zone_of(y, x, core):
    return ((y % 4) * 4 + (x % 4)) * 2 + core


PLACES = [(y, x, core) for y in range(4) for x in range(4) for core in range(2)]


def other_core(value):
    return lax.ppermute(value, "zone", [(zone_of(y, x, c), zone_of(y, x, 1 - c)) for y, x, c in PLACES])


def along_z(value, step):
    return lax.ppermute(value, "sub", [(i, (i + step) % SUBS) for i in range(SUBS)])


def plane_step(value, stage, step):
    pairs = []
    for y, x, c in PLACES:
        to = (y, x + step, c) if stage == c else (y + step, x, c)
        pairs.append((zone_of(y, x, c), zone_of(*to)))
    return lax.ppermute(value, "zone", pairs)


def pack_kernel(count_ref, embed_ref, cap_ref, block_ref, row_ref, sem):
    copy = pltpu.make_async_copy(embed_ref, block_ref.at[pl.ds(0, BLOCK), :], sem.at[0])
    copy_row = pltpu.make_async_copy(embed_ref, row_ref.at[pl.ds(0, BLOCK), :], sem.at[1])
    copy.start()
    copy_row.start()
    lane = lax.broadcasted_iota(jnp.int32, (1, BLOCK), 1)
    cap = jnp.where(lane < count_ref[0], cap_ref[...].astype(jnp.float32), 0.0)
    rows = [cap[:, i * EMB : (i + 1) * EMB] for i in range(4)]
    tail = jnp.concatenate(rows + [jnp.zeros((12, EMB), jnp.float32)], axis=0).astype(jnp.bfloat16)
    block_ref[pl.ds(BLOCK, 16), :] = tail
    row_ref[pl.ds(BLOCK, 16), :] = tail
    copy.wait()
    copy_row.wait()


def pack(count, embed, cap):
    vmem = pl.BlockSpec(memory_space=pltpu.VMEM)
    return pl.pallas_call(
        pack_kernel,
        out_shape=(
            jax.ShapeDtypeStruct((COURIER_ROWS, EMB), jnp.bfloat16),
            jax.ShapeDtypeStruct((4 * COURIER_ROWS, EMB), jnp.bfloat16),
        ),
        in_specs=[pl.BlockSpec(memory_space=pltpu.SMEM), pl.BlockSpec(memory_space=pltpu.HBM), vmem],
        out_specs=(vmem, vmem),
        scratch_shapes=[pltpu.SemaphoreType.DMA((2,))],
        compiler_params=pltpu.CompilerParams(vmem_limit_bytes=4 * 1024 * 1024),
        name="pack",
    )(count, pltpu.with_memory_space_constraint(embed, pltpu.HBM), cap.reshape(1, BLOCK))


def gather_row(block, row):
    for step in (1, 2, 3):
        row = lax.dynamic_update_slice(row, plane_step(block, 0, step), (step * COURIER_ROWS, 0))
    return row


def gather_plane(row, meanwhile):
    own = [row] + [plane_step(row, 1, step) for step in (1, 2, 3)]
    swapped = [other_core(row)]
    own[1], own[2], own[3], meanwhile = lax.optimization_barrier((own[1], own[2], own[3], meanwhile))
    return own + swapped + [other_core(part) for part in own[1:]], meanwhile


def slot_of(zone, me):
    back_x = ((me >> 1) - (zone >> 1)) & 3
    back_y = ((me >> 3) - (zone >> 3)) & 3
    odd = zone & 1
    first = jnp.where(odd == 0, back_x, back_y)
    second = jnp.where(odd == 0, back_y, back_x)
    return ((me ^ zone) & 1) * 16 + second * 4 + first


def join(*parts):
    highest = parts[0]
    for part in parts[1:]:
        highest = jnp.maximum(highest, part)
    total = jnp.exp2(parts[0] - highest)
    for part in parts[1:]:
        total = total + jnp.exp2(part - highest)
    return highest + jnp.log2(total)


def join_subs(value):
    return join(value, along_z(value, 1), along_z(value, 2), along_z(value, 3))


def join_zones(value):
    value = join(value, other_core(value))
    for stage in range(2):
        value = join(value, *[plane_step(value, stage, step) for step in (1, 2, 3)])
    return value


EMBED_ROWS = 4096


def embed_kernel(x_hbm, w_in_hbm, b_in_hbm, w_out_hbm, b_out_hbm, o_ref, x_ref, w_in_ref, b_in_ref, w_out_ref, b_out_ref, sem):
    steps = x_ref.shape[0] // EMBED_ROWS

    def rows_copy(i):
        rows = pl.ds(pl.multiple_of(i * EMBED_ROWS, EMBED_ROWS), EMBED_ROWS)
        return pltpu.make_async_copy(x_hbm.at[rows, :], x_ref.at[rows, :], sem.at[i])

    parameters = [
        pltpu.make_async_copy(source, target, sem.at[steps + i])
        for i, (source, target) in enumerate(
            [(w_in_hbm, w_in_ref), (b_in_hbm, b_in_ref), (w_out_hbm, w_out_ref), (b_out_hbm, b_out_ref)]
        )
    ]
    for copy in parameters:
        copy.start()
    for i in range(steps):
        rows_copy(i).start()
    for copy in parameters:
        copy.wait()

    def one_step(i, carry):
        rows_copy(i).wait()
        for start in range(0, EMBED_ROWS, BLOCK):
            rows = pl.ds(pl.multiple_of(i * EMBED_ROWS + start, BLOCK), BLOCK)
            v = jnp.dot(x_ref[rows, :], w_in_ref[...], preferred_element_type=jnp.float32)
            v = 0.5 * (v + b_in_ref[...])
            hidden = (v + v * jnp.tanh(v)).astype(jnp.bfloat16)
            out = jnp.dot(hidden, w_out_ref[...], preferred_element_type=jnp.float32)
            o_ref[rows, :] = ((out + b_out_ref[...]) * SCORE_SCALE).astype(jnp.bfloat16)
        return carry

    lax.fori_loop(0, steps, one_step, 0)


def embed_orders(features, w_in, bias_in, w_out, bias_out):
    rows = features.shape[0]
    operands = (features, w_in, bias_in.reshape(1, HID), w_out, bias_out.reshape(1, EMB))
    return pl.pallas_call(
        embed_kernel,
        out_shape=jax.ShapeDtypeStruct((rows, EMB), jnp.bfloat16),
        in_specs=[pl.BlockSpec(memory_space=pltpu.HBM)] * len(operands),
        out_specs=pl.BlockSpec(memory_space=pltpu.VMEM),
        scratch_shapes=[pltpu.VMEM(value.shape, value.dtype) for value in operands]
        + [pltpu.SemaphoreType.DMA((rows // EMBED_ROWS + 4,))],
        compiler_params=pltpu.CompilerParams(vmem_limit_bytes=VMEM_LIMIT),
        cost_estimate=pl.CostEstimate(
            flops=4 * rows * EMB * HID, bytes_accessed=4 * rows * EMB, transcendentals=rows * HID
        ),
        name="embed_orders",
    )(*[pltpu.with_memory_space_constraint(value, pltpu.HBM) for value in operands])


def list_kernel(pair_ref, two_ref, list_ref, rounds_ref):
    def one_pair(p, n):
        e = pair_ref[p]
        mine = (e >> 24) & 1
        order_two = (e >> 25) & 1
        courier_two = mine * two_ref[(e >> 9) & 31]
        e = e & 0xFFFFFF
        list_ref[n] = e
        n = n + mine
        list_ref[n] = e + 257
        n = n + courier_two
        list_ref[n] = e + 65536
        n = n + order_two
        list_ref[n] = e + 65536 + 257
        return n + (order_two & courier_two)

    n = lax.fori_loop(0, OB_DEV * ADJ, one_pair, jnp.int32(0), unroll=8)
    for i in range(REST):
        list_ref[n + i] = jnp.int32(NO_ORDER * 65536 + NO_COURIER * 256)
    rounds_ref[0] = (n + REST - 1) // REST


def work_list(adjacency, order_count, courier_two, name):
    zone, sub = lax.axis_index("zone"), lax.axis_index("sub")
    flat = adjacency.reshape(-1)
    z = flat >> 2
    mine = jnp.where((flat & 3) == sub, 1, 0)
    two = jnp.repeat(jnp.where(order_count > HALF, 1, 0), ADJ)
    block = jnp.arange(OB_DEV * ADJ, dtype=jnp.int32) // ADJ
    entry = (2 * block << 16) + (2 * z << 8) + 2 * slot_of(z, zone)
    pairs = entry + (mine << 24) + ((mine * two) << 25)
    smem = pl.BlockSpec(memory_space=pltpu.SMEM)
    return pl.pallas_call(
        list_kernel,
        out_shape=(
            jax.ShapeDtypeStruct((LIST_SIZE,), jnp.int32),
            jax.ShapeDtypeStruct((1,), jnp.int32),
        ),
        in_specs=[smem] * 2,
        out_specs=(smem, smem),
        compiler_params=pltpu.CompilerParams(vmem_limit_bytes=1024 * 1024),
        name=name,
    )(pairs.astype(jnp.int32), courier_two)


def pass_kernel(sum_couriers, list_ref, rounds_ref, summed_ref, kept_ref, weight_ref, live_ref, out_ref, w_ref, r_ref, m_ref):
    summed_blocks, kept_blocks = weight_ref.shape[0], live_ref.shape[0]
    rounds = rounds_ref[0]
    weight = weight_ref[...]

    def put(cut, value):
        if len(out_ref.shape) == 3:
            out_ref[:, 0, cut] = value
        else:
            out_ref[:, cut] = value

    high = weight.astype(jnp.bfloat16).astype(jnp.float32)
    low = weight - high
    blank = jnp.zeros((64 - 2 * summed_blocks, 128), jnp.float32)
    for part in range(2):
        rows = []
        for value in (high, low):
            rows += [value[:, part * 128 : part * 128 + 128], value[:, HALF + part * 128 : HALF + part * 128 + 128]]
            if summed_blocks < 32:
                rows.append(blank)
        w_ref[part * 128 : part * 128 + 128, :] = jnp.transpose(jnp.concatenate(rows, axis=0)).astype(jnp.bfloat16)
    r_ref[...] = jnp.zeros(r_ref.shape, jnp.float32)
    lanes = lax.broadcasted_iota(jnp.int32, (1, 128), 1) % 64

    def piece(e):
        order, courier, slot = e >> 16, (e >> 8) & 255, e & 255
        order_row = jnp.minimum(order, 2 * OB_DEV - 1) * HALF
        courier_row = (slot >> 1) * COURIER_ROWS + (slot & 1) * HALF
        return (courier, order, courier_row, order_row) if sum_couriers else (order, courier, order_row, courier_row)

    def sides(s_row, k_row):
        left = summed_ref[pl.ds(pl.multiple_of(s_row, 16), HALF), :]
        right = kept_ref[pl.ds(pl.multiple_of(k_row, 16), HALF), :]
        return left, right

    def scores(left, right):
        return lax.dot_general(left, right, (((1,), (1,)), ((), ())), preferred_element_type=jnp.float32)

    def weighted(s, s_row, k_row):
        left, right = sides(s_row, k_row)
        lane = (s % 2) * summed_blocks + s // 2
        ones = jnp.where(lanes == lane, 1.0, 0.0).astype(jnp.bfloat16)
        left = jnp.concatenate([left, w_ref[...]], axis=1)
        right = jnp.concatenate([right, jnp.broadcast_to(ones, (HALF, 128))], axis=1)
        return scores(left, right)

    def steps(first, count):
        todo = [piece(list_ref[first + t]) for t in range(count)]
        sums = [
            jnp.sum(jnp.exp2(weighted(s, s_row, k_row)).reshape(HALF // 8, 8, HALF), axis=0)
            for s, _, s_row, k_row in todo
        ]
        for (_, k, _, _), part in zip(todo, sums):
            r_ref[k // 2, k % 2] += part

    large_steps = rounds // (UNROLL // REST)

    def large_step(i, carry):
        steps(i * UNROLL, UNROLL)
        return carry

    def small_step(i, carry):
        steps(i * REST, REST)
        return carry

    lax.fori_loop(0, large_steps, large_step, 0)
    lax.fori_loop(large_steps * (UNROLL // REST), rounds, small_step, 0)

    large = jnp.where((weight > 0.5 * LOWEST) & ~(jnp.abs(weight) <= 128.0), 1.0, 0.0)
    bad = jnp.max(large, axis=0, keepdims=True)
    bad = jnp.maximum(bad[:, 0:HALF], bad[:, HALF:])
    for half in range(2):
        cut = slice(half * HALF, (half + 1) * HALF)
        total = jnp.sum(r_ref[0:kept_blocks, half], axis=1)
        live = live_ref[:, cut] > 0.5 * LOWEST
        fine = (total >= 2.0**-86) & (total <= 2.0**126)
        off = jnp.where(live & ~fine, 1.0, 0.0)
        bad = jnp.maximum(bad, jnp.max(off, axis=0, keepdims=True))
        put(cut, jnp.where(live, jnp.log2(jnp.where(live, total, 1.0)), LOWEST))
    bad = jnp.max(bad)

    @pl.when(bad > 0.0)
    def _():
        m_ref[...] = jnp.full(m_ref.shape, LOWEST, jnp.float32)
        r_ref[...] = jnp.zeros(r_ref.shape, jnp.float32)

        def one_piece(i, carry):
            s, k, s_row, k_row = piece(list_ref[i])
            block = jnp.minimum(s // 2, summed_blocks - 1)
            w = weight_ref[pl.ds(block, 1), pl.ds(pl.multiple_of((s % 2) * HALF, HALF), HALF)]
            column = jnp.transpose(jnp.broadcast_to(w, (128, HALF)))
            x = scores(*sides(s_row, k_row)) + jnp.concatenate([column, column], axis=1)
            before = m_ref[k // 2, k % 2, 0:1]
            after = jnp.maximum(before, jnp.max(x, axis=0, keepdims=True))
            scaled = r_ref[k // 2, k % 2, 0:1] * jnp.exp2(before - after)
            m_ref[k // 2, k % 2, 0:1] = after
            r_ref[k // 2, k % 2, 0:1] = scaled + jnp.sum(jnp.exp2(x - after), axis=0, keepdims=True)
            return carry

        lax.fori_loop(0, rounds * REST, one_piece, 0)
        for half in range(2):
            cut = slice(half * HALF, (half + 1) * HALF)
            live = live_ref[:, cut] > 0.5 * LOWEST
            total = jnp.where(live, r_ref[0:kept_blocks, half, 0, :], 1.0)
            put(cut, jnp.where(live, m_ref[0:kept_blocks, half, 0, :] + jnp.log2(total), LOWEST))


def half_sweep(sum_couriers, work, rounds, summed, kept, weight, live, name, apart=False):
    smem = pl.BlockSpec(memory_space=pltpu.SMEM)
    vmem = pl.BlockSpec(memory_space=pltpu.VMEM)
    summed_blocks, kept_blocks = weight.shape[0], live.shape[0]

    def kernel(*refs):
        pass_kernel(sum_couriers, *refs)

    return pl.pallas_call(
        kernel,
        out_shape=jax.ShapeDtypeStruct((kept_blocks, 1, BLOCK) if apart else (kept_blocks, BLOCK), jnp.float32),
        in_specs=[smem, smem] + [vmem] * 4,
        out_specs=vmem,
        scratch_shapes=pass_scratch(kept_blocks),
        compiler_params=pltpu.CompilerParams(vmem_limit_bytes=VMEM_LIMIT),
        cost_estimate=PASS_COST,
        name=name,
    )(work, rounds, summed, kept, weight, live)


PASS_COST = pl.CostEstimate(flops=28 * 2 * 512 * 512 * 128, bytes_accessed=6 << 20, transcendentals=28 * 512 * 512)


def pass_scratch(kept_blocks):
    return [
        pltpu.VMEM((HALF, 128), jnp.bfloat16),
        pltpu.VMEM((kept_blocks + 1, 2, 8, HALF), jnp.float32),
        pltpu.VMEM((kept_blocks + 1, 2, 8, HALF), jnp.float32),
    ]


def first_kernel(work_ref, rounds_ref, zone_ref, *refs):
    parts, (orders_ref, live_ref, out_ref, couriers_ref, log_cap_ref, w_ref, r_ref, m_ref, weight_ref, sem) = (
        refs[:PARTS],
        refs[PARTS:],
    )
    rows = couriers_ref.shape[0] // PARTS
    copies = [
        pltpu.make_async_copy(part, couriers_ref.at[pl.ds(i * rows, rows), :], sem.at[i]) for i, part in enumerate(parts)
    ]
    for copy in copies:
        copy.start()
    for copy in copies:
        copy.wait()
    for zone in range(ZONES):
        row = slot_of(jnp.int32(zone), zone_ref[0]) * COURIER_ROWS + BLOCK
        tail = couriers_ref[pl.ds(pl.multiple_of(row, 16), 16), :].astype(jnp.float32)
        log_cap_ref[zone : zone + 1, :] = jnp.concatenate([tail[i : i + 1] for i in range(4)], axis=1)
    cap = log_cap_ref[...]
    live = cap > 0.0
    log_cap_ref[...] = jnp.where(live, jnp.log2(jnp.where(live, cap, 1.0)), LOWEST)
    weight_ref[...] = jnp.where(live, 0.0, LOWEST)
    pass_kernel(True, work_ref, rounds_ref, couriers_ref, orders_ref, weight_ref, live_ref, out_ref, w_ref, r_ref, m_ref)


def first_half_sweep(work, rounds, zone, parts, orders, live, name):
    smem = pl.BlockSpec(memory_space=pltpu.SMEM)
    vmem = pl.BlockSpec(memory_space=pltpu.VMEM)
    return pl.pallas_call(
        first_kernel,
        out_shape=(
            jax.ShapeDtypeStruct((OB_DEV, BLOCK), jnp.float32),
            jax.ShapeDtypeStruct((ZONES * COURIER_ROWS, EMB), jnp.bfloat16),
            jax.ShapeDtypeStruct((ZONES, BLOCK), jnp.float32),
        ),
        in_specs=[smem] * 3 + [pl.BlockSpec(memory_space=pl.ANY)] * PARTS + [vmem] * 2,
        out_specs=(vmem,) * 3,
        scratch_shapes=pass_scratch(OB_DEV)
        + [pltpu.VMEM((ZONES, BLOCK), jnp.float32), pltpu.SemaphoreType.DMA((PARTS,))],
        compiler_params=pltpu.CompilerParams(vmem_limit_bytes=VMEM_LIMIT),
        cost_estimate=PASS_COST,
        name=name,
    )(work, rounds, zone.reshape(1), *parts, orders, live)


def shards(
    order_features,
    w_in,
    bias_in,
    w_out,
    bias_out,
    courier_embed,
    courier_cap,
    adjacency,
    order_count,
    courier_count,
):
    sub = lax.axis_index("sub")
    positions = jnp.arange(BLOCK, dtype=jnp.int32)

    own_live = positions < courier_count[0]
    row = gather_row(*pack(courier_count, courier_embed, courier_cap))
    row, bias_in, adjacency, order_count = lax.optimization_barrier((row, bias_in, adjacency, order_count))
    orders = embed_orders(order_features, w_in, bias_in, w_out, bias_out)

    parts, orders = gather_plane(row, orders)

    mine = adjacency % SUBS == sub
    order_live = positions[None, :] < order_count[:, None]
    order_here = jnp.where(order_live & jnp.any(mine, axis=1, keepdims=True), 0.0, LOWEST)

    def order_dual_of(partial):
        return jnp.where(order_live, -join_subs(partial), LOWEST)

    work, rounds = work_list(adjacency, order_count, jnp.ones((ZONES,), jnp.int32), "first_list")
    partial, couriers, log_cap = first_half_sweep(
        work, rounds, lax.axis_index("zone"), parts, orders, order_here, "orders_1"
    )
    courier_live = log_cap > 0.5 * LOWEST
    work, rounds = work_list(adjacency, order_count, courier_live[:, HALF].astype(jnp.int32), "work_list")
    named = jnp.any(
        (adjacency.reshape(-1)[None, :] == jnp.arange(ZONES)[:, None] * SUBS + sub), axis=1, keepdims=True
    )
    courier_here = jnp.where(courier_live & named, 0.0, LOWEST)

    def courier_pass(order_dual, name, apart=False):
        return half_sweep(False, work, rounds, orders, couriers, order_dual, courier_here, name, apart)

    order_dual = order_dual_of(partial)
    sums = join_zones(courier_pass(order_dual, "couriers_1"))
    courier_dual = jnp.where(courier_live, log_cap - sums, LOWEST)
    order_dual = order_dual_of(half_sweep(True, work, rounds, couriers, orders, courier_dual, order_here, "orders_2"))
    partial = courier_pass(order_dual, "couriers_2", apart=True)
    parts = lax.all_to_all(partial, "zone", 0, 0, tiled=True)[:, 0]
    highest = jnp.max(parts, axis=0)
    total = highest + jnp.log2(jnp.sum(jnp.exp2(parts - highest[None]), axis=0))
    own_log_cap = jnp.log2(courier_cap.astype(jnp.float32))
    courier_out = jnp.where(own_live, DUAL_SCALE * (own_log_cap - total), 0.0)
    order_out = jnp.where(order_live, DUAL_SCALE * order_dual, 0.0)
    return order_out.reshape(-1), courier_out


def solution(mesh):
    return jax.shard_map(
        shards,
        mesh=mesh,
        in_specs=(
            P("zone", None),
            P(),
            P(),
            P(),
            P(),
            P(("zone", "sub"), None),
            P(("zone", "sub")),
            P("zone", None),
            P("zone"),
            P(("zone", "sub")),
        ),
        out_specs=(P("zone"), P(("zone", "sub"))),
        check_vma=False,
    )
```

```python
import math

import jax
import jax.numpy as jnp
from jax import lax
from jax.experimental import pallas as pl
from jax.experimental.pallas import tpu as pltpu
from jax.sharding import PartitionSpec as P

BLOCK = 512
EMB = 128
HID = 512
ADJ = 8
OB_DEV = 16
ZONES = 32
SUBS = 4
HALF = 256
COURIER_ROWS = BLOCK + 16
UNROLL = 32
REST = 8
MOST_ENTRIES = 256
LIST_SIZE = MOST_ENTRIES + 2 * REST
NO_ORDER = 2 * OB_DEV
NO_COURIER = 2 * ZONES

TEMPER = 0.2
LOWEST = -1e30
SCORE_SCALE = math.log2(math.e) / (TEMPER * math.sqrt(EMB))
DUAL_SCALE = TEMPER * math.log(2.0)

VMEM_LIMIT = 16 * 1024 * 1024


def zone_of(y, x, core):
    return ((y % 4) * 4 + (x % 4)) * 2 + core


PLACES = [(y, x, core) for y in range(4) for x in range(4) for core in range(2)]


def other_core(value):
    return lax.ppermute(value, "zone", [(zone_of(y, x, c), zone_of(y, x, 1 - c)) for y, x, c in PLACES])


def along_z(value, step):
    return lax.ppermute(value, "sub", [(i, (i + step) % SUBS) for i in range(SUBS)])


def plane_step(value, stage, step):
    pairs = []
    for y, x, c in PLACES:
        to = (y, x + step, c) if stage == c else (y + step, x, c)
        pairs.append((zone_of(y, x, c), zone_of(*to)))
    return lax.ppermute(value, "zone", pairs)


def pack_kernel(count_ref, embed_ref, cap_ref, block_ref, row_ref, sem):
    copy = pltpu.make_async_copy(embed_ref, block_ref.at[pl.ds(0, BLOCK), :], sem.at[0])
    copy_row = pltpu.make_async_copy(embed_ref, row_ref.at[pl.ds(0, BLOCK), :], sem.at[1])
    copy.start()
    copy_row.start()
    lane = lax.broadcasted_iota(jnp.int32, (1, BLOCK), 1)
    cap = jnp.where(lane < count_ref[0], cap_ref[...].astype(jnp.float32), 0.0)
    rows = [cap[:, i * EMB : (i + 1) * EMB] for i in range(4)]
    tail = jnp.concatenate(rows + [jnp.zeros((12, EMB), jnp.float32)], axis=0).astype(jnp.bfloat16)
    block_ref[pl.ds(BLOCK, 16), :] = tail
    row_ref[pl.ds(BLOCK, 16), :] = tail
    copy.wait()
    copy_row.wait()


def pack(count, embed, cap):
    vmem = pl.BlockSpec(memory_space=pltpu.VMEM)
    return pl.pallas_call(
        pack_kernel,
        out_shape=(
            jax.ShapeDtypeStruct((COURIER_ROWS, EMB), jnp.bfloat16),
            jax.ShapeDtypeStruct((4 * COURIER_ROWS, EMB), jnp.bfloat16),
        ),
        in_specs=[pl.BlockSpec(memory_space=pltpu.SMEM), pl.BlockSpec(memory_space=pltpu.HBM), vmem],
        out_specs=(vmem, vmem),
        scratch_shapes=[pltpu.SemaphoreType.DMA((2,))],
        compiler_params=pltpu.CompilerParams(vmem_limit_bytes=4 * 1024 * 1024),
        name="pack",
    )(count, pltpu.with_memory_space_constraint(embed, pltpu.HBM), cap.reshape(1, BLOCK))


def gather_row(block, row):
    for step in (1, 2, 3):
        row = lax.dynamic_update_slice(row, plane_step(block, 0, step), (step * COURIER_ROWS, 0))
    return row


PARTS = 8
EARLY = (0, 4)


def slot_of(zone, me):
    back_x = ((me >> 1) - (zone >> 1)) & 3
    back_y = ((me >> 3) - (zone >> 3)) & 3
    odd = zone & 1
    first = jnp.where(odd == 0, back_x, back_y)
    second = jnp.where(odd == 0, back_y, back_x)
    return ((me ^ zone) & 1) * 16 + second * 4 + first


def early_slot(slot):
    part = slot >> 2
    index = sum(jnp.where(part == p, i, 0) for i, p in enumerate(EARLY))
    is_early = sum(jnp.where(part == p, 1, 0) for p in EARLY)
    return is_early, index * 4 + (slot & 3)


def join(*parts):
    highest = parts[0]
    for part in parts[1:]:
        highest = jnp.maximum(highest, part)
    total = jnp.exp2(parts[0] - highest)
    for part in parts[1:]:
        total = total + jnp.exp2(part - highest)
    return highest + jnp.log2(total)


def join_subs(value):
    return join(value, along_z(value, 1), along_z(value, 2), along_z(value, 3))


def join_zones(value):
    value = join(value, other_core(value))
    for stage in range(2):
        value = join(value, *[plane_step(value, stage, step) for step in (1, 2, 3)])
    return value


EMBED_ROWS = 4096


def embed_kernel(x_hbm, w_in_hbm, b_in_hbm, w_out_hbm, b_out_hbm, o_ref, x_ref, w_in_ref, b_in_ref, w_out_ref, b_out_ref, sem):
    steps = x_ref.shape[0] // EMBED_ROWS

    def rows_copy(i):
        rows = pl.ds(pl.multiple_of(i * EMBED_ROWS, EMBED_ROWS), EMBED_ROWS)
        return pltpu.make_async_copy(x_hbm.at[rows, :], x_ref.at[rows, :], sem.at[i])

    parameters = [
        pltpu.make_async_copy(source, target, sem.at[steps + i])
        for i, (source, target) in enumerate(
            [(w_in_hbm, w_in_ref), (b_in_hbm, b_in_ref), (w_out_hbm, w_out_ref), (b_out_hbm, b_out_ref)]
        )
    ]
    for copy in parameters:
        copy.start()
    for i in range(steps):
        rows_copy(i).start()
    for copy in parameters:
        copy.wait()

    def one_step(i, carry):
        rows_copy(i).wait()
        for start in range(0, EMBED_ROWS, BLOCK):
            rows = pl.ds(pl.multiple_of(i * EMBED_ROWS + start, BLOCK), BLOCK)
            v = jnp.dot(x_ref[rows, :], w_in_ref[...], preferred_element_type=jnp.float32)
            v = 0.5 * (v + b_in_ref[...])
            hidden = (v + v * jnp.tanh(v)).astype(jnp.bfloat16)
            out = jnp.dot(hidden, w_out_ref[...], preferred_element_type=jnp.float32)
            o_ref[rows, :] = ((out + b_out_ref[...]) * SCORE_SCALE).astype(jnp.bfloat16)
        return carry

    lax.fori_loop(0, steps, one_step, 0)


def embed_orders(features, w_in, bias_in, w_out, bias_out):
    rows = features.shape[0]
    operands = (features, w_in, bias_in.reshape(1, HID), w_out, bias_out.reshape(1, EMB))
    return pl.pallas_call(
        embed_kernel,
        out_shape=jax.ShapeDtypeStruct((rows, EMB), jnp.bfloat16),
        in_specs=[pl.BlockSpec(memory_space=pltpu.HBM)] * len(operands),
        out_specs=pl.BlockSpec(memory_space=pltpu.VMEM),
        scratch_shapes=[pltpu.VMEM(value.shape, value.dtype) for value in operands]
        + [pltpu.SemaphoreType.DMA((rows // EMBED_ROWS + 4,))],
        compiler_params=pltpu.CompilerParams(vmem_limit_bytes=VMEM_LIMIT),
        cost_estimate=pl.CostEstimate(
            flops=4 * rows * EMB * HID, bytes_accessed=4 * rows * EMB, transcendentals=rows * HID
        ),
        name="embed_orders",
    )(*[pltpu.with_memory_space_constraint(value, pltpu.HBM) for value in operands])


def list_kernel(pair_ref, two_ref, list_ref, rounds_ref):
    def one_pair(p, n):
        e = pair_ref[p]
        mine = (e >> 24) & 1
        order_two = (e >> 25) & 1
        courier_two = mine * two_ref[(e >> 9) & 31]
        e = e & 0xFFFFFF
        list_ref[n] = e
        n = n + mine
        list_ref[n] = e + 257
        n = n + courier_two
        list_ref[n] = e + 65536
        n = n + order_two
        list_ref[n] = e + 65536 + 257
        return n + (order_two & courier_two)

    n = lax.fori_loop(0, OB_DEV * ADJ, one_pair, jnp.int32(0), unroll=8)
    for i in range(REST):
        list_ref[n + i] = jnp.int32(NO_ORDER * 65536 + NO_COURIER * 256)
    rounds_ref[0] = (n + REST - 1) // REST


def first_list_kernel(pair_ref, early_ref, late_ref, early_rounds_ref, late_rounds_ref, has_ref):
    def one_block(b, counts):
        early_n, late_n = counts
        early_any, late_any = jnp.int32(0), jnp.int32(0)
        for i in range(ADJ):
            e = pair_ref[b * ADJ + i]
            early = (e >> 24) & 1
            late = (e >> 25) & 1
            two = (e >> 26) & 1
            e = e & 0xFFFFFF
            early_any, late_any = early_any | early, late_any | late
            for step, more in ((0, 1), (257, 1), (65536, two), (65536 + 257, two)):
                early_ref[early_n] = e + step
                late_ref[late_n] = e + step
                early_n = early_n + (early & more)
                late_n = late_n + (late & more)
        has_ref[b] = early_any
        has_ref[OB_DEV + b] = late_any
        return early_n, late_n

    counts = lax.fori_loop(0, OB_DEV, one_block, (jnp.int32(0), jnp.int32(0)))
    for n, list_ref, rounds_ref in ((counts[0], early_ref, early_rounds_ref), (counts[1], late_ref, late_rounds_ref)):
        for i in range(REST):
            list_ref[n + i] = jnp.int32(NO_ORDER * 65536 + NO_COURIER * 256)
        rounds_ref[0] = (n + REST - 1) // REST


def call_on_scalars(kernel, sizes, name, *operands):
    smem = pl.BlockSpec(memory_space=pltpu.SMEM)
    return pl.pallas_call(
        kernel,
        out_shape=tuple(jax.ShapeDtypeStruct((size,), jnp.int32) for size in sizes),
        in_specs=[smem] * len(operands),
        out_specs=(smem,) * len(sizes),
        compiler_params=pltpu.CompilerParams(vmem_limit_bytes=1024 * 1024),
        name=name,
    )(*operands)


def pair_fields(adjacency, order_count):
    flat = adjacency.reshape(-1)
    z = flat >> 2
    mine = jnp.where((flat & 3) == lax.axis_index("sub"), 1, 0)
    two = jnp.repeat(jnp.where(order_count > HALF, 1, 0), ADJ)
    block = jnp.arange(OB_DEV * ADJ, dtype=jnp.int32) // ADJ
    slot = slot_of(z, lax.axis_index("zone"))
    return (2 * block << 16) + (2 * z << 8), slot, mine, two


def first_lists(adjacency, order_count):
    entry, slot, mine, two = pair_fields(adjacency, order_count)
    is_early, place = early_slot(slot)
    entry = entry + 2 * jnp.where(is_early == 1, place, slot)
    pairs = entry + ((mine & is_early) << 24) + ((mine & (1 - is_early)) << 25) + (two << 26)
    sizes = (LIST_SIZE, LIST_SIZE, 1, 1, 2 * OB_DEV)
    return call_on_scalars(first_list_kernel, sizes, "first_lists", pairs.astype(jnp.int32))


def work_list(adjacency, order_count, courier_two):
    entry, slot, mine, two = pair_fields(adjacency, order_count)
    pairs = entry + 2 * slot + (mine << 24) + ((mine * two) << 25)
    return call_on_scalars(list_kernel, (LIST_SIZE, 1), "work_list", pairs.astype(jnp.int32), courier_two)


def pass_kernel(sum_couriers, list_ref, rounds_ref, summed_ref, kept_ref, weight_ref, live_ref, out_ref, w_ref, r_ref, m_ref):
    summed_blocks, kept_blocks = weight_ref.shape[0], live_ref.shape[0]
    rounds = rounds_ref[0]
    weight = weight_ref[...]

    high = weight.astype(jnp.bfloat16).astype(jnp.float32)
    low = weight - high
    blank = jnp.zeros((64 - 2 * summed_blocks, 128), jnp.float32)
    for part in range(2):
        rows = []
        for value in (high, low):
            rows += [value[:, part * 128 : part * 128 + 128], value[:, HALF + part * 128 : HALF + part * 128 + 128]]
            if summed_blocks < 32:
                rows.append(blank)
        w_ref[part * 128 : part * 128 + 128, :] = jnp.transpose(jnp.concatenate(rows, axis=0)).astype(jnp.bfloat16)
    r_ref[...] = jnp.zeros(r_ref.shape, jnp.float32)
    lanes = lax.broadcasted_iota(jnp.int32, (1, 128), 1) % 64

    def piece(e):
        order, courier, slot = e >> 16, (e >> 8) & 255, e & 255
        order_row = jnp.minimum(order, 2 * OB_DEV - 1) * HALF
        courier_row = (slot >> 1) * COURIER_ROWS + (slot & 1) * HALF
        return (courier, order, courier_row, order_row) if sum_couriers else (order, courier, order_row, courier_row)

    def sides(s_row, k_row):
        left = summed_ref[pl.ds(pl.multiple_of(s_row, 16), HALF), :]
        right = kept_ref[pl.ds(pl.multiple_of(k_row, 16), HALF), :]
        return left, right

    def scores(left, right):
        return lax.dot_general(left, right, (((1,), (1,)), ((), ())), preferred_element_type=jnp.float32)

    def weighted(s, s_row, k_row):
        left, right = sides(s_row, k_row)
        lane = (s % 2) * summed_blocks + s // 2
        ones = jnp.where(lanes == lane, 1.0, 0.0).astype(jnp.bfloat16)
        left = jnp.concatenate([left, w_ref[...]], axis=1)
        right = jnp.concatenate([right, jnp.broadcast_to(ones, (HALF, 128))], axis=1)
        return scores(left, right)

    def steps(first, count):
        todo = [piece(list_ref[first + t]) for t in range(count)]
        sums = [
            jnp.sum(jnp.exp2(weighted(s, s_row, k_row)).reshape(HALF // 8, 8, HALF), axis=0)
            for s, _, s_row, k_row in todo
        ]
        for (_, k, _, _), part in zip(todo, sums):
            r_ref[k // 2, k % 2] += part

    large_steps = rounds // (UNROLL // REST)

    def large_step(i, carry):
        steps(i * UNROLL, UNROLL)
        return carry

    def small_step(i, carry):
        steps(i * REST, REST)
        return carry

    lax.fori_loop(0, large_steps, large_step, 0)
    lax.fori_loop(large_steps * (UNROLL // REST), rounds, small_step, 0)

    large = jnp.where((weight > 0.5 * LOWEST) & ~(jnp.abs(weight) <= 128.0), 1.0, 0.0)
    bad = jnp.max(large, axis=0, keepdims=True)
    bad = jnp.maximum(bad[:, 0:HALF], bad[:, HALF:])
    for half in range(2):
        cut = slice(half * HALF, (half + 1) * HALF)
        total = jnp.sum(r_ref[0:kept_blocks, half], axis=1)
        live = live_ref[:, cut] > 0.5 * LOWEST
        fine = (total >= 2.0**-86) & (total <= 2.0**126)
        off = jnp.where(live & ~fine, 1.0, 0.0)
        bad = jnp.maximum(bad, jnp.max(off, axis=0, keepdims=True))
        out_ref[:, cut] = jnp.where(live, jnp.log2(jnp.where(live, total, 1.0)), LOWEST)
    bad = jnp.max(bad)

    @pl.when(bad > 0.0)
    def _():
        m_ref[...] = jnp.full(m_ref.shape, LOWEST, jnp.float32)
        r_ref[...] = jnp.zeros(r_ref.shape, jnp.float32)

        def one_piece(i, carry):
            s, k, s_row, k_row = piece(list_ref[i])
            block = jnp.minimum(s // 2, summed_blocks - 1)
            w = weight_ref[pl.ds(block, 1), pl.ds(pl.multiple_of((s % 2) * HALF, HALF), HALF)]
            column = jnp.transpose(jnp.broadcast_to(w, (128, HALF)))
            x = scores(*sides(s_row, k_row)) + jnp.concatenate([column, column], axis=1)
            before = m_ref[k // 2, k % 2, 0:1]
            after = jnp.maximum(before, jnp.max(x, axis=0, keepdims=True))
            scaled = r_ref[k // 2, k % 2, 0:1] * jnp.exp2(before - after)
            m_ref[k // 2, k % 2, 0:1] = after
            r_ref[k // 2, k % 2, 0:1] = scaled + jnp.sum(jnp.exp2(x - after), axis=0, keepdims=True)
            return carry

        lax.fori_loop(0, rounds * REST, one_piece, 0)
        for half in range(2):
            cut = slice(half * HALF, (half + 1) * HALF)
            live = live_ref[:, cut] > 0.5 * LOWEST
            total = jnp.where(live, r_ref[0:kept_blocks, half, 0, :], 1.0)
            out_ref[:, cut] = jnp.where(live, m_ref[0:kept_blocks, half, 0, :] + jnp.log2(total), LOWEST)


def half_sweep(sum_couriers, work, rounds, summed, kept, weight, live, name):
    smem = pl.BlockSpec(memory_space=pltpu.SMEM)
    vmem = pl.BlockSpec(memory_space=pltpu.VMEM)
    summed_blocks, kept_blocks = weight.shape[0], live.shape[0]

    def kernel(*refs):
        pass_kernel(sum_couriers, *refs)

    return pl.pallas_call(
        kernel,
        out_shape=jax.ShapeDtypeStruct((kept_blocks, BLOCK), jnp.float32),
        in_specs=[smem, smem] + [vmem] * 4,
        out_specs=vmem,
        scratch_shapes=pass_scratch(kept_blocks),
        compiler_params=pltpu.CompilerParams(vmem_limit_bytes=VMEM_LIMIT),
        cost_estimate=PASS_COST,
        name=name,
    )(work, rounds, summed, kept, weight, live)


PASS_COST = pl.CostEstimate(flops=28 * 2 * 512 * 512 * 128, bytes_accessed=6 << 20, transcendentals=28 * 512 * 512)


def pass_scratch(kept_blocks):
    return [
        pltpu.VMEM((HALF, 128), jnp.bfloat16),
        pltpu.VMEM((kept_blocks + 1, 2, 8, HALF), jnp.float32),
        pltpu.VMEM((kept_blocks + 1, 2, 8, HALF), jnp.float32),
    ]


def first_kernel(early, work_ref, rounds_ref, zone_ref, has_ref, *refs):
    count = len(EARLY) if early else PARTS
    parts, (orders_ref, live_ref, out_ref, couriers_ref, log_cap_ref, w_ref, r_ref, m_ref, weight_ref, here_ref, sem) = (
        refs[:count],
        refs[count:],
    )
    rows = couriers_ref.shape[0] // count
    copies = [
        pltpu.make_async_copy(part, couriers_ref.at[pl.ds(i * rows, rows), :], sem.at[i]) for i, part in enumerate(parts)
    ]
    for copy in copies:
        copy.start()
    for block in range(OB_DEV):
        named = has_ref[block if early else OB_DEV + block] > 0
        here_ref[block : block + 1, :] = jnp.where(named, live_ref[block : block + 1, :], LOWEST)
    for copy in copies:
        copy.wait()
    for zone in range(ZONES):
        slot = slot_of(jnp.int32(zone), zone_ref[0])
        if early:
            _, slot = early_slot(slot)
        row = slot * COURIER_ROWS + BLOCK
        tail = couriers_ref[pl.ds(pl.multiple_of(row, 16), 16), :].astype(jnp.float32)
        log_cap_ref[zone : zone + 1, :] = jnp.concatenate([tail[i : i + 1] for i in range(4)], axis=1)
    cap = log_cap_ref[...]
    live = cap > 0.0
    log_cap_ref[...] = jnp.where(live, jnp.log2(jnp.where(live, cap, 1.0)), LOWEST)
    weight_ref[...] = jnp.where(live, 0.0, LOWEST)
    pass_kernel(True, work_ref, rounds_ref, couriers_ref, orders_ref, weight_ref, here_ref, out_ref, w_ref, r_ref, m_ref)


def first_half_sweep(early, work, rounds, zone, has, parts, orders, live, name):
    smem = pl.BlockSpec(memory_space=pltpu.SMEM)
    vmem = pl.BlockSpec(memory_space=pltpu.VMEM)

    def kernel(*refs):
        first_kernel(early, *refs)

    couriers = (len(parts) * 4 * COURIER_ROWS, EMB)
    kept_out = () if early else (
        jax.ShapeDtypeStruct(couriers, jnp.bfloat16),
        jax.ShapeDtypeStruct((ZONES, BLOCK), jnp.float32),
    )
    as_scratch = [pltpu.VMEM(couriers, jnp.bfloat16), pltpu.VMEM((ZONES, BLOCK), jnp.float32)] if early else []
    return pl.pallas_call(
        kernel,
        out_shape=(jax.ShapeDtypeStruct((OB_DEV, BLOCK), jnp.float32),) + kept_out,
        in_specs=[smem] * 4 + [pl.BlockSpec(memory_space=pl.ANY)] * len(parts) + [vmem] * 2,
        out_specs=(vmem,) * (1 + len(kept_out)),
        scratch_shapes=as_scratch
        + pass_scratch(OB_DEV)
        + [
            pltpu.VMEM((ZONES, BLOCK), jnp.float32),
            pltpu.VMEM((OB_DEV, BLOCK), jnp.float32),
            pltpu.SemaphoreType.DMA((len(parts),)),
        ],
        compiler_params=pltpu.CompilerParams(vmem_limit_bytes=VMEM_LIMIT),
        cost_estimate=pl.CostEstimate(flops=14 * 2 * 512 * 512 * 128, bytes_accessed=6 << 20, transcendentals=14 * 512 * 512),
        name=name,
    )(work, rounds, zone.reshape(1), has, *parts, orders, live)


def shards(
    order_features,
    w_in,
    bias_in,
    w_out,
    bias_out,
    courier_embed,
    courier_cap,
    adjacency,
    order_count,
    courier_count,
):
    sub = lax.axis_index("sub")
    positions = jnp.arange(BLOCK, dtype=jnp.int32)

    own_live = positions < courier_count[0]
    row = gather_row(*pack(courier_count, courier_embed, courier_cap))
    row, bias_in, adjacency, order_count = lax.optimization_barrier((row, bias_in, adjacency, order_count))
    orders = embed_orders(order_features, w_in, bias_in, w_out, bias_out)
    order_live = positions[None, :] < order_count[:, None]
    live = jnp.where(order_live, 0.0, LOWEST)
    early_list, late_list, early_rounds, late_rounds, has = first_lists(adjacency, order_count)
    zone = lax.axis_index("zone")

    own = [row] + [plane_step(row, 1, step) for step in (1, 2, 3)]
    other = [other_core(row)] + [None] * 3
    parts = own + other
    (early_partial,) = first_half_sweep(
        True, early_list, early_rounds, zone, has, [parts[p] for p in EARLY], orders, live, "orders_1_early"
    )
    own[1], own[2], own[3], early_partial = lax.optimization_barrier((own[1], own[2], own[3], early_partial))
    for step in (1, 2, 3):
        other[step] = other_core(own[step])
    late_partial, couriers, log_cap = first_half_sweep(
        False, late_list, late_rounds, zone, has, own + other, orders, live, "orders_1"
    )
    partial = join(early_partial, late_partial)

    mine = adjacency % SUBS == sub
    order_here = jnp.where(order_live & jnp.any(mine, axis=1, keepdims=True), 0.0, LOWEST)

    def order_dual_of(partial):
        return jnp.where(order_live, -join_subs(partial), LOWEST)

    courier_live = log_cap > 0.5 * LOWEST
    work, rounds = work_list(adjacency, order_count, courier_live[:, HALF].astype(jnp.int32))
    named = jnp.any(
        (adjacency.reshape(-1)[None, :] == jnp.arange(ZONES)[:, None] * SUBS + sub), axis=1, keepdims=True
    )
    courier_here = jnp.where(courier_live & named, 0.0, LOWEST)

    def courier_pass(order_dual, name):
        return half_sweep(False, work, rounds, orders, couriers, order_dual, courier_here, name)

    order_dual = order_dual_of(partial)
    sums = join_zones(courier_pass(order_dual, "couriers_1"))
    courier_dual = jnp.where(courier_live, log_cap - sums, LOWEST)
    order_dual = order_dual_of(half_sweep(True, work, rounds, couriers, orders, courier_dual, order_here, "orders_2"))
    partial = courier_pass(order_dual, "couriers_2")
    parts = lax.all_to_all(partial, "zone", 0, 0, tiled=True)
    highest = jnp.max(parts, axis=0)
    total = highest + jnp.log2(jnp.sum(jnp.exp2(parts - highest[None]), axis=0))
    own_log_cap = jnp.log2(courier_cap.astype(jnp.float32))
    courier_out = jnp.where(own_live, DUAL_SCALE * (own_log_cap - total), 0.0)
    order_out = jnp.where(order_live, DUAL_SCALE * order_dual, 0.0)
    return order_out.reshape(-1), courier_out


def solution(mesh):
    return jax.shard_map(
        shards,
        mesh=mesh,
        in_specs=(
            P("zone", None),
            P(),
            P(),
            P(),
            P(),
            P(("zone", "sub"), None),
            P(("zone", "sub")),
            P("zone", None),
            P("zone"),
            P(("zone", "sub")),
        ),
        out_specs=(P("zone"), P(("zone", "sub"))),
        check_vma=False,
    )
```

```python
import math

import jax
import jax.numpy as jnp
from jax import lax
from jax.experimental import pallas as pl
from jax.experimental.pallas import tpu as pltpu
from jax.sharding import PartitionSpec as P

BLOCK = 512
EMB = 128
HID = 512
ADJ = 8
OB_DEV = 16
ZONES = 32
SUBS = 4
HALF = 256
COURIER_ROWS = BLOCK + 16
UNROLL = 32
REST = 8
MOST_ENTRIES = 256
LIST_SIZE = MOST_ENTRIES + 2 * REST
NO_ORDER = 2 * OB_DEV
NO_COURIER = 2 * ZONES

TEMPER = 0.2
LOWEST = -1e30
SCORE_SCALE = math.log2(math.e) / (TEMPER * math.sqrt(EMB))
DUAL_SCALE = TEMPER * math.log(2.0)

VMEM_LIMIT = 16 * 1024 * 1024


def zone_of(y, x, core):
    return ((y % 4) * 4 + (x % 4)) * 2 + core


PLACES = [(y, x, core) for y in range(4) for x in range(4) for core in range(2)]


def other_core(value):
    return lax.ppermute(value, "zone", [(zone_of(y, x, c), zone_of(y, x, 1 - c)) for y, x, c in PLACES])


def along_z(value, step):
    return lax.ppermute(value, "sub", [(i, (i + step) % SUBS) for i in range(SUBS)])


def plane_step(value, stage, step):
    pairs = []
    for y, x, c in PLACES:
        to = (y, x + step, c) if stage == c else (y + step, x, c)
        pairs.append((zone_of(y, x, c), zone_of(*to)))
    return lax.ppermute(value, "zone", pairs)


def pack_kernel(count_ref, embed_ref, cap_hbm, block_ref, row_ref, cap_ref, sem):
    copy = pltpu.make_async_copy(embed_ref, block_ref.at[pl.ds(0, BLOCK), :], sem.at[0])
    copy_row = pltpu.make_async_copy(embed_ref, row_ref.at[pl.ds(0, BLOCK), :], sem.at[1])
    copy.start()
    copy_row.start()
    copy_cap = pltpu.make_async_copy(cap_hbm, cap_ref, sem.at[2])
    copy_cap.start()
    copy_cap.wait()
    lane = lax.broadcasted_iota(jnp.int32, (1, BLOCK), 1)
    cap = jnp.where(lane < count_ref[0], cap_ref[...].astype(jnp.float32).reshape(1, BLOCK), 0.0)
    rows = [cap[:, i * EMB : (i + 1) * EMB] for i in range(4)]
    tail = jnp.concatenate(rows + [jnp.zeros((12, EMB), jnp.float32)], axis=0).astype(jnp.bfloat16)
    block_ref[pl.ds(BLOCK, 16), :] = tail
    row_ref[pl.ds(BLOCK, 16), :] = tail
    copy.wait()
    copy_row.wait()


def pack(count, embed, cap):
    vmem = pl.BlockSpec(memory_space=pltpu.VMEM)
    return pl.pallas_call(
        pack_kernel,
        out_shape=(
            jax.ShapeDtypeStruct((COURIER_ROWS, EMB), jnp.bfloat16),
            jax.ShapeDtypeStruct((4 * COURIER_ROWS, EMB), jnp.bfloat16),
        ),
        in_specs=[pl.BlockSpec(memory_space=pltpu.SMEM)] + [pl.BlockSpec(memory_space=pltpu.HBM)] * 2,
        out_specs=(vmem, vmem),
        scratch_shapes=[pltpu.VMEM((BLOCK,), cap.dtype), pltpu.SemaphoreType.DMA((3,))],
        compiler_params=pltpu.CompilerParams(vmem_limit_bytes=4 * 1024 * 1024),
        name="pack",
    )(count, *[pltpu.with_memory_space_constraint(value, pltpu.HBM) for value in (embed, cap)])


def gather_row(block, row):
    for step in (1, 2, 3):
        row = lax.dynamic_update_slice(row, plane_step(block, 0, step), (step * COURIER_ROWS, 0))
    return row


PARTS = 8
EARLY = (0, 4)


def slot_of(zone, me):
    back_x = ((me >> 1) - (zone >> 1)) & 3
    back_y = ((me >> 3) - (zone >> 3)) & 3
    odd = zone & 1
    first = jnp.where(odd == 0, back_x, back_y)
    second = jnp.where(odd == 0, back_y, back_x)
    return ((me ^ zone) & 1) * 16 + second * 4 + first


def early_slot(slot):
    part = slot >> 2
    index = sum(jnp.where(part == p, i, 0) for i, p in enumerate(EARLY))
    is_early = sum(jnp.where(part == p, 1, 0) for p in EARLY)
    return is_early, index * 4 + (slot & 3)


def join(*parts):
    highest = parts[0]
    for part in parts[1:]:
        highest = jnp.maximum(highest, part)
    total = jnp.exp2(parts[0] - highest)
    for part in parts[1:]:
        total = total + jnp.exp2(part - highest)
    return highest + jnp.log2(total)


def join_subs(value):
    return join(value, along_z(value, 1), along_z(value, 2), along_z(value, 3))


def join_zones(value):
    value = join(value, other_core(value))
    for stage in range(2):
        value = join(value, *[plane_step(value, stage, step) for step in (1, 2, 3)])
    return value


EMBED_ROWS = 4096


def embed_kernel(x_hbm, w_in_hbm, b_in_hbm, w_out_hbm, b_out_hbm, o_ref, x_ref, w_in_ref, b_in_ref, w_out_ref, b_out_ref, sem):
    steps = x_ref.shape[0] // EMBED_ROWS

    def rows_copy(i):
        rows = pl.ds(pl.multiple_of(i * EMBED_ROWS, EMBED_ROWS), EMBED_ROWS)
        return pltpu.make_async_copy(x_hbm.at[rows, :], x_ref.at[rows, :], sem.at[i])

    parameters = [
        pltpu.make_async_copy(source, target, sem.at[steps + i])
        for i, (source, target) in enumerate(
            [(w_in_hbm, w_in_ref), (b_in_hbm, b_in_ref), (w_out_hbm, w_out_ref), (b_out_hbm, b_out_ref)]
        )
    ]
    for copy in parameters:
        copy.start()
    for i in range(steps):
        rows_copy(i).start()
    for copy in parameters:
        copy.wait()

    def one_step(i, carry):
        rows_copy(i).wait()
        for start in range(0, EMBED_ROWS, BLOCK):
            rows = pl.ds(pl.multiple_of(i * EMBED_ROWS + start, BLOCK), BLOCK)
            v = jnp.dot(x_ref[rows, :], w_in_ref[...], preferred_element_type=jnp.float32)
            v = 0.5 * (v + b_in_ref[...])
            hidden = (v + v * jnp.tanh(v)).astype(jnp.bfloat16)
            out = jnp.dot(hidden, w_out_ref[...], preferred_element_type=jnp.float32)
            o_ref[rows, :] = ((out + b_out_ref[...]) * SCORE_SCALE).astype(jnp.bfloat16)
        return carry

    lax.fori_loop(0, steps, one_step, 0)


def embed_orders(features, w_in, bias_in, w_out, bias_out):
    rows = features.shape[0]
    operands = (features, w_in, bias_in.reshape(1, HID), w_out, bias_out.reshape(1, EMB))
    return pl.pallas_call(
        embed_kernel,
        out_shape=jax.ShapeDtypeStruct((rows, EMB), jnp.bfloat16),
        in_specs=[pl.BlockSpec(memory_space=pltpu.HBM)] * len(operands),
        out_specs=pl.BlockSpec(memory_space=pltpu.VMEM),
        scratch_shapes=[pltpu.VMEM(value.shape, value.dtype) for value in operands]
        + [pltpu.SemaphoreType.DMA((rows // EMBED_ROWS + 4,))],
        compiler_params=pltpu.CompilerParams(vmem_limit_bytes=VMEM_LIMIT),
        cost_estimate=pl.CostEstimate(
            flops=4 * rows * EMB * HID, bytes_accessed=4 * rows * EMB, transcendentals=rows * HID
        ),
        name="embed_orders",
    )(*[pltpu.with_memory_space_constraint(value, pltpu.HBM) for value in operands])


def list_kernel(pair_ref, two_ref, list_ref, rounds_ref):
    def one_pair(p, n):
        e = pair_ref[p]
        mine = (e >> 24) & 1
        order_two = (e >> 25) & 1
        courier_two = mine * two_ref[(e >> 9) & 31]
        e = e & 0xFFFFFF
        list_ref[n] = e
        n = n + mine
        list_ref[n] = e + 257
        n = n + courier_two
        list_ref[n] = e + 65536
        n = n + order_two
        list_ref[n] = e + 65536 + 257
        return n + (order_two & courier_two)

    n = lax.fori_loop(0, OB_DEV * ADJ, one_pair, jnp.int32(0), unroll=8)
    for i in range(REST):
        list_ref[n + i] = jnp.int32(NO_ORDER * 65536 + NO_COURIER * 256)
    rounds_ref[0] = (n + REST - 1) // REST


def first_list_kernel(pair_ref, early_ref, late_ref, early_rounds_ref, late_rounds_ref, has_ref):
    def one_block(b, counts):
        early_n, late_n = counts
        early_any, late_any = jnp.int32(0), jnp.int32(0)
        for i in range(ADJ):
            e = pair_ref[b * ADJ + i]
            early = (e >> 24) & 1
            late = (e >> 25) & 1
            two = (e >> 26) & 1
            e = e & 0xFFFFFF
            early_any, late_any = early_any | early, late_any | late
            for step, more in ((0, 1), (257, 1), (65536, two), (65536 + 257, two)):
                early_ref[early_n] = e + step
                late_ref[late_n] = e + step
                early_n = early_n + (early & more)
                late_n = late_n + (late & more)
        has_ref[b] = early_any
        has_ref[OB_DEV + b] = late_any
        return early_n, late_n

    counts = lax.fori_loop(0, OB_DEV, one_block, (jnp.int32(0), jnp.int32(0)))
    for n, list_ref, rounds_ref in ((counts[0], early_ref, early_rounds_ref), (counts[1], late_ref, late_rounds_ref)):
        for i in range(REST):
            list_ref[n + i] = jnp.int32(NO_ORDER * 65536 + NO_COURIER * 256)
        rounds_ref[0] = (n + REST - 1) // REST


def call_on_scalars(kernel, sizes, name, *operands):
    smem = pl.BlockSpec(memory_space=pltpu.SMEM)
    return pl.pallas_call(
        kernel,
        out_shape=tuple(jax.ShapeDtypeStruct((size,), jnp.int32) for size in sizes),
        in_specs=[smem] * len(operands),
        out_specs=(smem,) * len(sizes),
        compiler_params=pltpu.CompilerParams(vmem_limit_bytes=1024 * 1024),
        name=name,
    )(*operands)


def pair_fields(adjacency, order_count):
    flat = adjacency.reshape(-1)
    z = flat >> 2
    mine = jnp.where((flat & 3) == lax.axis_index("sub"), 1, 0)
    two = jnp.repeat(jnp.where(order_count > HALF, 1, 0), ADJ)
    block = jnp.arange(OB_DEV * ADJ, dtype=jnp.int32) // ADJ
    slot = slot_of(z, lax.axis_index("zone"))
    return (2 * block << 16) + (2 * z << 8), slot, mine, two


def first_lists(adjacency, order_count):
    entry, slot, mine, two = pair_fields(adjacency, order_count)
    is_early, place = early_slot(slot)
    entry = entry + 2 * jnp.where(is_early == 1, place, slot)
    pairs = entry + ((mine & is_early) << 24) + ((mine & (1 - is_early)) << 25) + (two << 26)
    sizes = (LIST_SIZE, LIST_SIZE, 1, 1, 2 * OB_DEV)
    return call_on_scalars(first_list_kernel, sizes, "first_lists", pairs.astype(jnp.int32))


def work_list(adjacency, order_count, courier_two):
    entry, slot, mine, two = pair_fields(adjacency, order_count)
    pairs = entry + 2 * slot + (mine << 24) + ((mine * two) << 25)
    return call_on_scalars(list_kernel, (LIST_SIZE, 1), "work_list", pairs.astype(jnp.int32), courier_two)


def pass_kernel(sum_couriers, list_ref, rounds_ref, summed_ref, kept_ref, weight_ref, live_ref, out_ref, w_ref, r_ref, m_ref):
    summed_blocks, kept_blocks = weight_ref.shape[0], live_ref.shape[0]
    rounds = rounds_ref[0]
    weight = weight_ref[...]

    high = weight.astype(jnp.bfloat16).astype(jnp.float32)
    low = weight - high
    blank = jnp.zeros((64 - 2 * summed_blocks, 128), jnp.float32)
    for part in range(2):
        rows = []
        for value in (high, low):
            rows += [value[:, part * 128 : part * 128 + 128], value[:, HALF + part * 128 : HALF + part * 128 + 128]]
            if summed_blocks < 32:
                rows.append(blank)
        w_ref[part * 128 : part * 128 + 128, :] = jnp.transpose(jnp.concatenate(rows, axis=0)).astype(jnp.bfloat16)
    r_ref[...] = jnp.zeros(r_ref.shape, jnp.float32)
    lanes = lax.broadcasted_iota(jnp.int32, (1, 128), 1) % 64

    def piece(e):
        order, courier, slot = e >> 16, (e >> 8) & 255, e & 255
        order_row = jnp.minimum(order, 2 * OB_DEV - 1) * HALF
        courier_row = (slot >> 1) * COURIER_ROWS + (slot & 1) * HALF
        return (courier, order, courier_row, order_row) if sum_couriers else (order, courier, order_row, courier_row)

    def sides(s_row, k_row):
        left = summed_ref[pl.ds(pl.multiple_of(s_row, 16), HALF), :]
        right = kept_ref[pl.ds(pl.multiple_of(k_row, 16), HALF), :]
        return left, right

    def scores(left, right):
        return lax.dot_general(left, right, (((1,), (1,)), ((), ())), preferred_element_type=jnp.float32)

    def weighted(s, s_row, k_row):
        left, right = sides(s_row, k_row)
        lane = (s % 2) * summed_blocks + s // 2
        ones = jnp.where(lanes == lane, 1.0, 0.0).astype(jnp.bfloat16)
        left = jnp.concatenate([left, w_ref[...]], axis=1)
        right = jnp.concatenate([right, jnp.broadcast_to(ones, (HALF, 128))], axis=1)
        return scores(left, right)

    def steps(first, count):
        todo = [piece(list_ref[first + t]) for t in range(count)]
        sums = [
            jnp.sum(jnp.exp2(weighted(s, s_row, k_row)).reshape(HALF // 8, 8, HALF), axis=0)
            for s, _, s_row, k_row in todo
        ]
        for (_, k, _, _), part in zip(todo, sums):
            r_ref[k // 2, k % 2] += part

    large_steps = rounds // (UNROLL // REST)

    def large_step(i, carry):
        steps(i * UNROLL, UNROLL)
        return carry

    def small_step(i, carry):
        steps(i * REST, REST)
        return carry

    lax.fori_loop(0, large_steps, large_step, 0)
    lax.fori_loop(large_steps * (UNROLL // REST), rounds, small_step, 0)

    large = jnp.where((weight > 0.5 * LOWEST) & ~(jnp.abs(weight) <= 128.0), 1.0, 0.0)
    bad = jnp.max(large, axis=0, keepdims=True)
    bad = jnp.maximum(bad[:, 0:HALF], bad[:, HALF:])
    for half in range(2):
        cut = slice(half * HALF, (half + 1) * HALF)
        total = jnp.sum(r_ref[0:kept_blocks, half], axis=1)
        live = live_ref[:, cut] > 0.5 * LOWEST
        fine = (total >= 2.0**-86) & (total <= 2.0**126)
        off = jnp.where(live & ~fine, 1.0, 0.0)
        bad = jnp.maximum(bad, jnp.max(off, axis=0, keepdims=True))
        out_ref[:, cut] = jnp.where(live, jnp.log2(jnp.where(live, total, 1.0)), LOWEST)
    bad = jnp.max(bad)

    @pl.when(bad > 0.0)
    def _():
        m_ref[...] = jnp.full(m_ref.shape, LOWEST, jnp.float32)
        r_ref[...] = jnp.zeros(r_ref.shape, jnp.float32)

        def one_piece(i, carry):
            s, k, s_row, k_row = piece(list_ref[i])
            block = jnp.minimum(s // 2, summed_blocks - 1)
            w = weight_ref[pl.ds(block, 1), pl.ds(pl.multiple_of((s % 2) * HALF, HALF), HALF)]
            column = jnp.transpose(jnp.broadcast_to(w, (128, HALF)))
            x = scores(*sides(s_row, k_row)) + jnp.concatenate([column, column], axis=1)
            before = m_ref[k // 2, k % 2, 0:1]
            after = jnp.maximum(before, jnp.max(x, axis=0, keepdims=True))
            scaled = r_ref[k // 2, k % 2, 0:1] * jnp.exp2(before - after)
            m_ref[k // 2, k % 2, 0:1] = after
            r_ref[k // 2, k % 2, 0:1] = scaled + jnp.sum(jnp.exp2(x - after), axis=0, keepdims=True)
            return carry

        lax.fori_loop(0, rounds * REST, one_piece, 0)
        for half in range(2):
            cut = slice(half * HALF, (half + 1) * HALF)
            live = live_ref[:, cut] > 0.5 * LOWEST
            total = jnp.where(live, r_ref[0:kept_blocks, half, 0, :], 1.0)
            out_ref[:, cut] = jnp.where(live, m_ref[0:kept_blocks, half, 0, :] + jnp.log2(total), LOWEST)


def half_sweep(sum_couriers, work, rounds, summed, kept, weight, live, name):
    smem = pl.BlockSpec(memory_space=pltpu.SMEM)
    vmem = pl.BlockSpec(memory_space=pltpu.VMEM)
    summed_blocks, kept_blocks = weight.shape[0], live.shape[0]

    def kernel(*refs):
        pass_kernel(sum_couriers, *refs)

    return pl.pallas_call(
        kernel,
        out_shape=jax.ShapeDtypeStruct((kept_blocks, BLOCK), jnp.float32),
        in_specs=[smem, smem] + [vmem] * 4,
        out_specs=vmem,
        scratch_shapes=pass_scratch(kept_blocks),
        compiler_params=pltpu.CompilerParams(vmem_limit_bytes=VMEM_LIMIT),
        cost_estimate=PASS_COST,
        name=name,
    )(work, rounds, summed, kept, weight, live)


PASS_COST = pl.CostEstimate(flops=28 * 2 * 512 * 512 * 128, bytes_accessed=6 << 20, transcendentals=28 * 512 * 512)


def pass_scratch(kept_blocks):
    return [
        pltpu.VMEM((HALF, 128), jnp.bfloat16),
        pltpu.VMEM((kept_blocks + 1, 2, 8, HALF), jnp.float32),
        pltpu.VMEM((kept_blocks + 1, 2, 8, HALF), jnp.float32),
    ]


def first_kernel(early, work_ref, rounds_ref, zone_ref, has_ref, *refs):
    count = len(EARLY) if early else PARTS
    parts, (orders_ref, live_ref, out_ref, couriers_ref, log_cap_ref, w_ref, r_ref, m_ref, weight_ref, here_ref, sem) = (
        refs[:count],
        refs[count:],
    )
    rows = couriers_ref.shape[0] // count
    copies = [
        pltpu.make_async_copy(part, couriers_ref.at[pl.ds(i * rows, rows), :], sem.at[i]) for i, part in enumerate(parts)
    ]
    for copy in copies:
        copy.start()
    for block in range(OB_DEV):
        named = has_ref[block if early else OB_DEV + block] > 0
        here_ref[block : block + 1, :] = jnp.where(named, live_ref[block : block + 1, :], LOWEST)
    for copy in copies:
        copy.wait()
    for zone in range(ZONES):
        slot = slot_of(jnp.int32(zone), zone_ref[0])
        if early:
            _, slot = early_slot(slot)
        row = slot * COURIER_ROWS + BLOCK
        tail = couriers_ref[pl.ds(pl.multiple_of(row, 16), 16), :].astype(jnp.float32)
        log_cap_ref[zone : zone + 1, :] = jnp.concatenate([tail[i : i + 1] for i in range(4)], axis=1)
    cap = log_cap_ref[...]
    live = cap > 0.0
    log_cap_ref[...] = jnp.where(live, jnp.log2(jnp.where(live, cap, 1.0)), LOWEST)
    weight_ref[...] = jnp.where(live, 0.0, LOWEST)
    pass_kernel(True, work_ref, rounds_ref, couriers_ref, orders_ref, weight_ref, here_ref, out_ref, w_ref, r_ref, m_ref)


def first_half_sweep(early, work, rounds, zone, has, parts, orders, live, name):
    smem = pl.BlockSpec(memory_space=pltpu.SMEM)
    vmem = pl.BlockSpec(memory_space=pltpu.VMEM)

    def kernel(*refs):
        first_kernel(early, *refs)

    couriers = (len(parts) * 4 * COURIER_ROWS, EMB)
    kept_out = () if early else (
        jax.ShapeDtypeStruct(couriers, jnp.bfloat16),
        jax.ShapeDtypeStruct((ZONES, BLOCK), jnp.float32),
    )
    as_scratch = [pltpu.VMEM(couriers, jnp.bfloat16), pltpu.VMEM((ZONES, BLOCK), jnp.float32)] if early else []
    return pl.pallas_call(
        kernel,
        out_shape=(jax.ShapeDtypeStruct((OB_DEV, BLOCK), jnp.float32),) + kept_out,
        in_specs=[smem] * 4 + [pl.BlockSpec(memory_space=pl.ANY)] * len(parts) + [vmem] * 2,
        out_specs=(vmem,) * (1 + len(kept_out)),
        scratch_shapes=as_scratch
        + pass_scratch(OB_DEV)
        + [
            pltpu.VMEM((ZONES, BLOCK), jnp.float32),
            pltpu.VMEM((OB_DEV, BLOCK), jnp.float32),
            pltpu.SemaphoreType.DMA((len(parts),)),
        ],
        compiler_params=pltpu.CompilerParams(vmem_limit_bytes=VMEM_LIMIT),
        cost_estimate=pl.CostEstimate(flops=14 * 2 * 512 * 512 * 128, bytes_accessed=6 << 20, transcendentals=14 * 512 * 512),
        name=name,
    )(work, rounds, zone.reshape(1), has, *parts, orders, live)


def shards(
    order_features,
    w_in,
    bias_in,
    w_out,
    bias_out,
    courier_embed,
    courier_cap,
    adjacency,
    order_count,
    courier_count,
):
    sub = lax.axis_index("sub")
    positions = jnp.arange(BLOCK, dtype=jnp.int32)

    own_live = positions < courier_count[0]
    row = gather_row(*pack(courier_count, courier_embed, courier_cap))
    row, bias_in = lax.optimization_barrier((row, bias_in))
    orders = embed_orders(order_features, w_in, bias_in, w_out, bias_out)
    order_live = positions[None, :] < order_count[:, None]
    live = jnp.where(order_live, 0.0, LOWEST)
    early_list, late_list, early_rounds, late_rounds, has = first_lists(adjacency, order_count)
    zone = lax.axis_index("zone")

    own = [row] + [plane_step(row, 1, step) for step in (1, 2, 3)]
    other = [other_core(row)] + [None] * 3
    parts = own + other
    (early_partial,) = first_half_sweep(
        True, early_list, early_rounds, zone, has, [parts[p] for p in EARLY], orders, live, "orders_1_early"
    )
    own[1], own[2], own[3], early_partial = lax.optimization_barrier((own[1], own[2], own[3], early_partial))
    for step in (1, 2, 3):
        other[step] = other_core(own[step])
    late_partial, couriers, log_cap = first_half_sweep(
        False, late_list, late_rounds, zone, has, own + other, orders, live, "orders_1"
    )
    partial = join(early_partial, late_partial)

    mine = adjacency % SUBS == sub
    order_here = jnp.where(order_live & jnp.any(mine, axis=1, keepdims=True), 0.0, LOWEST)

    def order_dual_of(partial):
        return jnp.where(order_live, -join_subs(partial), LOWEST)

    courier_live = log_cap > 0.5 * LOWEST
    work, rounds = work_list(adjacency, order_count, courier_live[:, HALF].astype(jnp.int32))
    named = jnp.any(
        (adjacency.reshape(-1)[None, :] == jnp.arange(ZONES)[:, None] * SUBS + sub), axis=1, keepdims=True
    )
    courier_here = jnp.where(courier_live & named, 0.0, LOWEST)

    def courier_pass(order_dual, name):
        return half_sweep(False, work, rounds, orders, couriers, order_dual, courier_here, name)

    order_dual = order_dual_of(partial)
    sums = join_zones(courier_pass(order_dual, "couriers_1"))
    courier_dual = jnp.where(courier_live, log_cap - sums, LOWEST)
    order_dual = order_dual_of(half_sweep(True, work, rounds, couriers, orders, courier_dual, order_here, "orders_2"))
    partial = courier_pass(order_dual, "couriers_2")
    parts = lax.all_to_all(partial, "zone", 0, 0, tiled=True)
    highest = jnp.max(parts, axis=0)
    total = highest + jnp.log2(jnp.sum(jnp.exp2(parts - highest[None]), axis=0))
    own_log_cap = jnp.log2(courier_cap.astype(jnp.float32))
    courier_out = jnp.where(own_live, DUAL_SCALE * (own_log_cap - total), 0.0)
    order_out = jnp.where(order_live, DUAL_SCALE * order_dual, 0.0)
    return order_out.reshape(-1), courier_out


def solution(mesh):
    return jax.shard_map(
        shards,
        mesh=mesh,
        in_specs=(
            P("zone", None),
            P(),
            P(),
            P(),
            P(),
            P(("zone", "sub"), None),
            P(("zone", "sub")),
            P("zone", None),
            P("zone"),
            P(("zone", "sub")),
        ),
        out_specs=(P("zone"), P(("zone", "sub"))),
        check_vma=False,
    )
```

```python
import math

import jax
import jax.numpy as jnp
from jax import lax
from jax.experimental import pallas as pl
from jax.experimental.pallas import tpu as pltpu
from jax.sharding import PartitionSpec as P

BLOCK = 512
EMB = 128
HID = 512
ADJ = 8
OB_DEV = 16
ZONES = 32
SUBS = 4
HALF = 256
COURIER_ROWS = BLOCK + 16
UNROLL = 32
REST = 8
MOST_ENTRIES = 256
LIST_SIZE = MOST_ENTRIES + 2 * REST
NO_ORDER = 2 * OB_DEV
NO_COURIER = 2 * ZONES

TEMPER = 0.2
LOWEST = -1e30
SCORE_SCALE = math.log2(math.e) / (TEMPER * math.sqrt(EMB))
DUAL_SCALE = TEMPER * math.log(2.0)

VMEM_LIMIT = 16 * 1024 * 1024


def zone_of(y, x, core):
    return ((y % 4) * 4 + (x % 4)) * 2 + core


PLACES = [(y, x, core) for y in range(4) for x in range(4) for core in range(2)]


def other_core(value):
    return lax.ppermute(value, "zone", [(zone_of(y, x, c), zone_of(y, x, 1 - c)) for y, x, c in PLACES])


def along_z(value, step):
    return lax.ppermute(value, "sub", [(i, (i + step) % SUBS) for i in range(SUBS)])


def plane_step(value, stage, step):
    pairs = []
    for y, x, c in PLACES:
        to = (y, x + step, c) if stage == c else (y + step, x, c)
        pairs.append((zone_of(y, x, c), zone_of(*to)))
    return lax.ppermute(value, "zone", pairs)


def pack_kernel(count_ref, embed_ref, cap_hbm, block_ref, row_ref, cap_ref, sem):
    copy = pltpu.make_async_copy(embed_ref, block_ref.at[pl.ds(0, BLOCK), :], sem.at[0])
    copy_row = pltpu.make_async_copy(embed_ref, row_ref.at[pl.ds(0, BLOCK), :], sem.at[1])
    copy.start()
    copy_row.start()
    copy_cap = pltpu.make_async_copy(cap_hbm, cap_ref, sem.at[2])
    copy_cap.start()
    copy_cap.wait()
    lane = lax.broadcasted_iota(jnp.int32, (1, BLOCK), 1)
    cap = jnp.where(lane < count_ref[0], cap_ref[...].astype(jnp.float32).reshape(1, BLOCK), 0.0)
    rows = [cap[:, i * EMB : (i + 1) * EMB] for i in range(4)]
    tail = jnp.concatenate(rows + [jnp.zeros((12, EMB), jnp.float32)], axis=0).astype(jnp.bfloat16)
    block_ref[pl.ds(BLOCK, 16), :] = tail
    row_ref[pl.ds(BLOCK, 16), :] = tail
    copy.wait()
    copy_row.wait()


def pack(count, embed, cap):
    vmem = pl.BlockSpec(memory_space=pltpu.VMEM)
    return pl.pallas_call(
        pack_kernel,
        out_shape=(
            jax.ShapeDtypeStruct((COURIER_ROWS, EMB), jnp.bfloat16),
            jax.ShapeDtypeStruct((4 * COURIER_ROWS, EMB), jnp.bfloat16),
        ),
        in_specs=[pl.BlockSpec(memory_space=pltpu.SMEM)] + [pl.BlockSpec(memory_space=pltpu.HBM)] * 2,
        out_specs=(vmem, vmem),
        scratch_shapes=[pltpu.VMEM((BLOCK,), cap.dtype), pltpu.SemaphoreType.DMA((3,))],
        compiler_params=pltpu.CompilerParams(vmem_limit_bytes=4 * 1024 * 1024),
        name="pack",
    )(count, *[pltpu.with_memory_space_constraint(value, pltpu.HBM) for value in (embed, cap)])


def gather_row(block, row):
    for step in (1, 2, 3):
        row = lax.dynamic_update_slice(row, plane_step(block, 0, step), (step * COURIER_ROWS, 0))
    return row


PARTS = 8
EARLY = (0, 4)


def slot_of(zone, me):
    back_x = ((me >> 1) - (zone >> 1)) & 3
    back_y = ((me >> 3) - (zone >> 3)) & 3
    odd = zone & 1
    first = jnp.where(odd == 0, back_x, back_y)
    second = jnp.where(odd == 0, back_y, back_x)
    return ((me ^ zone) & 1) * 16 + second * 4 + first


def early_slot(slot):
    part = slot >> 2
    index = sum(jnp.where(part == p, i, 0) for i, p in enumerate(EARLY))
    is_early = sum(jnp.where(part == p, 1, 0) for p in EARLY)
    return is_early, index * 4 + (slot & 3)


def join(*parts):
    highest = parts[0]
    for part in parts[1:]:
        highest = jnp.maximum(highest, part)
    total = jnp.exp2(parts[0] - highest)
    for part in parts[1:]:
        total = total + jnp.exp2(part - highest)
    return highest + jnp.log2(total)


def join_subs(value):
    return join(value, along_z(value, 1), along_z(value, 2), along_z(value, 3))


def join_zones(value):
    value = join(value, other_core(value))
    for stage in range(2):
        value = join(value, *[plane_step(value, stage, step) for step in (1, 2, 3)])
    return value


EMBED_ROWS = 4096


def embed_kernel(x_hbm, w_in_hbm, b_in_hbm, w_out_hbm, b_out_hbm, o_ref, x_ref, w_in_ref, b_in_ref, w_out_ref, b_out_ref, sem):
    steps = x_ref.shape[0] // EMBED_ROWS

    def rows_copy(i):
        rows = pl.ds(pl.multiple_of(i * EMBED_ROWS, EMBED_ROWS), EMBED_ROWS)
        return pltpu.make_async_copy(x_hbm.at[rows, :], x_ref.at[rows, :], sem.at[i])

    parameters = [
        pltpu.make_async_copy(source, target, sem.at[steps + i])
        for i, (source, target) in enumerate(
            [(w_in_hbm, w_in_ref), (b_in_hbm, b_in_ref), (w_out_hbm, w_out_ref), (b_out_hbm, b_out_ref)]
        )
    ]
    for copy in parameters:
        copy.start()
    for i in range(steps):
        rows_copy(i).start()
    for copy in parameters:
        copy.wait()

    def one_step(i, carry):
        rows_copy(i).wait()
        for start in range(0, EMBED_ROWS, BLOCK):
            rows = pl.ds(pl.multiple_of(i * EMBED_ROWS + start, BLOCK), BLOCK)
            v = jnp.dot(x_ref[rows, :], w_in_ref[...], preferred_element_type=jnp.float32)
            v = 0.5 * (v + b_in_ref[...])
            hidden = (v + v * jnp.tanh(v)).astype(jnp.bfloat16)
            out = jnp.dot(hidden, w_out_ref[...], preferred_element_type=jnp.float32)
            o_ref[rows, :] = ((out + b_out_ref[...]) * SCORE_SCALE).astype(jnp.bfloat16)
        return carry

    lax.fori_loop(0, steps, one_step, 0)


def embed_orders(features, w_in, bias_in, w_out, bias_out):
    rows = features.shape[0]
    operands = (features, w_in, bias_in.reshape(1, HID), w_out, bias_out.reshape(1, EMB))
    return pl.pallas_call(
        embed_kernel,
        out_shape=jax.ShapeDtypeStruct((rows, EMB), jnp.bfloat16),
        in_specs=[pl.BlockSpec(memory_space=pltpu.HBM)] * len(operands),
        out_specs=pl.BlockSpec(memory_space=pltpu.VMEM),
        scratch_shapes=[pltpu.VMEM(value.shape, value.dtype) for value in operands]
        + [pltpu.SemaphoreType.DMA((rows // EMBED_ROWS + 4,))],
        compiler_params=pltpu.CompilerParams(vmem_limit_bytes=VMEM_LIMIT),
        cost_estimate=pl.CostEstimate(
            flops=4 * rows * EMB * HID, bytes_accessed=4 * rows * EMB, transcendentals=rows * HID
        ),
        name="embed_orders",
    )(*[pltpu.with_memory_space_constraint(value, pltpu.HBM) for value in operands])


def list_kernel(pair_ref, two_ref, list_ref, rounds_ref):
    def one_pair(p, n):
        e = pair_ref[p]
        mine = (e >> 24) & 1
        order_two = (e >> 25) & 1
        courier_two = mine * two_ref[(e >> 9) & 31]
        e = e & 0xFFFFFF
        list_ref[n] = e
        n = n + mine
        list_ref[n] = e + 257
        n = n + courier_two
        list_ref[n] = e + 65536
        n = n + order_two
        list_ref[n] = e + 65536 + 257
        return n + (order_two & courier_two)

    n = lax.fori_loop(0, OB_DEV * ADJ, one_pair, jnp.int32(0), unroll=8)
    for i in range(REST):
        list_ref[n + i] = jnp.int32(NO_ORDER * 65536 + NO_COURIER * 256)
    rounds_ref[0] = (n + REST - 1) // REST


def first_list_kernel(pair_ref, early_ref, late_ref, early_rounds_ref, late_rounds_ref, has_ref):
    def one_block(b, counts):
        early_n, late_n = counts
        early_any, late_any = jnp.int32(0), jnp.int32(0)
        for i in range(ADJ):
            e = pair_ref[b * ADJ + i]
            early = (e >> 24) & 1
            late = (e >> 25) & 1
            two = (e >> 26) & 1
            e = e & 0xFFFFFF
            early_any, late_any = early_any | early, late_any | late
            for step, more in ((0, 1), (257, 1), (65536, two), (65536 + 257, two)):
                early_ref[early_n] = e + step
                late_ref[late_n] = e + step
                early_n = early_n + (early & more)
                late_n = late_n + (late & more)
        has_ref[b] = early_any
        has_ref[OB_DEV + b] = late_any
        return early_n, late_n

    counts = lax.fori_loop(0, OB_DEV, one_block, (jnp.int32(0), jnp.int32(0)))
    for n, list_ref, rounds_ref in ((counts[0], early_ref, early_rounds_ref), (counts[1], late_ref, late_rounds_ref)):
        for i in range(REST):
            list_ref[n + i] = jnp.int32(NO_ORDER * 65536 + NO_COURIER * 256)
        rounds_ref[0] = (n + REST - 1) // REST


def call_on_scalars(kernel, sizes, name, *operands):
    smem = pl.BlockSpec(memory_space=pltpu.SMEM)
    return pl.pallas_call(
        kernel,
        out_shape=tuple(jax.ShapeDtypeStruct((size,), jnp.int32) for size in sizes),
        in_specs=[smem] * len(operands),
        out_specs=(smem,) * len(sizes),
        compiler_params=pltpu.CompilerParams(vmem_limit_bytes=1024 * 1024),
        name=name,
    )(*operands)


def pair_fields(adjacency, order_count):
    flat = adjacency.reshape(-1)
    z = flat >> 2
    mine = jnp.where((flat & 3) == lax.axis_index("sub"), 1, 0)
    two = jnp.repeat(jnp.where(order_count > HALF, 1, 0), ADJ)
    block = jnp.arange(OB_DEV * ADJ, dtype=jnp.int32) // ADJ
    slot = slot_of(z, lax.axis_index("zone"))
    return (2 * block << 16) + (2 * z << 8), slot, mine, two


def first_lists(adjacency, order_count):
    entry, slot, mine, two = pair_fields(adjacency, order_count)
    is_early, place = early_slot(slot)
    entry = entry + 2 * jnp.where(is_early == 1, place, slot)
    pairs = entry + ((mine & is_early) << 24) + ((mine & (1 - is_early)) << 25) + (two << 26)
    sizes = (LIST_SIZE, LIST_SIZE, 1, 1, 2 * OB_DEV)
    return call_on_scalars(first_list_kernel, sizes, "first_lists", pairs.astype(jnp.int32))


def work_list(adjacency, order_count, courier_two):
    entry, slot, mine, two = pair_fields(adjacency, order_count)
    pairs = entry + 2 * slot + (mine << 24) + ((mine * two) << 25)
    return call_on_scalars(list_kernel, (LIST_SIZE, 1), "work_list", pairs.astype(jnp.int32), courier_two)


def pass_kernel(sum_couriers, list_ref, rounds_ref, summed_ref, kept_ref, weight_ref, live_ref, out_ref, w_ref, r_ref, m_ref):
    summed_blocks, kept_blocks = weight_ref.shape[0], live_ref.shape[0]
    rounds = rounds_ref[0]
    weight = weight_ref[...]

    high = weight.astype(jnp.bfloat16).astype(jnp.float32)
    low = weight - high
    blank = jnp.zeros((64 - 2 * summed_blocks, 128), jnp.float32)
    for part in range(2):
        rows = []
        for value in (high, low):
            rows += [value[:, part * 128 : part * 128 + 128], value[:, HALF + part * 128 : HALF + part * 128 + 128]]
            if summed_blocks < 32:
                rows.append(blank)
        w_ref[part * 128 : part * 128 + 128, :] = jnp.transpose(jnp.concatenate(rows, axis=0)).astype(jnp.bfloat16)
    r_ref[...] = jnp.zeros(r_ref.shape, jnp.float32)
    lanes = lax.broadcasted_iota(jnp.int32, (1, 128), 1) % 64

    def piece(e):
        order, courier, slot = e >> 16, (e >> 8) & 255, e & 255
        order_row = jnp.minimum(order, 2 * OB_DEV - 1) * HALF
        courier_row = (slot >> 1) * COURIER_ROWS + (slot & 1) * HALF
        return (courier, order, courier_row, order_row) if sum_couriers else (order, courier, order_row, courier_row)

    def sides(s_row, k_row):
        left = summed_ref[pl.ds(pl.multiple_of(s_row, 16), HALF), :]
        right = kept_ref[pl.ds(pl.multiple_of(k_row, 16), HALF), :]
        return left, right

    def scores(left, right):
        return lax.dot_general(left, right, (((1,), (1,)), ((), ())), preferred_element_type=jnp.float32)

    def weighted(s, s_row, k_row):
        left, right = sides(s_row, k_row)
        lane = (s % 2) * summed_blocks + s // 2
        ones = jnp.where(lanes == lane, 1.0, 0.0).astype(jnp.bfloat16)
        left = jnp.concatenate([left, w_ref[...]], axis=1)
        right = jnp.concatenate([right, jnp.broadcast_to(ones, (HALF, 128))], axis=1)
        return scores(left, right)

    def steps(first, count):
        todo = [piece(list_ref[first + t]) for t in range(count)]
        sums = [
            jnp.sum(jnp.exp2(weighted(s, s_row, k_row)).reshape(HALF // 8, 8, HALF), axis=0)
            for s, _, s_row, k_row in todo
        ]
        for (_, k, _, _), part in zip(todo, sums):
            r_ref[k // 2, k % 2] += part

    large_steps = rounds // (UNROLL // REST)

    def large_step(i, carry):
        steps(i * UNROLL, UNROLL)
        return carry

    def small_step(i, carry):
        steps(i * REST, REST)
        return carry

    lax.fori_loop(0, large_steps, large_step, 0)
    lax.fori_loop(large_steps * (UNROLL // REST), rounds, small_step, 0)

    large = jnp.where((weight > 0.5 * LOWEST) & ~(jnp.abs(weight) <= 128.0), 1.0, 0.0)
    bad = jnp.max(large, axis=0, keepdims=True)
    bad = jnp.maximum(bad[:, 0:HALF], bad[:, HALF:])
    for half in range(2):
        cut = slice(half * HALF, (half + 1) * HALF)
        total = jnp.sum(r_ref[0:kept_blocks, half], axis=1)
        live = live_ref[:, cut] > 0.5 * LOWEST
        fine = (total >= 2.0**-86) & (total <= 2.0**126)
        off = jnp.where(live & ~fine, 1.0, 0.0)
        bad = jnp.maximum(bad, jnp.max(off, axis=0, keepdims=True))
        out_ref[:, cut] = jnp.where(live, jnp.log2(jnp.where(live, total, 1.0)), LOWEST)
    bad = jnp.max(bad)

    @pl.when(bad > 0.0)
    def _():
        m_ref[...] = jnp.full(m_ref.shape, LOWEST, jnp.float32)
        r_ref[...] = jnp.zeros(r_ref.shape, jnp.float32)

        def one_piece(i, carry):
            s, k, s_row, k_row = piece(list_ref[i])
            block = jnp.minimum(s // 2, summed_blocks - 1)
            w = weight_ref[pl.ds(block, 1), pl.ds(pl.multiple_of((s % 2) * HALF, HALF), HALF)]
            column = jnp.transpose(jnp.broadcast_to(w, (128, HALF)))
            x = scores(*sides(s_row, k_row)) + jnp.concatenate([column, column], axis=1)
            before = m_ref[k // 2, k % 2, 0:1]
            after = jnp.maximum(before, jnp.max(x, axis=0, keepdims=True))
            scaled = r_ref[k // 2, k % 2, 0:1] * jnp.exp2(before - after)
            m_ref[k // 2, k % 2, 0:1] = after
            r_ref[k // 2, k % 2, 0:1] = scaled + jnp.sum(jnp.exp2(x - after), axis=0, keepdims=True)
            return carry

        lax.fori_loop(0, rounds * REST, one_piece, 0)
        for half in range(2):
            cut = slice(half * HALF, (half + 1) * HALF)
            live = live_ref[:, cut] > 0.5 * LOWEST
            total = jnp.where(live, r_ref[0:kept_blocks, half, 0, :], 1.0)
            out_ref[:, cut] = jnp.where(live, m_ref[0:kept_blocks, half, 0, :] + jnp.log2(total), LOWEST)


def half_sweep(sum_couriers, work, rounds, summed, kept, weight, live, name):
    smem = pl.BlockSpec(memory_space=pltpu.SMEM)
    vmem = pl.BlockSpec(memory_space=pltpu.VMEM)
    summed_blocks, kept_blocks = weight.shape[0], live.shape[0]

    def kernel(*refs):
        pass_kernel(sum_couriers, *refs)

    return pl.pallas_call(
        kernel,
        out_shape=jax.ShapeDtypeStruct((kept_blocks, BLOCK), jnp.float32),
        in_specs=[smem, smem] + [vmem] * 4,
        out_specs=vmem,
        scratch_shapes=pass_scratch(kept_blocks),
        compiler_params=pltpu.CompilerParams(vmem_limit_bytes=VMEM_LIMIT),
        cost_estimate=PASS_COST,
        name=name,
    )(work, rounds, summed, kept, weight, live)


PASS_COST = pl.CostEstimate(flops=28 * 2 * 512 * 512 * 128, bytes_accessed=6 << 20, transcendentals=28 * 512 * 512)


def pass_scratch(kept_blocks):
    return [
        pltpu.VMEM((HALF, 128), jnp.bfloat16),
        pltpu.VMEM((kept_blocks + 1, 2, 8, HALF), jnp.float32),
        pltpu.VMEM((kept_blocks + 1, 2, 8, HALF), jnp.float32),
    ]


def first_kernel(early, work_ref, rounds_ref, zone_ref, has_ref, *refs):
    count = len(EARLY) if early else PARTS
    parts, (orders_ref, live_ref, out_ref, couriers_ref, log_cap_ref, w_ref, r_ref, m_ref, weight_ref, here_ref, sem) = (
        refs[:count],
        refs[count:],
    )
    rows = couriers_ref.shape[0] // count
    copies = [
        pltpu.make_async_copy(part, couriers_ref.at[pl.ds(i * rows, rows), :], sem.at[i]) for i, part in enumerate(parts)
    ]
    for copy in copies:
        copy.start()
    for block in range(OB_DEV):
        named = has_ref[block if early else OB_DEV + block] > 0
        here_ref[block : block + 1, :] = jnp.where(named, live_ref[block : block + 1, :], LOWEST)
    for copy in copies:
        copy.wait()
    for zone in range(ZONES):
        slot = slot_of(jnp.int32(zone), zone_ref[0])
        if early:
            _, slot = early_slot(slot)
        row = slot * COURIER_ROWS + BLOCK
        tail = couriers_ref[pl.ds(pl.multiple_of(row, 16), 16), :].astype(jnp.float32)
        log_cap_ref[zone : zone + 1, :] = jnp.concatenate([tail[i : i + 1] for i in range(4)], axis=1)
    cap = log_cap_ref[...]
    live = cap > 0.0
    log_cap_ref[...] = jnp.where(live, jnp.log2(jnp.where(live, cap, 1.0)), LOWEST)
    weight_ref[...] = jnp.where(live, 0.0, LOWEST)
    pass_kernel(True, work_ref, rounds_ref, couriers_ref, orders_ref, weight_ref, here_ref, out_ref, w_ref, r_ref, m_ref)


def first_half_sweep(early, work, rounds, zone, has, parts, orders, live, name):
    smem = pl.BlockSpec(memory_space=pltpu.SMEM)
    vmem = pl.BlockSpec(memory_space=pltpu.VMEM)

    def kernel(*refs):
        first_kernel(early, *refs)

    couriers = (len(parts) * 4 * COURIER_ROWS, EMB)
    kept_out = () if early else (
        jax.ShapeDtypeStruct(couriers, jnp.bfloat16),
        jax.ShapeDtypeStruct((ZONES, BLOCK), jnp.float32),
    )
    as_scratch = [pltpu.VMEM(couriers, jnp.bfloat16), pltpu.VMEM((ZONES, BLOCK), jnp.float32)] if early else []
    return pl.pallas_call(
        kernel,
        out_shape=(jax.ShapeDtypeStruct((OB_DEV, BLOCK), jnp.float32),) + kept_out,
        in_specs=[smem] * 4 + [pl.BlockSpec(memory_space=pl.ANY)] * len(parts) + [vmem] * 2,
        out_specs=(vmem,) * (1 + len(kept_out)),
        scratch_shapes=as_scratch
        + pass_scratch(OB_DEV)
        + [
            pltpu.VMEM((ZONES, BLOCK), jnp.float32),
            pltpu.VMEM((OB_DEV, BLOCK), jnp.float32),
            pltpu.SemaphoreType.DMA((len(parts),)),
        ],
        compiler_params=pltpu.CompilerParams(vmem_limit_bytes=VMEM_LIMIT),
        cost_estimate=pl.CostEstimate(flops=14 * 2 * 512 * 512 * 128, bytes_accessed=6 << 20, transcendentals=14 * 512 * 512),
        name=name,
    )(work, rounds, zone.reshape(1), has, *parts, orders, live)


def shards(
    order_features,
    w_in,
    bias_in,
    w_out,
    bias_out,
    courier_embed,
    courier_cap,
    adjacency,
    order_count,
    courier_count,
):
    sub = lax.axis_index("sub")
    positions = jnp.arange(BLOCK, dtype=jnp.int32)

    own_live = positions < courier_count[0]
    row = gather_row(*pack(courier_count, courier_embed, courier_cap))
    lists = first_lists(adjacency, order_count)
    row, bias_in, lists = lax.optimization_barrier((row, bias_in, lists))
    early_list, late_list, early_rounds, late_rounds, has = lists
    orders = embed_orders(order_features, w_in, bias_in, w_out, bias_out)
    order_live = positions[None, :] < order_count[:, None]
    live = jnp.where(order_live, 0.0, LOWEST)
    zone = lax.axis_index("zone")

    own = [row] + [plane_step(row, 1, step) for step in (1, 2, 3)]
    other = [other_core(row)] + [None] * 3
    parts = own + other
    (early_partial,) = first_half_sweep(
        True, early_list, early_rounds, zone, has, [parts[p] for p in EARLY], orders, live, "orders_1_early"
    )
    own[1], own[2], own[3], early_partial = lax.optimization_barrier((own[1], own[2], own[3], early_partial))
    for step in (1, 2, 3):
        other[step] = other_core(own[step])
    late_partial, couriers, log_cap = first_half_sweep(
        False, late_list, late_rounds, zone, has, own + other, orders, live, "orders_1"
    )
    partial = join(early_partial, late_partial)

    mine = adjacency % SUBS == sub
    order_here = jnp.where(order_live & jnp.any(mine, axis=1, keepdims=True), 0.0, LOWEST)

    def order_dual_of(partial):
        return jnp.where(order_live, -join_subs(partial), LOWEST)

    courier_live = log_cap > 0.5 * LOWEST
    work, rounds = work_list(adjacency, order_count, courier_live[:, HALF].astype(jnp.int32))
    named = jnp.any(
        (adjacency.reshape(-1)[None, :] == jnp.arange(ZONES)[:, None] * SUBS + sub), axis=1, keepdims=True
    )
    courier_here = jnp.where(courier_live & named, 0.0, LOWEST)

    def courier_pass(order_dual, name):
        return half_sweep(False, work, rounds, orders, couriers, order_dual, courier_here, name)

    order_dual = order_dual_of(partial)
    sums = join_zones(courier_pass(order_dual, "couriers_1"))
    courier_dual = jnp.where(courier_live, log_cap - sums, LOWEST)
    order_dual = order_dual_of(half_sweep(True, work, rounds, couriers, orders, courier_dual, order_here, "orders_2"))
    partial = courier_pass(order_dual, "couriers_2")
    parts = lax.all_to_all(partial, "zone", 0, 0, tiled=True)
    highest = jnp.max(parts, axis=0)
    total = highest + jnp.log2(jnp.sum(jnp.exp2(parts - highest[None]), axis=0))
    own_log_cap = jnp.log2(courier_cap.astype(jnp.float32))
    courier_out = jnp.where(own_live, DUAL_SCALE * (own_log_cap - total), 0.0)
    order_out = jnp.where(order_live, DUAL_SCALE * order_dual, 0.0)
    return order_out.reshape(-1), courier_out


def solution(mesh):
    return jax.shard_map(
        shards,
        mesh=mesh,
        in_specs=(
            P("zone", None),
            P(),
            P(),
            P(),
            P(),
            P(("zone", "sub"), None),
            P(("zone", "sub")),
            P("zone", None),
            P("zone"),
            P(("zone", "sub")),
        ),
        out_specs=(P("zone"), P(("zone", "sub"))),
        check_vma=False,
    )
```

```python
import math

import jax
import jax.numpy as jnp
from jax import lax
from jax.experimental import pallas as pl
from jax.experimental.pallas import tpu as pltpu
from jax.sharding import PartitionSpec as P

BLOCK = 512
EMB = 128
HID = 512
ADJ = 8
OB_DEV = 16
ZONES = 32
SUBS = 4
HALF = 256
COURIER_ROWS = BLOCK + 16
UNROLL = 32
REST = 8
MOST_ENTRIES = 256
LIST_SIZE = MOST_ENTRIES + 2 * REST
NO_ORDER = 2 * OB_DEV
NO_COURIER = 2 * ZONES

TEMPER = 0.2
LOWEST = -1e30
SCORE_SCALE = math.log2(math.e) / (TEMPER * math.sqrt(EMB))
DUAL_SCALE = TEMPER * math.log(2.0)

VMEM_LIMIT = 16 * 1024 * 1024


def zone_of(y, x, core):
    return ((y % 4) * 4 + (x % 4)) * 2 + core


PLACES = [(y, x, core) for y in range(4) for x in range(4) for core in range(2)]


def other_core(value):
    return lax.ppermute(value, "zone", [(zone_of(y, x, c), zone_of(y, x, 1 - c)) for y, x, c in PLACES])


def along_z(value, step):
    return lax.ppermute(value, "sub", [(i, (i + step) % SUBS) for i in range(SUBS)])


def plane_step(value, stage, step):
    pairs = []
    for y, x, c in PLACES:
        to = (y, x + step, c) if stage == c else (y + step, x, c)
        pairs.append((zone_of(y, x, c), zone_of(*to)))
    return lax.ppermute(value, "zone", pairs)


def pack_kernel(count_ref, embed_ref, cap_hbm, block_ref, row_ref, cap_ref, sem):
    copy = pltpu.make_async_copy(embed_ref, block_ref.at[pl.ds(0, BLOCK), :], sem.at[0])
    copy_row = pltpu.make_async_copy(embed_ref, row_ref.at[pl.ds(0, BLOCK), :], sem.at[1])
    copy.start()
    copy_row.start()
    copy_cap = pltpu.make_async_copy(cap_hbm, cap_ref, sem.at[2])
    copy_cap.start()
    copy_cap.wait()
    lane = lax.broadcasted_iota(jnp.int32, (1, BLOCK), 1)
    cap = jnp.where(lane < count_ref[0], cap_ref[...].astype(jnp.float32).reshape(1, BLOCK), 0.0)
    rows = [cap[:, i * EMB : (i + 1) * EMB] for i in range(4)]
    tail = jnp.concatenate(rows + [jnp.zeros((12, EMB), jnp.float32)], axis=0).astype(jnp.bfloat16)
    block_ref[pl.ds(BLOCK, 16), :] = tail
    row_ref[pl.ds(BLOCK, 16), :] = tail
    copy.wait()
    copy_row.wait()


def pack(count, embed, cap):
    vmem = pl.BlockSpec(memory_space=pltpu.VMEM)
    return pl.pallas_call(
        pack_kernel,
        out_shape=(
            jax.ShapeDtypeStruct((COURIER_ROWS, EMB), jnp.bfloat16),
            jax.ShapeDtypeStruct((4 * COURIER_ROWS, EMB), jnp.bfloat16),
        ),
        in_specs=[pl.BlockSpec(memory_space=pltpu.SMEM)] + [pl.BlockSpec(memory_space=pltpu.HBM)] * 2,
        out_specs=(vmem, vmem),
        scratch_shapes=[pltpu.VMEM((BLOCK,), cap.dtype), pltpu.SemaphoreType.DMA((3,))],
        compiler_params=pltpu.CompilerParams(vmem_limit_bytes=4 * 1024 * 1024),
        name="pack",
    )(count, *[pltpu.with_memory_space_constraint(value, pltpu.HBM) for value in (embed, cap)])


def gather_row(block, row):
    for step in (1, 2, 3):
        row = lax.dynamic_update_slice(row, plane_step(block, 0, step), (step * COURIER_ROWS, 0))
    return row


PARTS = 8
EARLY = (0, 4)


def slot_of(zone, me):
    back_x = ((me >> 1) - (zone >> 1)) & 3
    back_y = ((me >> 3) - (zone >> 3)) & 3
    odd = zone & 1
    first = jnp.where(odd == 0, back_x, back_y)
    second = jnp.where(odd == 0, back_y, back_x)
    return ((me ^ zone) & 1) * 16 + second * 4 + first


def early_slot(slot):
    part = slot >> 2
    index = sum(jnp.where(part == p, i, 0) for i, p in enumerate(EARLY))
    is_early = sum(jnp.where(part == p, 1, 0) for p in EARLY)
    return is_early, index * 4 + (slot & 3)


def join(*parts):
    highest = parts[0]
    for part in parts[1:]:
        highest = jnp.maximum(highest, part)
    total = jnp.exp2(parts[0] - highest)
    for part in parts[1:]:
        total = total + jnp.exp2(part - highest)
    return highest + jnp.log2(total)


def join_subs(value):
    return join(value, along_z(value, 1), along_z(value, 2), along_z(value, 3))


def join_zones(value):
    value = join(value, other_core(value))
    for stage in range(2):
        value = join(value, *[plane_step(value, stage, step) for step in (1, 2, 3)])
    return value


EMBED_ROWS = 4096


def embed_kernel(x_hbm, w_in_hbm, b_in_hbm, w_out_hbm, b_out_hbm, o_ref, x_ref, w_in_ref, b_in_ref, w_out_ref, b_out_ref, sem):
    steps = x_ref.shape[0] // EMBED_ROWS

    def rows_copy(i):
        rows = pl.ds(pl.multiple_of(i * EMBED_ROWS, EMBED_ROWS), EMBED_ROWS)
        return pltpu.make_async_copy(x_hbm.at[rows, :], x_ref.at[rows, :], sem.at[i])

    parameters = [
        pltpu.make_async_copy(source, target, sem.at[steps + i])
        for i, (source, target) in enumerate(
            [(w_in_hbm, w_in_ref), (b_in_hbm, b_in_ref), (w_out_hbm, w_out_ref), (b_out_hbm, b_out_ref)]
        )
    ]
    for copy in parameters:
        copy.start()
    for i in range(steps):
        rows_copy(i).start()
    for copy in parameters:
        copy.wait()

    def one_step(i, carry):
        rows_copy(i).wait()
        for start in range(0, EMBED_ROWS, BLOCK):
            rows = pl.ds(pl.multiple_of(i * EMBED_ROWS + start, BLOCK), BLOCK)
            v = jnp.dot(x_ref[rows, :], w_in_ref[...], preferred_element_type=jnp.float32)
            v = 0.5 * (v + b_in_ref[...])
            hidden = (v + v * jnp.tanh(v)).astype(jnp.bfloat16)
            out = jnp.dot(hidden, w_out_ref[...], preferred_element_type=jnp.float32)
            o_ref[rows, :] = ((out + b_out_ref[...]) * SCORE_SCALE).astype(jnp.bfloat16)
        return carry

    lax.fori_loop(0, steps, one_step, 0)


def embed_orders(features, w_in, bias_in, w_out, bias_out):
    rows = features.shape[0]
    operands = (features, w_in, bias_in.reshape(1, HID), w_out, bias_out.reshape(1, EMB))
    return pl.pallas_call(
        embed_kernel,
        out_shape=jax.ShapeDtypeStruct((rows, EMB), jnp.bfloat16),
        in_specs=[pl.BlockSpec(memory_space=pltpu.HBM)] * len(operands),
        out_specs=pl.BlockSpec(memory_space=pltpu.VMEM),
        scratch_shapes=[pltpu.VMEM(value.shape, value.dtype) for value in operands]
        + [pltpu.SemaphoreType.DMA((rows // EMBED_ROWS + 4,))],
        compiler_params=pltpu.CompilerParams(vmem_limit_bytes=VMEM_LIMIT),
        cost_estimate=pl.CostEstimate(
            flops=4 * rows * EMB * HID, bytes_accessed=4 * rows * EMB, transcendentals=rows * HID
        ),
        name="embed_orders",
    )(*[pltpu.with_memory_space_constraint(value, pltpu.HBM) for value in operands])


def list_kernel(pair_ref, two_ref, list_ref, rounds_ref):
    def one_pair(p, n):
        e = pair_ref[p]
        mine = (e >> 24) & 1
        order_two = (e >> 25) & 1
        courier_two = mine * two_ref[(e >> 9) & 31]
        e = e & 0xFFFFFF
        list_ref[n] = e
        n = n + mine
        list_ref[n] = e + 257
        n = n + courier_two
        list_ref[n] = e + 65536
        n = n + order_two
        list_ref[n] = e + 65536 + 257
        return n + (order_two & courier_two)

    n = lax.fori_loop(0, OB_DEV * ADJ, one_pair, jnp.int32(0), unroll=8)
    for i in range(REST):
        list_ref[n + i] = jnp.int32(NO_ORDER * 65536 + NO_COURIER * 256)
    rounds_ref[0] = (n + REST - 1) // REST


def first_list_kernel(pair_ref, early_ref, late_ref, early_rounds_ref, late_rounds_ref, has_ref):
    def one_block(b, counts):
        early_n, late_n = counts
        early_any, late_any = jnp.int32(0), jnp.int32(0)
        for i in range(ADJ):
            e = pair_ref[b * ADJ + i]
            early = (e >> 24) & 1
            late = (e >> 25) & 1
            two = (e >> 26) & 1
            e = e & 0xFFFFFF
            early_any, late_any = early_any | early, late_any | late
            for step, more in ((0, 1), (257, 1), (65536, two), (65536 + 257, two)):
                early_ref[early_n] = e + step
                late_ref[late_n] = e + step
                early_n = early_n + (early & more)
                late_n = late_n + (late & more)
        has_ref[b] = early_any
        has_ref[OB_DEV + b] = late_any
        return early_n, late_n

    counts = lax.fori_loop(0, OB_DEV, one_block, (jnp.int32(0), jnp.int32(0)))
    for n, list_ref, rounds_ref in ((counts[0], early_ref, early_rounds_ref), (counts[1], late_ref, late_rounds_ref)):
        for i in range(REST):
            list_ref[n + i] = jnp.int32(NO_ORDER * 65536 + NO_COURIER * 256)
        rounds_ref[0] = (n + REST - 1) // REST


def call_on_scalars(kernel, sizes, name, *operands):
    smem = pl.BlockSpec(memory_space=pltpu.SMEM)
    return pl.pallas_call(
        kernel,
        out_shape=tuple(jax.ShapeDtypeStruct((size,), jnp.int32) for size in sizes),
        in_specs=[smem] * len(operands),
        out_specs=(smem,) * len(sizes),
        compiler_params=pltpu.CompilerParams(vmem_limit_bytes=1024 * 1024),
        name=name,
    )(*operands)


def pair_fields(adjacency, order_count):
    flat = adjacency.reshape(-1)
    z = flat >> 2
    mine = jnp.where((flat & 3) == lax.axis_index("sub"), 1, 0)
    two = jnp.repeat(jnp.where(order_count > HALF, 1, 0), ADJ)
    block = jnp.arange(OB_DEV * ADJ, dtype=jnp.int32) // ADJ
    slot = slot_of(z, lax.axis_index("zone"))
    return (2 * block << 16) + (2 * z << 8), slot, mine, two


def first_lists(adjacency, order_count):
    entry, slot, mine, two = pair_fields(adjacency, order_count)
    is_early, place = early_slot(slot)
    entry = entry + 2 * jnp.where(is_early == 1, place, slot)
    pairs = entry + ((mine & is_early) << 24) + ((mine & (1 - is_early)) << 25) + (two << 26)
    sizes = (LIST_SIZE, LIST_SIZE, 1, 1, 2 * OB_DEV)
    return call_on_scalars(first_list_kernel, sizes, "first_lists", pairs.astype(jnp.int32))


def work_list(adjacency, order_count, courier_two):
    entry, slot, mine, two = pair_fields(adjacency, order_count)
    pairs = entry + 2 * slot + (mine << 24) + ((mine * two) << 25)
    return call_on_scalars(list_kernel, (LIST_SIZE, 1), "work_list", pairs.astype(jnp.int32), courier_two)


def pass_kernel(sum_couriers, list_ref, rounds_ref, summed_ref, kept_ref, weight_ref, live_ref, out_ref, w_ref, r_ref, m_ref):
    summed_blocks, kept_blocks = weight_ref.shape[0], live_ref.shape[0]
    rounds = rounds_ref[0]
    weight = weight_ref[...]

    high = weight.astype(jnp.bfloat16).astype(jnp.float32)
    low = weight - high
    blank = jnp.zeros((64 - 2 * summed_blocks, 128), jnp.float32)
    for part in range(2):
        rows = []
        for value in (high, low):
            rows += [value[:, part * 128 : part * 128 + 128], value[:, HALF + part * 128 : HALF + part * 128 + 128]]
            if summed_blocks < 32:
                rows.append(blank)
        w_ref[part * 128 : part * 128 + 128, :] = jnp.transpose(jnp.concatenate(rows, axis=0)).astype(jnp.bfloat16)
    r_ref[...] = jnp.zeros(r_ref.shape, jnp.float32)
    lanes = lax.broadcasted_iota(jnp.int32, (1, 128), 1) % 64

    def piece(e):
        order, courier, slot = e >> 16, (e >> 8) & 255, e & 255
        order_row = jnp.minimum(order, 2 * OB_DEV - 1) * HALF
        courier_row = (slot >> 1) * COURIER_ROWS + (slot & 1) * HALF
        return (courier, order, courier_row, order_row) if sum_couriers else (order, courier, order_row, courier_row)

    def sides(s_row, k_row):
        left = summed_ref[pl.ds(pl.multiple_of(s_row, 16), HALF), :]
        right = kept_ref[pl.ds(pl.multiple_of(k_row, 16), HALF), :]
        return left, right

    def scores(left, right):
        return lax.dot_general(left, right, (((1,), (1,)), ((), ())), preferred_element_type=jnp.float32)

    def weighted(s, s_row, k_row):
        left, right = sides(s_row, k_row)
        lane = (s % 2) * summed_blocks + s // 2
        ones = jnp.where(lanes == lane, 1.0, 0.0).astype(jnp.bfloat16)
        left = jnp.concatenate([left, w_ref[...]], axis=1)
        right = jnp.concatenate([right, jnp.broadcast_to(ones, (HALF, 128))], axis=1)
        return scores(left, right)

    def steps(first, count):
        todo = [piece(list_ref[first + t]) for t in range(count)]
        sums = [
            jnp.sum(jnp.exp2(weighted(s, s_row, k_row)).reshape(HALF // 8, 8, HALF), axis=0)
            for s, _, s_row, k_row in todo
        ]
        for (_, k, _, _), part in zip(todo, sums):
            r_ref[k // 2, k % 2] += part

    large_steps = rounds // (UNROLL // REST)

    def large_step(i, carry):
        steps(i * UNROLL, UNROLL)
        return carry

    def small_step(i, carry):
        steps(i * REST, REST)
        return carry

    lax.fori_loop(0, large_steps, large_step, 0)
    lax.fori_loop(large_steps * (UNROLL // REST), rounds, small_step, 0)

    large = jnp.where((weight > 0.5 * LOWEST) & ~(jnp.abs(weight) <= 128.0), 1.0, 0.0)
    bad = jnp.max(large, axis=0, keepdims=True)
    bad = jnp.maximum(bad[:, 0:HALF], bad[:, HALF:])
    for half in range(2):
        cut = slice(half * HALF, (half + 1) * HALF)
        total = jnp.sum(r_ref[0:kept_blocks, half], axis=1)
        live = live_ref[:, cut] > 0.5 * LOWEST
        fine = (total >= 2.0**-86) & (total <= 2.0**126)
        off = jnp.where(live & ~fine, 1.0, 0.0)
        bad = jnp.maximum(bad, jnp.max(off, axis=0, keepdims=True))
        out_ref[:, cut] = jnp.where(live, jnp.log2(jnp.where(live, total, 1.0)), LOWEST)
    bad = jnp.max(bad)

    @pl.when(bad > 0.0)
    def _():
        m_ref[...] = jnp.full(m_ref.shape, LOWEST, jnp.float32)
        r_ref[...] = jnp.zeros(r_ref.shape, jnp.float32)

        def one_piece(i, carry):
            s, k, s_row, k_row = piece(list_ref[i])
            block = jnp.minimum(s // 2, summed_blocks - 1)
            w = weight_ref[pl.ds(block, 1), pl.ds(pl.multiple_of((s % 2) * HALF, HALF), HALF)]
            column = jnp.transpose(jnp.broadcast_to(w, (128, HALF)))
            x = scores(*sides(s_row, k_row)) + jnp.concatenate([column, column], axis=1)
            before = m_ref[k // 2, k % 2, 0:1]
            after = jnp.maximum(before, jnp.max(x, axis=0, keepdims=True))
            scaled = r_ref[k // 2, k % 2, 0:1] * jnp.exp2(before - after)
            m_ref[k // 2, k % 2, 0:1] = after
            r_ref[k // 2, k % 2, 0:1] = scaled + jnp.sum(jnp.exp2(x - after), axis=0, keepdims=True)
            return carry

        lax.fori_loop(0, rounds * REST, one_piece, 0)
        for half in range(2):
            cut = slice(half * HALF, (half + 1) * HALF)
            live = live_ref[:, cut] > 0.5 * LOWEST
            total = jnp.where(live, r_ref[0:kept_blocks, half, 0, :], 1.0)
            out_ref[:, cut] = jnp.where(live, m_ref[0:kept_blocks, half, 0, :] + jnp.log2(total), LOWEST)


def half_sweep(sum_couriers, work, rounds, summed, kept, weight, live, name):
    smem = pl.BlockSpec(memory_space=pltpu.SMEM)
    vmem = pl.BlockSpec(memory_space=pltpu.VMEM)
    summed_blocks, kept_blocks = weight.shape[0], live.shape[0]

    def kernel(*refs):
        pass_kernel(sum_couriers, *refs)

    return pl.pallas_call(
        kernel,
        out_shape=jax.ShapeDtypeStruct((kept_blocks, BLOCK), jnp.float32),
        in_specs=[smem, smem] + [vmem] * 4,
        out_specs=vmem,
        scratch_shapes=pass_scratch(kept_blocks),
        compiler_params=pltpu.CompilerParams(vmem_limit_bytes=VMEM_LIMIT),
        cost_estimate=PASS_COST,
        name=name,
    )(work, rounds, summed, kept, weight, live)


PASS_COST = pl.CostEstimate(flops=28 * 2 * 512 * 512 * 128, bytes_accessed=6 << 20, transcendentals=28 * 512 * 512)


def pass_scratch(kept_blocks):
    return [
        pltpu.VMEM((HALF, 128), jnp.bfloat16),
        pltpu.VMEM((kept_blocks + 1, 2, 8, HALF), jnp.float32),
        pltpu.VMEM((kept_blocks + 1, 2, 8, HALF), jnp.float32),
    ]


def first_kernel(early, work_ref, rounds_ref, zone_ref, has_ref, *refs):
    count = len(EARLY) if early else PARTS
    parts, (orders_ref, live_ref, out_ref, couriers_ref, log_cap_ref, w_ref, r_ref, m_ref, weight_ref, here_ref, sem) = (
        refs[:count],
        refs[-11:],
    )
    rows = couriers_ref.shape[0] // count
    copies = [
        pltpu.make_async_copy(part, couriers_ref.at[pl.ds(i * rows, rows), :], sem.at[i]) for i, part in enumerate(parts)
    ]
    for copy in copies:
        copy.start()
    for block in range(OB_DEV):
        named = has_ref[block if early else OB_DEV + block] > 0
        here_ref[block : block + 1, :] = jnp.where(named, live_ref[block : block + 1, :], LOWEST)
    for copy in copies:
        copy.wait()
    for zone in range(ZONES):
        slot = slot_of(jnp.int32(zone), zone_ref[0])
        if early:
            _, slot = early_slot(slot)
        row = slot * COURIER_ROWS + BLOCK
        tail = couriers_ref[pl.ds(pl.multiple_of(row, 16), 16), :].astype(jnp.float32)
        log_cap_ref[zone : zone + 1, :] = jnp.concatenate([tail[i : i + 1] for i in range(4)], axis=1)
    cap = log_cap_ref[...]
    live = cap > 0.0
    log_cap_ref[...] = jnp.where(live, jnp.log2(jnp.where(live, cap, 1.0)), LOWEST)
    weight_ref[...] = jnp.where(live, 0.0, LOWEST)
    pass_kernel(True, work_ref, rounds_ref, couriers_ref, orders_ref, weight_ref, here_ref, out_ref, w_ref, r_ref, m_ref)


def first_half_sweep(early, work, rounds, zone, has, parts, orders, live, name):
    smem = pl.BlockSpec(memory_space=pltpu.SMEM)
    vmem = pl.BlockSpec(memory_space=pltpu.VMEM)

    def kernel(*refs):
        first_kernel(early, *refs)

    couriers = ((len(EARLY) if early else PARTS) * 4 * COURIER_ROWS, EMB)
    kept_out = () if early else (
        jax.ShapeDtypeStruct(couriers, jnp.bfloat16),
        jax.ShapeDtypeStruct((ZONES, BLOCK), jnp.float32),
    )
    as_scratch = [pltpu.VMEM(couriers, jnp.bfloat16), pltpu.VMEM((ZONES, BLOCK), jnp.float32)] if early else []
    return pl.pallas_call(
        kernel,
        out_shape=(jax.ShapeDtypeStruct((OB_DEV, BLOCK), jnp.float32),) + kept_out,
        in_specs=[smem] * 4 + [pl.BlockSpec(memory_space=pl.ANY)] * len(parts) + [vmem] * 2,
        out_specs=(vmem,) * (1 + len(kept_out)),
        scratch_shapes=as_scratch
        + pass_scratch(OB_DEV)
        + [
            pltpu.VMEM((ZONES, BLOCK), jnp.float32),
            pltpu.VMEM((OB_DEV, BLOCK), jnp.float32),
            pltpu.SemaphoreType.DMA((len(parts),)),
        ],
        compiler_params=pltpu.CompilerParams(vmem_limit_bytes=VMEM_LIMIT),
        cost_estimate=pl.CostEstimate(flops=14 * 2 * 512 * 512 * 128, bytes_accessed=6 << 20, transcendentals=14 * 512 * 512),
        name=name,
    )(work, rounds, zone.reshape(1), has, *parts, orders, live)


def shards(
    order_features,
    w_in,
    bias_in,
    w_out,
    bias_out,
    courier_embed,
    courier_cap,
    adjacency,
    order_count,
    courier_count,
):
    sub = lax.axis_index("sub")
    positions = jnp.arange(BLOCK, dtype=jnp.int32)

    own_live = positions < courier_count[0]
    row = gather_row(*pack(courier_count, courier_embed, courier_cap))
    lists = first_lists(adjacency, order_count)
    row, bias_in, lists = lax.optimization_barrier((row, bias_in, lists))
    early_list, late_list, early_rounds, late_rounds, has = lists
    orders = embed_orders(order_features, w_in, bias_in, w_out, bias_out)
    order_live = positions[None, :] < order_count[:, None]
    live = jnp.where(order_live, 0.0, LOWEST)
    zone = lax.axis_index("zone")

    own = [row] + [plane_step(row, 1, step) for step in (1, 2, 3)]
    other = [other_core(row)] + [None] * 3
    for step in (3, 2):
        own[step], orders = lax.optimization_barrier((own[step], orders))
        other[step] = other_core(own[step])
    parts = own + other
    (early_partial,) = first_half_sweep(
        True, early_list, early_rounds, zone, has, [parts[p] for p in (*EARLY, 2, 3)], orders, live, "orders_1_early"
    )
    own[1], early_partial = lax.optimization_barrier((own[1], early_partial))
    other[1] = other_core(own[1])
    late_partial, couriers, log_cap = first_half_sweep(
        False, late_list, late_rounds, zone, has, own + other, orders, live, "orders_1"
    )
    partial = join(early_partial, late_partial)

    mine = adjacency % SUBS == sub
    order_here = jnp.where(order_live & jnp.any(mine, axis=1, keepdims=True), 0.0, LOWEST)

    def order_dual_of(partial):
        return jnp.where(order_live, -join_subs(partial), LOWEST)

    courier_live = log_cap > 0.5 * LOWEST
    work, rounds = work_list(adjacency, order_count, courier_live[:, HALF].astype(jnp.int32))
    named = jnp.any(
        (adjacency.reshape(-1)[None, :] == jnp.arange(ZONES)[:, None] * SUBS + sub), axis=1, keepdims=True
    )
    courier_here = jnp.where(courier_live & named, 0.0, LOWEST)

    def courier_pass(order_dual, name):
        return half_sweep(False, work, rounds, orders, couriers, order_dual, courier_here, name)

    order_dual = order_dual_of(partial)
    sums = join_zones(courier_pass(order_dual, "couriers_1"))
    courier_dual = jnp.where(courier_live, log_cap - sums, LOWEST)
    order_dual = order_dual_of(half_sweep(True, work, rounds, couriers, orders, courier_dual, order_here, "orders_2"))
    partial = courier_pass(order_dual, "couriers_2")
    parts = lax.all_to_all(partial, "zone", 0, 0, tiled=True)
    highest = jnp.max(parts, axis=0)
    total = highest + jnp.log2(jnp.sum(jnp.exp2(parts - highest[None]), axis=0))
    own_log_cap = jnp.log2(courier_cap.astype(jnp.float32))
    courier_out = jnp.where(own_live, DUAL_SCALE * (own_log_cap - total), 0.0)
    order_out = jnp.where(order_live, DUAL_SCALE * order_dual, 0.0)
    return order_out.reshape(-1), courier_out


def solution(mesh):
    return jax.shard_map(
        shards,
        mesh=mesh,
        in_specs=(
            P("zone", None),
            P(),
            P(),
            P(),
            P(),
            P(("zone", "sub"), None),
            P(("zone", "sub")),
            P("zone", None),
            P("zone"),
            P(("zone", "sub")),
        ),
        out_specs=(P("zone"), P(("zone", "sub"))),
        check_vma=False,
    )
```

```python
import math

import jax
import jax.numpy as jnp
from jax import lax
from jax.experimental import pallas as pl
from jax.experimental.pallas import tpu as pltpu
from jax.sharding import PartitionSpec as P

BLOCK = 512
EMB = 128
HID = 512
ADJ = 8
OB_DEV = 16
ZONES = 32
SUBS = 4
HALF = 256
COURIER_ROWS = BLOCK + 16
UNROLL = 32
REST = 8
MOST_ENTRIES = 256
LIST_SIZE = MOST_ENTRIES + 2 * REST
NO_ORDER = 2 * OB_DEV
NO_COURIER = 2 * ZONES

TEMPER = 0.2
LOWEST = -1e30
SCORE_SCALE = math.log2(math.e) / (TEMPER * math.sqrt(EMB))
DUAL_SCALE = TEMPER * math.log(2.0)

VMEM_LIMIT = 16 * 1024 * 1024


def zone_of(y, x, core):
    return ((y % 4) * 4 + (x % 4)) * 2 + core


PLACES = [(y, x, core) for y in range(4) for x in range(4) for core in range(2)]


def other_core(value):
    return lax.ppermute(value, "zone", [(zone_of(y, x, c), zone_of(y, x, 1 - c)) for y, x, c in PLACES])


def along_z(value, step):
    return lax.ppermute(value, "sub", [(i, (i + step) % SUBS) for i in range(SUBS)])


def plane_step(value, stage, step):
    pairs = []
    for y, x, c in PLACES:
        to = (y, x + step, c) if stage == c else (y + step, x, c)
        pairs.append((zone_of(y, x, c), zone_of(*to)))
    return lax.ppermute(value, "zone", pairs)


def pack_kernel(count_ref, embed_ref, cap_hbm, block_ref, row_ref, cap_ref, sem):
    copy = pltpu.make_async_copy(embed_ref, block_ref.at[pl.ds(0, BLOCK), :], sem.at[0])
    copy_row = pltpu.make_async_copy(embed_ref, row_ref.at[pl.ds(0, BLOCK), :], sem.at[1])
    copy.start()
    copy_row.start()
    copy_cap = pltpu.make_async_copy(cap_hbm, cap_ref, sem.at[2])
    copy_cap.start()
    copy_cap.wait()
    lane = lax.broadcasted_iota(jnp.int32, (1, BLOCK), 1)
    cap = jnp.where(lane < count_ref[0], cap_ref[...].astype(jnp.float32).reshape(1, BLOCK), 0.0)
    rows = [cap[:, i * EMB : (i + 1) * EMB] for i in range(4)]
    tail = jnp.concatenate(rows + [jnp.zeros((12, EMB), jnp.float32)], axis=0).astype(jnp.bfloat16)
    block_ref[pl.ds(BLOCK, 16), :] = tail
    row_ref[pl.ds(BLOCK, 16), :] = tail
    copy.wait()
    copy_row.wait()


def pack(count, embed, cap):
    vmem = pl.BlockSpec(memory_space=pltpu.VMEM)
    return pl.pallas_call(
        pack_kernel,
        out_shape=(
            jax.ShapeDtypeStruct((COURIER_ROWS, EMB), jnp.bfloat16),
            jax.ShapeDtypeStruct((4 * COURIER_ROWS, EMB), jnp.bfloat16),
        ),
        in_specs=[pl.BlockSpec(memory_space=pltpu.SMEM)] + [pl.BlockSpec(memory_space=pltpu.HBM)] * 2,
        out_specs=(vmem, vmem),
        scratch_shapes=[pltpu.VMEM((BLOCK,), cap.dtype), pltpu.SemaphoreType.DMA((3,))],
        compiler_params=pltpu.CompilerParams(vmem_limit_bytes=4 * 1024 * 1024),
        name="pack",
    )(count, *[pltpu.with_memory_space_constraint(value, pltpu.HBM) for value in (embed, cap)])


def gather_row(block, row):
    for step in (1, 2, 3):
        row = lax.dynamic_update_slice(row, plane_step(block, 0, step), (step * COURIER_ROWS, 0))
    return row


PARTS = 8
EARLY = (0, 4)


def slot_of(zone, me):
    back_x = ((me >> 1) - (zone >> 1)) & 3
    back_y = ((me >> 3) - (zone >> 3)) & 3
    odd = zone & 1
    first = jnp.where(odd == 0, back_x, back_y)
    second = jnp.where(odd == 0, back_y, back_x)
    return ((me ^ zone) & 1) * 16 + second * 4 + first


def early_slot(slot):
    part = slot >> 2
    index = sum(jnp.where(part == p, i, 0) for i, p in enumerate(EARLY))
    is_early = sum(jnp.where(part == p, 1, 0) for p in EARLY)
    return is_early, index * 4 + (slot & 3)


def join(*parts):
    highest = parts[0]
    for part in parts[1:]:
        highest = jnp.maximum(highest, part)
    total = jnp.exp2(parts[0] - highest)
    for part in parts[1:]:
        total = total + jnp.exp2(part - highest)
    return highest + jnp.log2(total)


def join_subs(value):
    return join(value, along_z(value, 1), along_z(value, 2), along_z(value, 3))


def join_zones(value):
    value = join(value, other_core(value))
    for stage in (1, 0):
        value = join(value, *[plane_step(value, stage, step) for step in (1, 2, 3)])
    return value


EMBED_ROWS = 4096


def embed_kernel(x_hbm, w_in_hbm, b_in_hbm, w_out_hbm, b_out_hbm, o_ref, x_ref, w_in_ref, b_in_ref, w_out_ref, b_out_ref, sem):
    steps = x_ref.shape[0] // EMBED_ROWS

    def rows_copy(i):
        rows = pl.ds(pl.multiple_of(i * EMBED_ROWS, EMBED_ROWS), EMBED_ROWS)
        return pltpu.make_async_copy(x_hbm.at[rows, :], x_ref.at[rows, :], sem.at[i])

    parameters = [
        pltpu.make_async_copy(source, target, sem.at[steps + i])
        for i, (source, target) in enumerate(
            [(w_in_hbm, w_in_ref), (b_in_hbm, b_in_ref), (w_out_hbm, w_out_ref), (b_out_hbm, b_out_ref)]
        )
    ]
    for copy in parameters:
        copy.start()
    for i in range(steps):
        rows_copy(i).start()
    for copy in parameters:
        copy.wait()

    def one_step(i, carry):
        rows_copy(i).wait()
        for start in range(0, EMBED_ROWS, BLOCK):
            rows = pl.ds(pl.multiple_of(i * EMBED_ROWS + start, BLOCK), BLOCK)
            v = jnp.dot(x_ref[rows, :], w_in_ref[...], preferred_element_type=jnp.float32)
            v = 0.5 * (v + b_in_ref[...])
            hidden = (v + v * jnp.tanh(v)).astype(jnp.bfloat16)
            out = jnp.dot(hidden, w_out_ref[...], preferred_element_type=jnp.float32)
            o_ref[rows, :] = ((out + b_out_ref[...]) * SCORE_SCALE).astype(jnp.bfloat16)
        return carry

    lax.fori_loop(0, steps, one_step, 0)


def embed_orders(features, w_in, bias_in, w_out, bias_out):
    rows = features.shape[0]
    operands = (features, w_in, bias_in.reshape(1, HID), w_out, bias_out.reshape(1, EMB))
    return pl.pallas_call(
        embed_kernel,
        out_shape=jax.ShapeDtypeStruct((rows, EMB), jnp.bfloat16),
        in_specs=[pl.BlockSpec(memory_space=pltpu.HBM)] * len(operands),
        out_specs=pl.BlockSpec(memory_space=pltpu.VMEM),
        scratch_shapes=[pltpu.VMEM(value.shape, value.dtype) for value in operands]
        + [pltpu.SemaphoreType.DMA((rows // EMBED_ROWS + 4,))],
        compiler_params=pltpu.CompilerParams(vmem_limit_bytes=VMEM_LIMIT),
        cost_estimate=pl.CostEstimate(
            flops=4 * rows * EMB * HID, bytes_accessed=4 * rows * EMB, transcendentals=rows * HID
        ),
        name="embed_orders",
    )(*[pltpu.with_memory_space_constraint(value, pltpu.HBM) for value in operands])


def list_kernel(pair_ref, two_ref, list_ref, rounds_ref):
    def one_pair(p, n):
        e = pair_ref[p]
        mine = (e >> 24) & 1
        order_two = (e >> 25) & 1
        courier_two = mine * two_ref[(e >> 9) & 31]
        e = e & 0xFFFFFF
        list_ref[n] = e
        n = n + mine
        list_ref[n] = e + 257
        n = n + courier_two
        list_ref[n] = e + 65536
        n = n + order_two
        list_ref[n] = e + 65536 + 257
        return n + (order_two & courier_two)

    n = lax.fori_loop(0, OB_DEV * ADJ, one_pair, jnp.int32(0), unroll=8)
    for i in range(REST):
        list_ref[n + i] = jnp.int32(NO_ORDER * 65536 + NO_COURIER * 256)
    rounds_ref[0] = (n + REST - 1) // REST


def first_list_kernel(pair_ref, early_ref, late_ref, early_rounds_ref, late_rounds_ref, has_ref):
    def one_block(b, counts):
        early_n, late_n = counts
        early_any, late_any = jnp.int32(0), jnp.int32(0)
        for i in range(ADJ):
            e = pair_ref[b * ADJ + i]
            early = (e >> 24) & 1
            late = (e >> 25) & 1
            two = (e >> 26) & 1
            e = e & 0xFFFFFF
            early_any, late_any = early_any | early, late_any | late
            for step, more in ((0, 1), (257, 1), (65536, two), (65536 + 257, two)):
                early_ref[early_n] = e + step
                late_ref[late_n] = e + step
                early_n = early_n + (early & more)
                late_n = late_n + (late & more)
        has_ref[b] = early_any
        has_ref[OB_DEV + b] = late_any
        return early_n, late_n

    counts = lax.fori_loop(0, OB_DEV, one_block, (jnp.int32(0), jnp.int32(0)))
    for n, list_ref, rounds_ref in ((counts[0], early_ref, early_rounds_ref), (counts[1], late_ref, late_rounds_ref)):
        for i in range(REST):
            list_ref[n + i] = jnp.int32(NO_ORDER * 65536 + NO_COURIER * 256)
        rounds_ref[0] = (n + REST - 1) // REST


def call_on_scalars(kernel, sizes, name, *operands):
    smem = pl.BlockSpec(memory_space=pltpu.SMEM)
    return pl.pallas_call(
        kernel,
        out_shape=tuple(jax.ShapeDtypeStruct((size,), jnp.int32) for size in sizes),
        in_specs=[smem] * len(operands),
        out_specs=(smem,) * len(sizes),
        compiler_params=pltpu.CompilerParams(vmem_limit_bytes=1024 * 1024),
        name=name,
    )(*operands)


def pair_fields(adjacency, order_count):
    flat = adjacency.reshape(-1)
    z = flat >> 2
    mine = jnp.where((flat & 3) == lax.axis_index("sub"), 1, 0)
    two = jnp.repeat(jnp.where(order_count > HALF, 1, 0), ADJ)
    block = jnp.arange(OB_DEV * ADJ, dtype=jnp.int32) // ADJ
    slot = slot_of(z, lax.axis_index("zone"))
    return (2 * block << 16) + (2 * z << 8), slot, mine, two


def first_lists(adjacency, order_count):
    entry, slot, mine, two = pair_fields(adjacency, order_count)
    is_early, place = early_slot(slot)
    entry = entry + 2 * jnp.where(is_early == 1, place, slot)
    pairs = entry + ((mine & is_early) << 24) + ((mine & (1 - is_early)) << 25) + (two << 26)
    sizes = (LIST_SIZE, LIST_SIZE, 1, 1, 2 * OB_DEV)
    return call_on_scalars(first_list_kernel, sizes, "first_lists", pairs.astype(jnp.int32))


def work_list(adjacency, order_count, courier_two):
    entry, slot, mine, two = pair_fields(adjacency, order_count)
    pairs = entry + 2 * slot + (mine << 24) + ((mine * two) << 25)
    return call_on_scalars(list_kernel, (LIST_SIZE, 1), "work_list", pairs.astype(jnp.int32), courier_two)


def pass_kernel(sum_couriers, list_ref, rounds_ref, summed_ref, kept_ref, weight_ref, live_ref, out_ref, w_ref, r_ref, m_ref):
    summed_blocks, kept_blocks = weight_ref.shape[0], live_ref.shape[0]
    rounds = rounds_ref[0]
    weight = weight_ref[...]

    high = weight.astype(jnp.bfloat16).astype(jnp.float32)
    low = weight - high
    blank = jnp.zeros((64 - 2 * summed_blocks, 128), jnp.float32)
    for part in range(2):
        rows = []
        for value in (high, low):
            rows += [value[:, part * 128 : part * 128 + 128], value[:, HALF + part * 128 : HALF + part * 128 + 128]]
            if summed_blocks < 32:
                rows.append(blank)
        w_ref[part * 128 : part * 128 + 128, :] = jnp.transpose(jnp.concatenate(rows, axis=0)).astype(jnp.bfloat16)
    r_ref[...] = jnp.zeros(r_ref.shape, jnp.float32)
    lanes = lax.broadcasted_iota(jnp.int32, (1, 128), 1) % 64

    def piece(e):
        order, courier, slot = e >> 16, (e >> 8) & 255, e & 255
        order_row = jnp.minimum(order, 2 * OB_DEV - 1) * HALF
        courier_row = (slot >> 1) * COURIER_ROWS + (slot & 1) * HALF
        return (courier, order, courier_row, order_row) if sum_couriers else (order, courier, order_row, courier_row)

    def sides(s_row, k_row):
        left = summed_ref[pl.ds(pl.multiple_of(s_row, 16), HALF), :]
        right = kept_ref[pl.ds(pl.multiple_of(k_row, 16), HALF), :]
        return left, right

    def scores(left, right):
        return lax.dot_general(left, right, (((1,), (1,)), ((), ())), preferred_element_type=jnp.float32)

    def weighted(s, s_row, k_row):
        left, right = sides(s_row, k_row)
        lane = (s % 2) * summed_blocks + s // 2
        ones = jnp.where(lanes == lane, 1.0, 0.0).astype(jnp.bfloat16)
        left = jnp.concatenate([left, w_ref[...]], axis=1)
        right = jnp.concatenate([right, jnp.broadcast_to(ones, (HALF, 128))], axis=1)
        return scores(left, right)

    def steps(first, count):
        todo = [piece(list_ref[first + t]) for t in range(count)]
        sums = [
            jnp.sum(jnp.exp2(weighted(s, s_row, k_row)).reshape(HALF // 8, 8, HALF), axis=0)
            for s, _, s_row, k_row in todo
        ]
        for (_, k, _, _), part in zip(todo, sums):
            r_ref[k // 2, k % 2] += part

    large_steps = rounds // (UNROLL // REST)

    def large_step(i, carry):
        steps(i * UNROLL, UNROLL)
        return carry

    def small_step(i, carry):
        steps(i * REST, REST)
        return carry

    lax.fori_loop(0, large_steps, large_step, 0)
    lax.fori_loop(large_steps * (UNROLL // REST), rounds, small_step, 0)

    large = jnp.where((weight > 0.5 * LOWEST) & ~(jnp.abs(weight) <= 128.0), 1.0, 0.0)
    bad = jnp.max(large, axis=0, keepdims=True)
    bad = jnp.maximum(bad[:, 0:HALF], bad[:, HALF:])
    for half in range(2):
        cut = slice(half * HALF, (half + 1) * HALF)
        total = jnp.sum(r_ref[0:kept_blocks, half], axis=1)
        live = live_ref[:, cut] > 0.5 * LOWEST
        fine = (total >= 2.0**-86) & (total <= 2.0**126)
        off = jnp.where(live & ~fine, 1.0, 0.0)
        bad = jnp.maximum(bad, jnp.max(off, axis=0, keepdims=True))
        out_ref[:, cut] = jnp.where(live, jnp.log2(jnp.where(live, total, 1.0)), LOWEST)
    bad = jnp.max(bad)

    @pl.when(bad > 0.0)
    def _():
        m_ref[...] = jnp.full(m_ref.shape, LOWEST, jnp.float32)
        r_ref[...] = jnp.zeros(r_ref.shape, jnp.float32)

        def one_piece(i, carry):
            s, k, s_row, k_row = piece(list_ref[i])
            block = jnp.minimum(s // 2, summed_blocks - 1)
            w = weight_ref[pl.ds(block, 1), pl.ds(pl.multiple_of((s % 2) * HALF, HALF), HALF)]
            column = jnp.transpose(jnp.broadcast_to(w, (128, HALF)))
            x = scores(*sides(s_row, k_row)) + jnp.concatenate([column, column], axis=1)
            before = m_ref[k // 2, k % 2, 0:1]
            after = jnp.maximum(before, jnp.max(x, axis=0, keepdims=True))
            scaled = r_ref[k // 2, k % 2, 0:1] * jnp.exp2(before - after)
            m_ref[k // 2, k % 2, 0:1] = after
            r_ref[k // 2, k % 2, 0:1] = scaled + jnp.sum(jnp.exp2(x - after), axis=0, keepdims=True)
            return carry

        lax.fori_loop(0, rounds * REST, one_piece, 0)
        for half in range(2):
            cut = slice(half * HALF, (half + 1) * HALF)
            live = live_ref[:, cut] > 0.5 * LOWEST
            total = jnp.where(live, r_ref[0:kept_blocks, half, 0, :], 1.0)
            out_ref[:, cut] = jnp.where(live, m_ref[0:kept_blocks, half, 0, :] + jnp.log2(total), LOWEST)


def half_sweep(sum_couriers, work, rounds, summed, kept, weight, live, name):
    smem = pl.BlockSpec(memory_space=pltpu.SMEM)
    vmem = pl.BlockSpec(memory_space=pltpu.VMEM)
    summed_blocks, kept_blocks = weight.shape[0], live.shape[0]

    def kernel(*refs):
        pass_kernel(sum_couriers, *refs)

    return pl.pallas_call(
        kernel,
        out_shape=jax.ShapeDtypeStruct((kept_blocks, BLOCK), jnp.float32),
        in_specs=[smem, smem] + [vmem] * 4,
        out_specs=vmem,
        scratch_shapes=pass_scratch(kept_blocks),
        compiler_params=pltpu.CompilerParams(vmem_limit_bytes=VMEM_LIMIT),
        cost_estimate=PASS_COST,
        name=name,
    )(work, rounds, summed, kept, weight, live)


PASS_COST = pl.CostEstimate(flops=28 * 2 * 512 * 512 * 128, bytes_accessed=6 << 20, transcendentals=28 * 512 * 512)


def pass_scratch(kept_blocks):
    return [
        pltpu.VMEM((HALF, 128), jnp.bfloat16),
        pltpu.VMEM((kept_blocks + 1, 2, 8, HALF), jnp.float32),
        pltpu.VMEM((kept_blocks + 1, 2, 8, HALF), jnp.float32),
    ]


def first_kernel(early, work_ref, rounds_ref, zone_ref, has_ref, *refs):
    count = len(EARLY) if early else PARTS
    parts, (orders_ref, live_ref, out_ref, couriers_ref, log_cap_ref, w_ref, r_ref, m_ref, weight_ref, here_ref, sem) = (
        refs[:count],
        refs[count:],
    )
    rows = couriers_ref.shape[0] // count
    copies = [
        pltpu.make_async_copy(part, couriers_ref.at[pl.ds(i * rows, rows), :], sem.at[i]) for i, part in enumerate(parts)
    ]
    for copy in copies:
        copy.start()
    for block in range(OB_DEV):
        named = has_ref[block if early else OB_DEV + block] > 0
        here_ref[block : block + 1, :] = jnp.where(named, live_ref[block : block + 1, :], LOWEST)
    for copy in copies:
        copy.wait()
    for zone in range(ZONES):
        slot = slot_of(jnp.int32(zone), zone_ref[0])
        if early:
            _, slot = early_slot(slot)
        row = slot * COURIER_ROWS + BLOCK
        tail = couriers_ref[pl.ds(pl.multiple_of(row, 16), 16), :].astype(jnp.float32)
        log_cap_ref[zone : zone + 1, :] = jnp.concatenate([tail[i : i + 1] for i in range(4)], axis=1)
    cap = log_cap_ref[...]
    live = cap > 0.0
    log_cap_ref[...] = jnp.where(live, jnp.log2(jnp.where(live, cap, 1.0)), LOWEST)
    weight_ref[...] = jnp.where(live, 0.0, LOWEST)
    pass_kernel(True, work_ref, rounds_ref, couriers_ref, orders_ref, weight_ref, here_ref, out_ref, w_ref, r_ref, m_ref)


def first_half_sweep(early, work, rounds, zone, has, parts, orders, live, name):
    smem = pl.BlockSpec(memory_space=pltpu.SMEM)
    vmem = pl.BlockSpec(memory_space=pltpu.VMEM)

    def kernel(*refs):
        first_kernel(early, *refs)

    couriers = (len(parts) * 4 * COURIER_ROWS, EMB)
    kept_out = () if early else (
        jax.ShapeDtypeStruct(couriers, jnp.bfloat16),
        jax.ShapeDtypeStruct((ZONES, BLOCK), jnp.float32),
    )
    as_scratch = [pltpu.VMEM(couriers, jnp.bfloat16), pltpu.VMEM((ZONES, BLOCK), jnp.float32)] if early else []
    return pl.pallas_call(
        kernel,
        out_shape=(jax.ShapeDtypeStruct((OB_DEV, BLOCK), jnp.float32),) + kept_out,
        in_specs=[smem] * 4 + [pl.BlockSpec(memory_space=pl.ANY)] * len(parts) + [vmem] * 2,
        out_specs=(vmem,) * (1 + len(kept_out)),
        scratch_shapes=as_scratch
        + pass_scratch(OB_DEV)
        + [
            pltpu.VMEM((ZONES, BLOCK), jnp.float32),
            pltpu.VMEM((OB_DEV, BLOCK), jnp.float32),
            pltpu.SemaphoreType.DMA((len(parts),)),
        ],
        compiler_params=pltpu.CompilerParams(vmem_limit_bytes=VMEM_LIMIT),
        cost_estimate=pl.CostEstimate(flops=14 * 2 * 512 * 512 * 128, bytes_accessed=6 << 20, transcendentals=14 * 512 * 512),
        name=name,
    )(work, rounds, zone.reshape(1), has, *parts, orders, live)


def shards(
    order_features,
    w_in,
    bias_in,
    w_out,
    bias_out,
    courier_embed,
    courier_cap,
    adjacency,
    order_count,
    courier_count,
):
    sub = lax.axis_index("sub")
    positions = jnp.arange(BLOCK, dtype=jnp.int32)

    own_live = positions < courier_count[0]
    row = gather_row(*pack(courier_count, courier_embed, courier_cap))
    lists = first_lists(adjacency, order_count)
    row, bias_in, lists = lax.optimization_barrier((row, bias_in, lists))
    early_list, late_list, early_rounds, late_rounds, has = lists
    orders = embed_orders(order_features, w_in, bias_in, w_out, bias_out)
    order_live = positions[None, :] < order_count[:, None]
    live = jnp.where(order_live, 0.0, LOWEST)
    zone = lax.axis_index("zone")

    own = [row] + [plane_step(row, 1, step) for step in (1, 2, 3)]
    other = [other_core(row)] + [None] * 3
    parts = own + other
    (early_partial,) = first_half_sweep(
        True, early_list, early_rounds, zone, has, [parts[p] for p in EARLY], orders, live, "orders_1_early"
    )
    own[1], own[2], own[3], early_partial = lax.optimization_barrier((own[1], own[2], own[3], early_partial))
    for step in (1, 2, 3):
        other[step] = other_core(own[step])
    late_partial, couriers, log_cap = first_half_sweep(
        False, late_list, late_rounds, zone, has, own + other, orders, live, "orders_1"
    )
    partial = join(early_partial, late_partial)

    mine = adjacency % SUBS == sub
    order_here = jnp.where(order_live & jnp.any(mine, axis=1, keepdims=True), 0.0, LOWEST)

    def order_dual_of(partial):
        return jnp.where(order_live, -join_subs(partial), LOWEST)

    courier_live = log_cap > 0.5 * LOWEST
    work, rounds = work_list(adjacency, order_count, courier_live[:, HALF].astype(jnp.int32))
    named = jnp.any(
        (adjacency.reshape(-1)[None, :] == jnp.arange(ZONES)[:, None] * SUBS + sub), axis=1, keepdims=True
    )
    courier_here = jnp.where(courier_live & named, 0.0, LOWEST)

    def courier_pass(order_dual, name):
        return half_sweep(False, work, rounds, orders, couriers, order_dual, courier_here, name)

    order_dual = order_dual_of(partial)
    sums = join_zones(courier_pass(order_dual, "couriers_1"))
    courier_dual = jnp.where(courier_live, log_cap - sums, LOWEST)
    order_dual = order_dual_of(half_sweep(True, work, rounds, couriers, orders, courier_dual, order_here, "orders_2"))
    partial = courier_pass(order_dual, "couriers_2")
    parts = lax.all_to_all(partial, "zone", 0, 0, tiled=True)
    highest = jnp.max(parts, axis=0)
    total = highest + jnp.log2(jnp.sum(jnp.exp2(parts - highest[None]), axis=0))
    own_log_cap = jnp.log2(courier_cap.astype(jnp.float32))
    courier_out = jnp.where(own_live, DUAL_SCALE * (own_log_cap - total), 0.0)
    order_out = jnp.where(order_live, DUAL_SCALE * order_dual, 0.0)
    return order_out.reshape(-1), courier_out


def solution(mesh):
    return jax.shard_map(
        shards,
        mesh=mesh,
        in_specs=(
            P("zone", None),
            P(),
            P(),
            P(),
            P(),
            P(("zone", "sub"), None),
            P(("zone", "sub")),
            P("zone", None),
            P("zone"),
            P(("zone", "sub")),
        ),
        out_specs=(P("zone"), P(("zone", "sub"))),
        check_vma=False,
    )
```
